32 devices in a mesh: wide: 8 (over y, x, core), narrow: 4 (over z).
Axes of the slice: x: 2, y: 2, z: 4, core: 2. Of those that a mesh axis runs over, the one named last changes fastest.
Arguments:
- tokens: bfloat16 [4096, 2048], P(('wide', 'narrow')), may hold values from -6 to 6
- memory: bfloat16 [8192, 2048], P(('wide', 'narrow')), may hold values from -6 to 6
- item_len: int32 [8, 4], P('wide'), may hold values from 1 to 128, 448 in all within a row
- item_kind: int32 [8, 4], P('wide'), may hold values from 0 to 1
- norm_gains: bfloat16 [3, 2048], replicated, may hold values from 0.5 to 1.5
- w_self_in: bfloat16 [2048, 3, 2048], P(('wide', 'narrow')), may hold values from -0.125 to 0.125
- w_self_out: bfloat16 [2048, 2048], P(('wide', 'narrow')), may hold values from -0.75 to 0.75
- w_cross_q: bfloat16 [2048, 2048], P(('wide', 'narrow')), may hold values from -0.125 to 0.125
- w_cross_kv: bfloat16 [2048, 2, 2048], P(('wide', 'narrow')), may hold values from -0.125 to 0.125
- w_cross_out: bfloat16 [2048, 2048], P(('wide', 'narrow')), may hold values from -2 to 2
- w_mlp_in: bfloat16 [5120, 2, 2048], P(('wide', 'narrow')), may hold values from -0.125 to 0.125
- w_mlp_out: bfloat16 [5120, 2048], P(('wide', 'narrow')), may hold values from -0.078125 to 0.078125
- cotangent: bfloat16 [4096, 2048], P(('wide', 'narrow')), may hold values from -6 to 6
Outputs:
- output: bfloat16 [4096, 2048], P(('wide', 'narrow'))
- grad_tokens: bfloat16 [4096, 2048], P(('wide', 'narrow'))
- grad_memory: bfloat16 [8192, 2048], P(('wide', 'narrow'))
- grad_gains: float32 [3, 2048], P(None, 'narrow')
- grad_self_in: float32 [2048, 3, 2048], P('narrow')
- grad_self_out: float32 [2048, 2048], P('narrow')
- grad_cross_q: float32 [2048, 2048], P('narrow')
- grad_cross_kv: float32 [2048, 2, 2048], P('narrow')
- grad_cross_out: float32 [2048, 2048], P('narrow')
- grad_mlp_in: float32 [5120, 2, 2048], P('narrow')
- grad_mlp_out: float32 [5120, 2048], P('narrow')
The draws below stay inside these ranges and needn't reach their ends.
Inputs may be any that keep to these rules, and one draw needn't show every extreme that they name: `item_len`: in each group the lengths sum to 448 and one item has exactly 128 tokens; the last 64 positions of a group are padding.
All inputs are finite; a program needn't handle non-finite values.
Results may differ from the reference program's by a relative error of at most 0.039.
Values may be sent and summed in bfloat16 or wider, within the bound.
No kernel may reach another device: no remote copies, remote signals or barrier semaphores. Data moves between devices by JAX's collectives and lax.ppermute only.
A program may use at most 512 MiB of HBM per device.

```python
import math
import jax
import jax.numpy as jnp
import numpy as np
from jax import lax

D = 2048
HEADS = 16
HEAD_DIM = 128
FF = 5120
PATCH = 256
MOST = 128
GROUP = 512
ITEMS = 4
USED = 448
MEM = 1024
GROUPS = 8
TOKENS = 4096


def with_ends(array, stream_key, smallest, top_value):
    longest = array.shape.index(max(array.shape))
    spots = []
    for shift in (0, 1):
        where = [jax.random.randint(jax.random.fold_in(stream_key, axis), (), 0, length) for axis, length in enumerate(array.shape)]
        where[longest] = (where[longest] + shift) % array.shape[longest]
        spots.append(tuple(where))
    return array.at[spots[0]].set(smallest).at[spots[1]].set(top_value)


def steps_of(own_key, extent, cuts, least, top_value):
    def one(axis_at, blocks):
        steps = jax.random.uniform(jax.random.fold_in(jax.random.fold_in(own_key, 6), axis_at), (blocks,), jnp.float32, least / len(cuts), top_value / len(cuts))
        return jnp.repeat(jnp.exp(steps), extent[axis_at] // blocks).reshape((-1,) + (1,) * (len(extent) - axis_at - 1))

    level = one(*cuts[0])
    for cut in cuts[1:]:
        level = level * one(*cut)
    return level


def length_profile(number_of, total, reach, slope):
    portions = [(1 << 20) // math.isqrt(standing ** slope) + 1 for standing in range(2, number_of + 1)]
    surplus, counts = total - reach - (number_of - 1), [1] * (number_of - 1)
    while surplus > 0:
        free = [i for i in range(number_of - 1) if counts[i] < reach]
        mass, left = sum([portions[i] for i in free]), surplus
        for i in free:
            addition = min(reach - counts[i], max(1, left * portions[i] // mass), surplus)
            counts[i] = counts[i] + addition
            surplus = surplus - addition
    return np.array([reach] + counts)


def ragged(own_key, number_of, total, bound, skew):
    if number_of == 2:
        one = jax.random.randint(own_key, (), max(1, total - bound), min(bound, total - 1) + 1)
        return jnp.stack([one, total - one])
    tallies = jnp.asarray(length_profile(number_of, total, bound, skew), jnp.int32)
    pairs = (number_of - 1) // 2
    source_of, receiver = tallies[1:1 + 2 * pairs:2], tallies[2:2 + 2 * pairs:2]
    room = jnp.minimum(source_of - 1, bound - receiver)
    passed = jax.random.randint(jax.random.fold_in(own_key, 1), (pairs,), 0, 1 << 20) % (room + 1)
    tallies = tallies.at[1:1 + 2 * pairs:2].set(source_of - passed).at[2:2 + 2 * pairs:2].set(receiver + passed)
    return tallies[jax.random.permutation(jax.random.fold_in(own_key, 2), number_of)]


def bell_draw(key, shape, deviation, limit, pieces=(), kind=jnp.bfloat16):
    values = jax.random.normal(key, shape, jnp.float32) * deviation
    if len(pieces) > 0:
        values = steps_of(key, shape, pieces, -0.22, 0.18) * values
    return jnp.clip(values, min=-limit, max=limit).astype(kind)


def setup_inputs(seed: int = 0) -> dict:
    keys = jax.random.split(jax.random.key(seed), 14)
    return {
        "tokens": bell_draw(keys[0], (TOKENS, D), 1.0, 6.0, ((0, 32),)),
        "memory": bell_draw(keys[1], (GROUPS * MEM, D), 1.0, 6.0, ((0, 32),)),
        "item_len": jax.vmap(lambda own: ragged(own, ITEMS, USED, MOST, 2))(jax.random.split(keys[2], GROUPS)).reshape((GROUPS, ITEMS)).astype(jnp.int32),
        "item_kind": with_ends(jax.random.randint(keys[3], (GROUPS, ITEMS), 0, 2), jax.random.fold_in(keys[3], 1), 0, 1).astype(jnp.int32),
        "norm_gains": jnp.clip(1.0 + 0.1 * jax.random.normal(keys[4], (3, D), jnp.float32), 0.5, 1.5).astype(jnp.bfloat16),
        "w_self_in": bell_draw(keys[5], (HEADS * HEAD_DIM, 3, D), D ** -0.5, 0.125, ((0, 32),)),
        "w_self_out": bell_draw(keys[6], (HEADS * HEAD_DIM, D), (HEADS * HEAD_DIM // 32) ** -0.5, 0.75, ((0, 32),)),
        "w_cross_q": bell_draw(keys[7], (HEADS * HEAD_DIM, D), D ** -0.5, 0.125, ((0, 32),)),
        "w_cross_kv": bell_draw(keys[8], (HEADS * HEAD_DIM, 2, D), D ** -0.5, 0.125, ((0, 32),)),
        "w_cross_out": bell_draw(keys[9], (HEADS * HEAD_DIM, D), (HEADS * HEAD_DIM // 256) ** -0.5, 2.0, ((0, 32),)),
        "w_mlp_in": bell_draw(keys[10], (FF, 2, D), D ** -0.5, 0.125, ((0, 32),)),
        "w_mlp_out": bell_draw(keys[11], (FF, D), FF ** -0.5, 0.078125, ((0, 32),)),
        "cotangent": bell_draw(keys[12], (TOKENS, D), 1.0, 6.0, ((0, 32),)),
    }


EPSILON = 1e-06
ROBOT_WEIGHT = 2.0
HIGHEST = lax.Precision.HIGHEST

@jax.custom_vjp
def low(v):
    return lax.optimization_barrier(v.astype(jnp.bfloat16)).astype(jnp.float32)

@jax.custom_vjp
def low_back(v):
    return v

def low_keep(v):
    return (low(v), None)

def low_pass(kept, grad):
    return (grad,)

def back_keep(v):
    return (v, None)

def back_low(kept, grad):
    return (low(grad),)
low.defvjp(low_keep, low_pass)
low_back.defvjp(back_keep, back_low)

def normed(values, gain_row):
    factor = lax.rsqrt(lax.optimization_barrier(jnp.mean(values * values, axis=-1, keepdims=True)) + EPSILON)
    return values * factor * gain_row

def attend(queries, keys_all, values_all, allowed):

    def one_head(head_parts):
        q, k, v = head_parts
        scores = low_back(jnp.dot(q, k.T, precision=HIGHEST) * HEAD_DIM ** (-0.5))
        scores = jnp.where(allowed, scores, -1e+30)
        row_top = lax.optimization_barrier(jnp.max(scores, axis=1, keepdims=True))
        exp_scores = jnp.exp(scores - row_top)
        soft_probs = low(exp_scores / lax.optimization_barrier(jnp.sum(exp_scores, axis=1, keepdims=True)))
        return jnp.dot(soft_probs, v, precision=HIGHEST)
    outs = lax.map(jax.checkpoint(one_head), (jnp.moveaxis(queries, 1, 0), jnp.moveaxis(keys_all, 1, 0), jnp.moveaxis(values_all, 1, 0)))
    return jnp.moveaxis(outs, 0, 1)

def group_masks(lengths, item_kinds):
    item_ends = jnp.cumsum(lengths)
    positions = jnp.arange(GROUP, dtype=jnp.int32)
    segment = lax.optimization_barrier(jnp.sum((positions[:, None] >= item_ends[None, :]).astype(jnp.int32), axis=1))
    token_valid = segment < ITEMS
    item_hit = segment[:, None] == jnp.arange(ITEMS, dtype=jnp.int32)[None, :]
    robot_flag = lax.optimization_barrier(jnp.sum(jnp.where(item_hit, item_kinds[None, :], 0), axis=1))
    weight = jnp.where(token_valid, jnp.where(robot_flag == 1, ROBOT_WEIGHT, 1.0), 0.0).astype(jnp.float32)
    self_ok = (segment[:, None] == segment[None, :]) & (positions[None, :] <= positions[:, None])
    mem_item = jnp.arange(MEM, dtype=jnp.int32) // PATCH
    cross_ok = mem_item[None, :] == jnp.minimum(segment, ITEMS - 1)[:, None]
    return (self_ok, cross_ok, token_valid.astype(jnp.float32), weight)

def block_forward(x, mem, gain_all, ws_in, ws_out, wc_q, wc_kv, wc_out, wm_in, wm_out, self_ok, cross_ok, token_valid):
    width = HEADS * HEAD_DIM
    h1 = low(normed(x, gain_all[0]))
    qkv = low(low_back(jnp.einsum('td,hkd->kth', h1, ws_in, precision=HIGHEST)))
    heads_view = qkv.reshape(3, GROUP, HEADS, HEAD_DIM)
    o1 = attend(heads_view[0], heads_view[1], heads_view[2], self_ok).reshape(GROUP, width)
    o1 = low(low_back(o1))
    x1 = x + low_back(jnp.dot(o1, ws_out, precision=HIGHEST))
    h2 = low(normed(x1, gain_all[1]))
    cq = low(low_back(jnp.dot(h2, wc_q.T, precision=HIGHEST)))
    ckv = low(low_back(jnp.einsum('md,hkd->kmh', mem, wc_kv, precision=HIGHEST)))
    o2 = attend(cq.reshape(GROUP, HEADS, HEAD_DIM), ckv[0].reshape(MEM, HEADS, HEAD_DIM), ckv[1].reshape(MEM, HEADS, HEAD_DIM), cross_ok)
    o2 = o2.reshape(GROUP, width) * token_valid[:, None]
    o2 = low(low_back(o2))
    x2 = x1 + low_back(jnp.dot(o2, wc_out, precision=HIGHEST))
    h3 = low(normed(x2, gain_all[2]))
    gate_up = low_back(jnp.einsum('td,fkd->ktf', h3, wm_in, precision=HIGHEST))
    hidden = low(jax.nn.gelu(gate_up[0], approximate=True) * gate_up[1])
    return x2 + low_back(jnp.dot(hidden, wm_out, precision=HIGHEST))

def reference(tokens, memory, item_len, item_kind, norm_gains, w_self_in, w_self_out, w_cross_q, w_cross_kv, w_cross_out, w_mlp_in, w_mlp_out, cotangent):
    params = tuple((w.astype(jnp.float32) for w in (norm_gains, w_self_in, w_self_out, w_cross_q, w_cross_kv, w_cross_out, w_mlp_in, w_mlp_out)))
    tok_groups = tokens.astype(jnp.float32).reshape(GROUPS, GROUP, D)
    mem_groups = memory.astype(jnp.float32).reshape(GROUPS, MEM, D)
    cot_groups = cotangent.astype(jnp.float32).reshape(GROUPS, GROUP, D)

    def group_step(totals, group_data):
        x, mem, cot, lengths, item_kinds = group_data
        self_ok, cross_ok, token_valid, weight = group_masks(lengths, item_kinds)

        def forward(x, mem, *weights):
            return block_forward(x, mem, *weights, self_ok, cross_ok, token_valid)
        result, pullback = jax.vjp(forward, x, mem, *params)
        gradients = pullback(cot * weight[:, None])
        totals = tuple((a + b for a, b in zip(totals, gradients[2:])))
        return (totals, (result.astype(jnp.bfloat16), gradients[0].astype(jnp.bfloat16), gradients[1].astype(jnp.bfloat16)))
    start = tuple((jnp.zeros(w.shape, jnp.float32) for w in params))
    totals, stacked = lax.scan(group_step, start, (tok_groups, mem_groups, cot_groups, item_len, item_kind))
    output = stacked[0].reshape(TOKENS, D)
    grad_tokens = stacked[1].reshape(TOKENS, D)
    grad_memory = stacked[2].reshape(GROUPS * MEM, D)
    return (output, grad_tokens, grad_memory, totals[0], totals[1], totals[2], totals[3], totals[4], totals[5], totals[6], totals[7])
```

```python
import jax
import jax.numpy as jnp
from jax import lax
from jax.sharding import PartitionSpec as P

HEAD_DIM = 128


EPSILON = 1e-06
ROBOT_WEIGHT = 2.0
NEGATIVE = -1e30


def normed(values, gain_row):
    factor = lax.rsqrt(jnp.mean(values * values, axis=-1, keepdims=True) + EPSILON)
    return values * factor * gain_row


def token_info(lengths, item_kinds, positions, item_count):
    item_ends = jnp.cumsum(lengths)
    segment = jnp.sum((positions[:, None] >= item_ends[None, :]).astype(jnp.int32), axis=1)
    token_valid = segment < item_count
    item_hit = segment[:, None] == jnp.arange(item_count, dtype=jnp.int32)[None, :]
    robot_flag = jnp.sum(jnp.where(item_hit, item_kinds[None, :], 0), axis=1)
    weight = jnp.where(token_valid, jnp.where(robot_flag == 1, ROBOT_WEIGHT, 1.0), 0.0).astype(
        jnp.float32
    )
    return (segment, token_valid, weight)


def attend_forward(queries, keys_all, values_all, allowed):
    scores = jnp.einsum(
        "qhd,khd->hqk", queries, keys_all, preferred_element_type=jnp.float32
    ) * HEAD_DIM ** (-0.5)
    scores = jnp.where(allowed[None], scores, NEGATIVE)
    row_top = jnp.max(scores, axis=2, keepdims=True)
    exp_scores = jnp.exp(scores - row_top)
    denom_sum = jnp.sum(exp_scores, axis=2, keepdims=True)
    soft_probs = (exp_scores / denom_sum).astype(jnp.bfloat16)
    result = jnp.einsum("hqk,khd->qhd", soft_probs, values_all, preferred_element_type=jnp.float32)
    return (result, row_top + jnp.log(denom_sum))


def attend_backward(queries, keys_all, values_all, allowed, log_sums, grad_out):
    score_scale = HEAD_DIM ** (-0.5)
    scores = (
        jnp.einsum("qhd,khd->hqk", queries, keys_all, preferred_element_type=jnp.float32)
        * score_scale
    )
    scores = jnp.where(allowed[None], scores, NEGATIVE)
    soft_probs = jnp.exp(scores - log_sums)
    grad_probs = jnp.einsum(
        "qhd,khd->hqk", grad_out, values_all, preferred_element_type=jnp.float32
    )
    row_inner = jnp.sum(soft_probs * grad_probs, axis=2, keepdims=True)
    grad_scores = (soft_probs * (grad_probs - row_inner)).astype(jnp.bfloat16)
    grad_query = (
        jnp.einsum("hqk,khd->qhd", grad_scores, keys_all, preferred_element_type=jnp.float32)
        * score_scale
    )
    grad_keys = (
        jnp.einsum("hqk,qhd->khd", grad_scores, queries, preferred_element_type=jnp.float32)
        * score_scale
    )
    grad_values = jnp.einsum(
        "hqk,qhd->khd",
        soft_probs.astype(jnp.bfloat16),
        grad_out,
        preferred_element_type=jnp.float32,
    )
    return (grad_query, grad_keys, grad_values)


def spread_tables(wide, narrow):
    total = wide * narrow
    ratio = wide // narrow
    if (wide, narrow) == (8, 4):
        first, second, spots = [], [], [[0] * wide for _ in range(narrow)]
        for block in range(total):
            w, n = divmod(block, narrow)
            q, c = divmod(w, ratio)
            z1, z0 = divmod(n, 2)
            spot = 2 * (q ^ (2 * c + z1)) + (z0 ^ c)
            first.append((block, spot * narrow + n))
            second.append((spot * narrow + n, spot * narrow + q))
            spots[q][block - q * wide] = spot
        return (first, second, spots)
    direct = []
    for block in range(total):
        n, w = divmod(block, wide)
        direct.append((block, w * narrow + n))
    return (direct, None, None)


def spread(piece):
    axes = ("wide", "narrow")
    first, second, _ = spread_tables(lax.axis_size("wide"), lax.axis_size("narrow"))
    piece = lax.ppermute(piece, axes, first)
    if second is not None:
        piece = lax.ppermute(piece, axes, second)
    return piece


def wide_gather(pieces):
    rows, width = pieces[0].shape
    moved = spread(jnp.concatenate(pieces, axis=0))
    full = lax.all_gather(moved, "wide", axis=0, tiled=False)
    full = full.reshape(-1, len(pieces), rows, width)
    return tuple(full[:, kind].reshape(-1, width) for kind in range(len(pieces)))


def wide_total(terms):
    wide_count = lax.axis_size("wide")
    width = terms[0].shape[1]
    parts = [term.astype(jnp.bfloat16).reshape(wide_count, -1, width) for term in terms]
    packed = jnp.concatenate(parts, axis=1)
    rows = packed.shape[1]
    shard = lax.psum_scatter(
        packed.reshape(wide_count * rows, width), "wide", scatter_dimension=0, tiled=True
    )
    full = lax.all_gather(shard, "wide", axis=0, tiled=False)
    _, _, spots = spread_tables(wide_count, lax.axis_size("narrow"))
    if spots is not None:
        order = jnp.asarray(spots, jnp.int32)[lax.axis_index("narrow")]
        full = jnp.concatenate(
            [lax.dynamic_slice_in_dim(full, order[j], 1, 0) for j in range(wide_count)], axis=0
        )
    full = full.reshape(wide_count, len(terms), -1, width)
    return [
        full[:, kind].reshape(-1, width).astype(jnp.float32) for kind in range(len(terms))
    ]


def row_gather(local_rows):
    return lax.all_gather(local_rows, "narrow", axis=0, tiled=True)


def branch_sum(partial_rows):
    return lax.psum_scatter(
        partial_rows.astype(jnp.bfloat16), "narrow", scatter_dimension=0, tiled=True
    ).astype(jnp.float32)


def matmul_nt(a, b):
    return lax.dot_general(a, b, (((1,), (1,)), ((), ())), preferred_element_type=jnp.float32)


def matmul_nn(a, b):
    return lax.dot_general(a, b, (((1,), (0,)), ((), ())), preferred_element_type=jnp.float32)


def matmul_tn(a, b):
    return lax.dot_general(a, b, (((0,), (0,)), ((), ())), preferred_element_type=jnp.float32)


def tensor_pass(tokens, memory, gain_float, weights, cotangent, masks):
    segment, token_valid, valid_float, local_weight, self_ok, cross_ok = masks
    tok_rows = tokens.shape[0]
    group_rows = tok_rows * lax.axis_size("narrow")
    mem_group = memory.shape[0] * lax.axis_size("narrow")
    w_self_in, w_self_out, w_cross_q, w_cross_kv, w_cross_out, w_mlp_in, w_mlp_out = weights
    tok_float = tokens.astype(jnp.float32)
    h1 = normed(tok_float, gain_float[0]).astype(jnp.bfloat16)
    rows_one = row_gather(h1)
    ws_q, ws_k, ws_v = wide_gather([w_self_in[:, 0], w_self_in[:, 1], w_self_in[:, 2]])
    ws_out, wc_q, wc_k, wc_v, wc_out = wide_gather(
        [w_self_out, w_cross_q, w_cross_kv[:, 0], w_cross_kv[:, 1], w_cross_out]
    )
    wm_gate, wm_up, wm_out = wide_gather([w_mlp_in[:, 0], w_mlp_in[:, 1], w_mlp_out])
    memory_all = row_gather(memory)
    grad_y = cotangent.astype(jnp.float32) * local_weight[:, None]
    grad_mlp = row_gather(grad_y.astype(jnp.bfloat16))
    own_width = ws_out.shape[0]
    heads_here = own_width // HEAD_DIM

    def split(mat):
        return mat.reshape(mat.shape[0], heads_here, HEAD_DIM)

    def project(rows, mat):
        return matmul_nt(rows, mat).astype(jnp.bfloat16)

    sq, sk, sv = (split(project(rows_one, mat)) for mat in (ws_q, ws_k, ws_v))
    self_result, self_lse = attend_forward(sq, sk, sv, self_ok)
    self_heads = self_result.reshape(group_rows, own_width).astype(jnp.bfloat16)
    x1 = tok_float + branch_sum(matmul_nn(self_heads, ws_out))
    h2 = normed(x1, gain_float[1]).astype(jnp.bfloat16)
    rows_two = row_gather(h2)
    ck, cv = (split(project(memory_all, mat)) for mat in (wc_k, wc_v))
    cq = split(project(rows_two, wc_q))
    cross_result, cross_lse = attend_forward(cq, ck, cv, cross_ok)
    cross_heads = (
        (cross_result * valid_float[:, None, None])
        .reshape(group_rows, own_width)
        .astype(jnp.bfloat16)
    )
    x2 = x1 + branch_sum(matmul_nn(cross_heads, wc_out))
    h3 = normed(x2, gain_float[2]).astype(jnp.bfloat16)
    rows_three = row_gather(h3)
    gate = matmul_nt(rows_three, wm_gate)
    up = matmul_nt(rows_three, wm_up)
    hidden = (jax.nn.gelu(gate, approximate=True) * up).astype(jnp.bfloat16)
    output = (x2 + branch_sum(matmul_nn(hidden, wm_out))).astype(jnp.bfloat16)
    grad_hidden = matmul_nt(grad_mlp, wm_out)
    _, gelu_pull = jax.vjp(
        lambda gate_part, up_part: jax.nn.gelu(gate_part, approximate=True) * up_part, gate, up
    )
    grad_gate, grad_up = gelu_pull(grad_hidden)
    grad_gate = grad_gate.astype(jnp.bfloat16)
    grad_up = grad_up.astype(jnp.bfloat16)
    grad_h3 = branch_sum(matmul_nn(grad_gate, wm_gate) + matmul_nn(grad_up, wm_up))
    _, norm_pull3 = jax.vjp(normed, x2, gain_float[2])
    part_x2, grad_gain3 = norm_pull3(grad_h3)
    grad_x2 = grad_y + part_x2
    mlp_totals = wide_total(
        [
            matmul_tn(grad_gate, rows_three),
            matmul_tn(grad_up, rows_three),
            matmul_tn(hidden, grad_mlp),
        ]
    )
    grad_cross = row_gather(grad_x2.astype(jnp.bfloat16))
    grad_cross_heads = split(project(grad_cross, wc_out))
    grad_cross_heads = jnp.where(
        token_valid[:, None, None], grad_cross_heads, jnp.zeros_like(grad_cross_heads)
    )
    gq_heads, gk_heads, gv_heads = attend_backward(
        cq, ck, cv, cross_ok, cross_lse, grad_cross_heads
    )
    grad_cq = gq_heads.reshape(group_rows, own_width).astype(jnp.bfloat16)
    grad_ck = gk_heads.reshape(mem_group, own_width).astype(jnp.bfloat16)
    grad_cv = gv_heads.reshape(mem_group, own_width).astype(jnp.bfloat16)
    grad_h2 = branch_sum(matmul_nn(grad_cq, wc_q))
    _, norm_pull2 = jax.vjp(normed, x1, gain_float[1])
    part_x1, grad_gain2 = norm_pull2(grad_h2)
    grad_x1 = grad_x2 + part_x1
    grad_self = row_gather(grad_x1.astype(jnp.bfloat16))
    grad_memory = branch_sum(matmul_nn(grad_ck, wc_k) + matmul_nn(grad_cv, wc_v)).astype(
        jnp.bfloat16
    )
    mid_totals = wide_total(
        [
            matmul_tn(self_heads, grad_self),
            matmul_tn(grad_cq, rows_two),
            matmul_tn(grad_ck, memory_all),
            matmul_tn(grad_cv, memory_all),
            matmul_tn(cross_heads, grad_cross),
        ]
    )
    grad_self_heads = split(project(grad_self, ws_out))
    gsq, gsk, gsv = (
        mat.reshape(group_rows, own_width).astype(jnp.bfloat16)
        for mat in attend_backward(sq, sk, sv, self_ok, self_lse, grad_self_heads)
    )
    in_totals = wide_total(
        [matmul_tn(gsq, rows_one), matmul_tn(gsk, rows_one), matmul_tn(gsv, rows_one)]
    )
    grad_h1 = branch_sum(matmul_nn(gsq, ws_q) + matmul_nn(gsk, ws_k) + matmul_nn(gsv, ws_v))
    _, norm_pull1 = jax.vjp(normed, tok_float, gain_float[0])
    part_x, grad_gain1 = norm_pull1(grad_h1)
    grad_tokens = (grad_x1 + part_x).astype(jnp.bfloat16)
    gain_terms = jnp.stack([grad_gain1, grad_gain2, grad_gain3])
    return (output, grad_tokens, grad_memory, gain_terms, in_totals, mid_totals, mlp_totals)


def per_device_general(
    tokens,
    memory,
    item_len,
    item_kind,
    norm_gains,
    w_self_in,
    w_self_out,
    w_cross_q,
    w_cross_kv,
    w_cross_out,
    w_mlp_in,
    w_mlp_out,
    cotangent,
):
    tok_rows = tokens.shape[0]
    narrow_size = lax.axis_size("narrow")
    group_rows = tok_rows * narrow_size
    mem_group = memory.shape[0] * narrow_size
    lengths = item_len[0]
    item_count = lengths.shape[0]
    patch_rows = mem_group // item_count
    positions = jnp.arange(group_rows, dtype=jnp.int32)
    segment, token_valid, weight = token_info(lengths, item_kind[0], positions, item_count)
    local_weight = lax.dynamic_slice_in_dim(weight, lax.axis_index("narrow") * tok_rows, tok_rows)
    self_ok = (segment[:, None] == segment[None, :]) & (positions[None, :] <= positions[:, None])
    mem_item = jnp.arange(mem_group, dtype=jnp.int32) // patch_rows
    cross_ok = mem_item[None, :] == jnp.minimum(segment, item_count - 1)[:, None]
    valid_float = token_valid.astype(jnp.float32)
    masks = (segment, token_valid, valid_float, local_weight, self_ok, cross_ok)
    gain_float = norm_gains.astype(jnp.float32)
    weights = (w_self_in, w_self_out, w_cross_q, w_cross_kv, w_cross_out, w_mlp_in, w_mlp_out)
    output, grad_tokens, grad_memory, gain_terms, in_totals, mid_totals, mlp_totals = tensor_pass(
        tokens, memory, gain_float, weights, cotangent, masks
    )
    gain_shard = lax.psum_scatter(gain_terms, "narrow", scatter_dimension=1, tiled=True)
    gain_total = lax.psum(gain_shard, "wide")
    return (
        output,
        grad_tokens,
        grad_memory,
        gain_total,
        jnp.stack(in_totals, axis=1),
        mid_totals[0],
        mid_totals[1],
        jnp.stack([mid_totals[2], mid_totals[3]], axis=1),
        mid_totals[4],
        jnp.stack([mlp_totals[0], mlp_totals[1]], axis=1),
        mlp_totals[2],
    )


CORE, XDIM, YDIM = 1, 2, 4
PLANE = 8


def flip(value, bit):
    return lax.ppermute(value, "wide", [(i, i ^ bit) for i in range(PLANE)])


def unspread(piece):
    axes = ("wide", "narrow")
    first, second, _ = spread_tables(lax.axis_size("wide"), lax.axis_size("narrow"))
    piece = lax.ppermute(piece, axes, [(b, a) for a, b in second])
    return lax.ppermute(piece, axes, [(b, a) for a, b in first])


def plane_pieces(shard):
    half = shard.shape[0] // 2
    over_x = flip(shard, XDIM)
    over_y = flip(shard, YDIM)
    over_xy = (flip(over_x[:half], YDIM), flip(over_y[half:], XDIM))
    own = [(shard[:half], shard[half:]), (over_x[:half], over_x[half:])]
    own += [(over_y[:half], over_y[half:]), over_xy]
    partner = [flip(shard, CORE), flip(over_x, CORE), flip(over_y, CORE)]
    partner = [(part[:half], part[half:]) for part in partner]
    partner.append((flip(over_xy[0], CORE), flip(over_xy[1], CORE)))
    return [pair for both in zip(own, partner) for pair in both]


def plane_gather(shard):
    return jnp.concatenate([part for pair in plane_pieces(shard) for part in pair], axis=0)


def low(value):
    return value.astype(jnp.bfloat16)


def plus(kept, moved):
    return kept.astype(jnp.float32) + moved.astype(jnp.float32)


def plane_scatter(partial_rows):
    rows = partial_rows.shape[0] // PLANE
    half = rows // 2
    view = partial_rows.reshape(2, 2, 2, rows, -1)
    chip = low(plus(view[:, :, 0], flip(low(view[:, :, 1]), CORE)))
    part_a, part_b = chip[:, :, :half], chip[:, :, half:]
    part_a = plus(part_a[:, 0], flip(part_a[:, 1], XDIM))
    part_b = plus(part_b[0], flip(part_b[1], YDIM))
    done_a = plus(part_a[0], flip(low(part_a[1]), YDIM))
    done_b = plus(part_b[0], flip(low(part_b[1]), XDIM))
    return jnp.concatenate([done_a, done_b], axis=0)


def group_attend(queries, keys_all, values_all, allowed):
    scores = jnp.einsum(
        "gqhd,gkhd->ghqk", queries, keys_all, preferred_element_type=jnp.float32
    ) * HEAD_DIM ** (-0.5)
    scores = jnp.where(allowed[:, None], scores, NEGATIVE)
    row_top = jnp.max(scores, axis=3, keepdims=True)
    exp_scores = jnp.exp(scores - row_top)
    denom_sum = jnp.sum(exp_scores, axis=3, keepdims=True)
    soft_probs = low(exp_scores / denom_sum)
    result = jnp.einsum(
        "ghqk,gkhd->gqhd", soft_probs, values_all, preferred_element_type=jnp.float32
    )
    return (result, row_top + jnp.log(denom_sum))


def group_attend_back(queries, keys_all, values_all, allowed, log_sums, grad_out):
    score_scale = HEAD_DIM ** (-0.5)
    scores = (
        jnp.einsum("gqhd,gkhd->ghqk", queries, keys_all, preferred_element_type=jnp.float32)
        * score_scale
    )
    scores = jnp.where(allowed[:, None], scores, NEGATIVE)
    soft_probs = jnp.exp(scores - log_sums)
    grad_probs = jnp.einsum(
        "gqhd,gkhd->ghqk", grad_out, values_all, preferred_element_type=jnp.float32
    )
    row_inner = jnp.sum(soft_probs * grad_probs, axis=3, keepdims=True)
    grad_scores = low(soft_probs * (grad_probs - row_inner))
    grad_query = (
        jnp.einsum("ghqk,gkhd->gqhd", grad_scores, keys_all, preferred_element_type=jnp.float32)
        * score_scale
    )
    grad_keys = (
        jnp.einsum("ghqk,gqhd->gkhd", grad_scores, queries, preferred_element_type=jnp.float32)
        * score_scale
    )
    grad_values = jnp.einsum(
        "ghqk,gqhd->gkhd", low(soft_probs), grad_out, preferred_element_type=jnp.float32
    )
    return (grad_query, grad_keys, grad_values)


def narrow_full(pieces):
    rows, width = pieces[0].shape
    full = lax.all_gather(jnp.concatenate(pieces, axis=0), "narrow", axis=0, tiled=False)
    full = full.reshape(-1, len(pieces), rows, width)
    return [full[:, kind].reshape(-1, width) for kind in range(len(pieces))]


def narrow_total(term):
    return lax.psum_scatter(low(term), "narrow", scatter_dimension=0, tiled=True)


def placed(shards, spot_zero):
    rows = shards[0].shape[0]
    moved = spread(jnp.concatenate(shards, axis=0))
    kinds = len(shards)
    stacked = plane_gather(
        moved.reshape(kinds, 2, rows // 2, -1).swapaxes(0, 1).reshape(kinds * rows, -1)
    )
    width = stacked.shape[-1]
    stacked = stacked.reshape(PLANE, 2, kinds, rows // 2, width)
    order = [0] * PLANE
    for e in range(PLANE):
        ey, ex, ec = e >> 2, (e >> 1) & 1, e & 1
        order[4 * ey + 2 * ex + (ec ^ ey)] = e
    outs = []
    for kind in range(kinds):
        by_flip = jnp.stack([stacked[e, :, kind].reshape(rows, width) for e in order], axis=0)
        blocks = [
            lax.dynamic_index_in_dim(by_flip, spot_zero ^ j, 0, keepdims=False)
            for j in range(PLANE)
        ]
        outs.append(jnp.concatenate(blocks, axis=0).astype(jnp.float32))
    return outs


def per_device(
    tokens,
    memory,
    item_len,
    item_kind,
    norm_gains,
    w_self_in,
    w_self_out,
    w_cross_q,
    w_cross_kv,
    w_cross_out,
    w_mlp_in,
    w_mlp_out,
    cotangent,
):
    tok_rows, width = tokens.shape
    mem_rows = memory.shape[0]
    item_count = item_len.shape[1]
    gain = norm_gains.astype(jnp.float32)
    x = spread(tokens).astype(jnp.float32)
    h1 = low(normed(x, gain[0]))
    rows_one = plane_gather(h1)
    ws_q, ws_k, ws_v = narrow_full([w_self_in[:, 0], w_self_in[:, 1], w_self_in[:, 2]])
    ws_out, wc_q = narrow_full([w_self_out, w_cross_q])
    wc_k, wc_v = narrow_full([w_cross_kv[:, 0], w_cross_kv[:, 1]])
    (wc_out,) = narrow_full([w_cross_out])
    memory_all = plane_gather(spread(memory))
    units = w_mlp_out.shape[0] // 2
    mlp_shard = jnp.concatenate(
        [
            part[lo : lo + units]
            for lo in (0, units)
            for part in (w_mlp_in[:, 0], w_mlp_in[:, 1], w_mlp_out)
        ],
        axis=0,
    )
    mlp_pieces = plane_pieces(mlp_shard)
    wm_gate, wm_up, wm_out = (
        jnp.concatenate(
            [part[kind * units : (kind + 1) * units] for pair in mlp_pieces for part in pair],
            axis=0,
        )
        for kind in range(3)
    )

    me, level = lax.axis_index("wide"), lax.axis_index("narrow")
    differ = (me >> 1) ^ level
    side, upper = differ >> 1, differ & 1
    quarter = 2 * upper + ((me & 1) ^ side)
    spot_zero = 4 * side + quarter
    info_own = spread(jnp.concatenate([item_len, item_kind], axis=1))
    info = jnp.stack([info_own[0], flip(info_own, YDIM)[0]], axis=0)
    order = jnp.arange(PLANE // 2, dtype=jnp.int32)
    quarters = jnp.stack([quarter ^ order, quarter ^ 1 ^ order], axis=0)
    positions = (
        quarters[:, :, None] * tok_rows + jnp.arange(tok_rows, dtype=jnp.int32)
    ).reshape(2, -1)
    segment, token_valid, weight = jax.vmap(token_info, in_axes=(0, 0, 0, None))(
        info[:, :item_count], info[:, item_count:], positions, item_count
    )
    local_weight = weight[0, :tok_rows]
    self_ok = (segment[:, :, None] == segment[:, None, :]) & (
        positions[:, None, :] <= positions[:, :, None]
    )
    patch_rows = mem_rows * (PLANE // 2) // item_count
    mem_item = (
        (quarters[:, :, None] * mem_rows + jnp.arange(mem_rows, dtype=jnp.int32)) // patch_rows
    ).reshape(2, -1)
    cross_ok = mem_item[:, None, :] == jnp.minimum(segment, item_count - 1)[:, :, None]
    valid_float = token_valid.astype(jnp.float32)

    own_width = ws_out.shape[0]
    heads_here = own_width // HEAD_DIM

    def split(mat):
        return mat.reshape(2, -1, heads_here, HEAD_DIM)

    def merge(mat):
        return low(mat.reshape(-1, own_width))

    def project(rows, mat):
        return low(matmul_nt(rows, mat))

    sq, sk, sv = (split(project(rows_one, mat)) for mat in (ws_q, ws_k, ws_v))
    self_result, self_lse = group_attend(sq, sk, sv, self_ok)
    self_heads = merge(self_result)
    x1 = x + plane_scatter(matmul_nn(self_heads, ws_out))
    h2 = low(normed(x1, gain[1]))
    rows_two = plane_gather(h2)
    ck, cv = (split(project(memory_all, mat)) for mat in (wc_k, wc_v))
    cq = split(project(rows_two, wc_q))
    cross_result, cross_lse = group_attend(cq, ck, cv, cross_ok)
    cross_heads = merge(cross_result * valid_float[:, :, None, None])
    x2 = x1 + plane_scatter(matmul_nn(cross_heads, wc_out))
    h3 = low(normed(x2, gain[2]))
    grad_y = spread(cotangent).astype(jnp.float32) * local_weight[:, None]
    grad_mlp = row_gather(low(grad_y))
    rows_three = row_gather(h3)
    gate = matmul_nt(rows_three, wm_gate)
    up = matmul_nt(rows_three, wm_up)
    hidden = low(jax.nn.gelu(gate, approximate=True) * up)
    grad_hidden = matmul_nt(grad_mlp, wm_out)
    _, gelu_pull = jax.vjp(
        lambda gate_part, up_part: jax.nn.gelu(gate_part, approximate=True) * up_part, gate, up
    )
    grad_gate, grad_up = gelu_pull(grad_hidden)
    grad_gate, grad_up = low(grad_gate), low(grad_up)
    grad_h3 = branch_sum(matmul_nn(grad_gate, wm_gate) + matmul_nn(grad_up, wm_up))
    output = unspread(low(x2 + branch_sum(matmul_nn(hidden, wm_out))))
    _, norm_pull3 = jax.vjp(normed, x2, gain[2])
    part_x2, grad_gain3 = norm_pull3(grad_h3)
    grad_x2 = grad_y + part_x2
    grad_cross = plane_gather(low(grad_x2))
    mlp_totals = placed(
        [
            low(plane_scatter(matmul_tn(term, rows)))
            for term, rows in (
                (grad_gate, rows_three),
                (grad_up, rows_three),
                (hidden, grad_mlp),
            )
        ],
        spot_zero,
    )
    grad_cross_heads = split(project(grad_cross, wc_out))
    grad_cross_heads = jnp.where(
        token_valid[:, :, None, None], grad_cross_heads, jnp.zeros_like(grad_cross_heads)
    )
    grad_cq, grad_ck, grad_cv = (
        merge(mat)
        for mat in group_attend_back(cq, ck, cv, cross_ok, cross_lse, grad_cross_heads)
    )
    grad_h2 = plane_scatter(matmul_nn(grad_cq, wc_q))
    _, norm_pull2 = jax.vjp(normed, x1, gain[1])
    part_x1, grad_gain2 = norm_pull2(grad_h2)
    grad_x1 = grad_x2 + part_x1
    grad_self = plane_gather(low(grad_x1))
    mid_totals = placed(
        [
            narrow_total(matmul_tn(cross_heads, grad_cross)),
            narrow_total(matmul_tn(grad_cv, memory_all)),
            narrow_total(matmul_tn(grad_ck, memory_all)),
            narrow_total(matmul_tn(grad_cq, rows_two)),
            narrow_total(matmul_tn(self_heads, grad_self)),
        ],
        spot_zero,
    )
    grad_memory = unspread(
        low(plane_scatter(matmul_nn(grad_ck, wc_k) + matmul_nn(grad_cv, wc_v)))
    )
    grad_self_heads = split(project(grad_self, ws_out))
    gsq, gsk, gsv = (
        merge(mat) for mat in group_attend_back(sq, sk, sv, self_ok, self_lse, grad_self_heads)
    )
    in_totals = placed(
        [narrow_total(matmul_tn(term, rows_one)) for term in (gsq, gsk, gsv)], spot_zero
    )
    grad_h1 = plane_scatter(matmul_nn(gsq, ws_q) + matmul_nn(gsk, ws_k) + matmul_nn(gsv, ws_v))
    _, norm_pull1 = jax.vjp(normed, x, gain[0])
    part_x, grad_gain1 = norm_pull1(grad_h1)
    grad_tokens = unspread(low(grad_x1 + part_x))
    gain_terms = lax.psum(jnp.stack([grad_gain1, grad_gain2, grad_gain3]), ("wide", "narrow"))
    own_gains = width // lax.axis_size("narrow")
    return (
        output,
        grad_tokens,
        grad_memory,
        lax.dynamic_slice_in_dim(gain_terms, level * own_gains, own_gains, 1),
        jnp.stack(in_totals, axis=1),
        mid_totals[4],
        mid_totals[3],
        jnp.stack([mid_totals[2], mid_totals[1]], axis=1),
        mid_totals[0],
        jnp.stack([mlp_totals[0], mlp_totals[1]], axis=1),
        mlp_totals[2],
    )


def solution(mesh):
    in_plane = (mesh.shape["wide"], mesh.shape["narrow"]) == (8, 4)
    return jax.shard_map(
        per_device if in_plane else per_device_general,
        mesh=mesh,
        in_specs=(
            P(("wide", "narrow"), None),
            P(("wide", "narrow"), None),
            P("wide", None),
            P("wide", None),
            P(),
            P(("wide", "narrow"), None, None),
            P(("wide", "narrow"), None),
            P(("wide", "narrow"), None),
            P(("wide", "narrow"), None, None),
            P(("wide", "narrow"), None),
            P(("wide", "narrow"), None, None),
            P(("wide", "narrow"), None),
            P(("wide", "narrow"), None),
        ),
        out_specs=(
            P(("wide", "narrow"), None),
            P(("wide", "narrow"), None),
            P(("wide", "narrow"), None),
            P(None, "narrow"),
            P("narrow", None, None),
            P("narrow", None),
            P("narrow", None),
            P("narrow", None, None),
            P("narrow", None),
            P("narrow", None, None),
            P("narrow", None),
        ),
        check_vma=False,
    )
```

```python
import jax
import jax.numpy as jnp
from jax import lax
from jax.experimental import pallas as pl
from jax.experimental.pallas import tpu as pltpu
from jax.sharding import PartitionSpec as P

HEAD_DIM = 128


EPSILON = 1e-06
ROBOT_WEIGHT = 2.0
NEGATIVE = -1e30


def normed(values, gain_row):
    factor = lax.rsqrt(jnp.mean(values * values, axis=-1, keepdims=True) + EPSILON)
    return values * factor * gain_row


def token_info(lengths, item_kinds, positions, item_count):
    item_ends = jnp.cumsum(lengths)
    segment = jnp.sum((positions[:, None] >= item_ends[None, :]).astype(jnp.int32), axis=1)
    token_valid = segment < item_count
    item_hit = segment[:, None] == jnp.arange(item_count, dtype=jnp.int32)[None, :]
    robot_flag = jnp.sum(jnp.where(item_hit, item_kinds[None, :], 0), axis=1)
    weight = jnp.where(token_valid, jnp.where(robot_flag == 1, ROBOT_WEIGHT, 1.0), 0.0).astype(
        jnp.float32
    )
    return (segment, token_valid, weight)


def attend_forward(queries, keys_all, values_all, allowed):
    scores = jnp.einsum(
        "qhd,khd->hqk", queries, keys_all, preferred_element_type=jnp.float32
    ) * HEAD_DIM ** (-0.5)
    scores = jnp.where(allowed[None], scores, NEGATIVE)
    row_top = jnp.max(scores, axis=2, keepdims=True)
    exp_scores = jnp.exp(scores - row_top)
    denom_sum = jnp.sum(exp_scores, axis=2, keepdims=True)
    soft_probs = (exp_scores / denom_sum).astype(jnp.bfloat16)
    result = jnp.einsum("hqk,khd->qhd", soft_probs, values_all, preferred_element_type=jnp.float32)
    return (result, row_top + jnp.log(denom_sum))


def attend_backward(queries, keys_all, values_all, allowed, log_sums, grad_out):
    score_scale = HEAD_DIM ** (-0.5)
    scores = (
        jnp.einsum("qhd,khd->hqk", queries, keys_all, preferred_element_type=jnp.float32)
        * score_scale
    )
    scores = jnp.where(allowed[None], scores, NEGATIVE)
    soft_probs = jnp.exp(scores - log_sums)
    grad_probs = jnp.einsum(
        "qhd,khd->hqk", grad_out, values_all, preferred_element_type=jnp.float32
    )
    row_inner = jnp.sum(soft_probs * grad_probs, axis=2, keepdims=True)
    grad_scores = (soft_probs * (grad_probs - row_inner)).astype(jnp.bfloat16)
    grad_query = (
        jnp.einsum("hqk,khd->qhd", grad_scores, keys_all, preferred_element_type=jnp.float32)
        * score_scale
    )
    grad_keys = (
        jnp.einsum("hqk,qhd->khd", grad_scores, queries, preferred_element_type=jnp.float32)
        * score_scale
    )
    grad_values = jnp.einsum(
        "hqk,qhd->khd",
        soft_probs.astype(jnp.bfloat16),
        grad_out,
        preferred_element_type=jnp.float32,
    )
    return (grad_query, grad_keys, grad_values)


def spread_tables(wide, narrow):
    total = wide * narrow
    ratio = wide // narrow
    if (wide, narrow) == (8, 4):
        first, second, spots = [], [], [[0] * wide for _ in range(narrow)]
        for block in range(total):
            w, n = divmod(block, narrow)
            q, c = divmod(w, ratio)
            z1, z0 = divmod(n, 2)
            spot = 2 * (q ^ (2 * c + z1)) + (z0 ^ c)
            first.append((block, spot * narrow + n))
            second.append((spot * narrow + n, spot * narrow + q))
            spots[q][block - q * wide] = spot
        return (first, second, spots)
    direct = []
    for block in range(total):
        n, w = divmod(block, wide)
        direct.append((block, w * narrow + n))
    return (direct, None, None)


def spread(piece):
    axes = ("wide", "narrow")
    first, second, _ = spread_tables(lax.axis_size("wide"), lax.axis_size("narrow"))
    piece = lax.ppermute(piece, axes, first)
    if second is not None:
        piece = lax.ppermute(piece, axes, second)
    return piece


def plane_hop(piece):
    first, _, _ = spread_tables(lax.axis_size("wide"), lax.axis_size("narrow"))
    return lax.ppermute(piece, ("wide", "narrow"), first)


def level_hop(piece):
    _, second, _ = spread_tables(lax.axis_size("wide"), lax.axis_size("narrow"))
    return lax.ppermute(piece, ("wide", "narrow"), second)


def wide_gather(pieces):
    rows, width = pieces[0].shape
    moved = spread(jnp.concatenate(pieces, axis=0))
    full = lax.all_gather(moved, "wide", axis=0, tiled=False)
    full = full.reshape(-1, len(pieces), rows, width)
    return tuple(full[:, kind].reshape(-1, width) for kind in range(len(pieces)))


def wide_total(terms):
    wide_count = lax.axis_size("wide")
    width = terms[0].shape[1]
    parts = [term.astype(jnp.bfloat16).reshape(wide_count, -1, width) for term in terms]
    packed = jnp.concatenate(parts, axis=1)
    rows = packed.shape[1]
    shard = lax.psum_scatter(
        packed.reshape(wide_count * rows, width), "wide", scatter_dimension=0, tiled=True
    )
    full = lax.all_gather(shard, "wide", axis=0, tiled=False)
    _, _, spots = spread_tables(wide_count, lax.axis_size("narrow"))
    if spots is not None:
        order = jnp.asarray(spots, jnp.int32)[lax.axis_index("narrow")]
        full = jnp.concatenate(
            [lax.dynamic_slice_in_dim(full, order[j], 1, 0) for j in range(wide_count)], axis=0
        )
    full = full.reshape(wide_count, len(terms), -1, width)
    return [
        full[:, kind].reshape(-1, width).astype(jnp.float32) for kind in range(len(terms))
    ]


def row_gather(local_rows):
    return lax.all_gather(local_rows, "narrow", axis=0, tiled=True)


def branch_sum(partial_rows):
    return lax.psum_scatter(
        partial_rows.astype(jnp.bfloat16), "narrow", scatter_dimension=0, tiled=True
    ).astype(jnp.float32)


def matmul_nt(a, b):
    return lax.dot_general(a, b, (((1,), (1,)), ((), ())), preferred_element_type=jnp.float32)


def matmul_nn(a, b):
    return lax.dot_general(a, b, (((1,), (0,)), ((), ())), preferred_element_type=jnp.float32)


def matmul_tn(a, b):
    return lax.dot_general(a, b, (((0,), (0,)), ((), ())), preferred_element_type=jnp.float32)


def tensor_pass(tokens, memory, gain_float, weights, cotangent, masks):
    segment, token_valid, valid_float, local_weight, self_ok, cross_ok = masks
    tok_rows = tokens.shape[0]
    group_rows = tok_rows * lax.axis_size("narrow")
    mem_group = memory.shape[0] * lax.axis_size("narrow")
    w_self_in, w_self_out, w_cross_q, w_cross_kv, w_cross_out, w_mlp_in, w_mlp_out = weights
    tok_float = tokens.astype(jnp.float32)
    h1 = normed(tok_float, gain_float[0]).astype(jnp.bfloat16)
    rows_one = row_gather(h1)
    ws_q, ws_k, ws_v = wide_gather([w_self_in[:, 0], w_self_in[:, 1], w_self_in[:, 2]])
    ws_out, wc_q, wc_k, wc_v, wc_out = wide_gather(
        [w_self_out, w_cross_q, w_cross_kv[:, 0], w_cross_kv[:, 1], w_cross_out]
    )
    wm_gate, wm_up, wm_out = wide_gather([w_mlp_in[:, 0], w_mlp_in[:, 1], w_mlp_out])
    memory_all = row_gather(memory)
    grad_y = cotangent.astype(jnp.float32) * local_weight[:, None]
    grad_mlp = row_gather(grad_y.astype(jnp.bfloat16))
    own_width = ws_out.shape[0]
    heads_here = own_width // HEAD_DIM

    def split(mat):
        return mat.reshape(mat.shape[0], heads_here, HEAD_DIM)

    def project(rows, mat):
        return matmul_nt(rows, mat).astype(jnp.bfloat16)

    sq, sk, sv = (split(project(rows_one, mat)) for mat in (ws_q, ws_k, ws_v))
    self_result, self_lse = attend_forward(sq, sk, sv, self_ok)
    self_heads = self_result.reshape(group_rows, own_width).astype(jnp.bfloat16)
    x1 = tok_float + branch_sum(matmul_nn(self_heads, ws_out))
    h2 = normed(x1, gain_float[1]).astype(jnp.bfloat16)
    rows_two = row_gather(h2)
    ck, cv = (split(project(memory_all, mat)) for mat in (wc_k, wc_v))
    cq = split(project(rows_two, wc_q))
    cross_result, cross_lse = attend_forward(cq, ck, cv, cross_ok)
    cross_heads = (
        (cross_result * valid_float[:, None, None])
        .reshape(group_rows, own_width)
        .astype(jnp.bfloat16)
    )
    x2 = x1 + branch_sum(matmul_nn(cross_heads, wc_out))
    h3 = normed(x2, gain_float[2]).astype(jnp.bfloat16)
    rows_three = row_gather(h3)
    gate = matmul_nt(rows_three, wm_gate)
    up = matmul_nt(rows_three, wm_up)
    hidden = (jax.nn.gelu(gate, approximate=True) * up).astype(jnp.bfloat16)
    output = (x2 + branch_sum(matmul_nn(hidden, wm_out))).astype(jnp.bfloat16)
    grad_hidden = matmul_nt(grad_mlp, wm_out)
    _, gelu_pull = jax.vjp(
        lambda gate_part, up_part: jax.nn.gelu(gate_part, approximate=True) * up_part, gate, up
    )
    grad_gate, grad_up = gelu_pull(grad_hidden)
    grad_gate = grad_gate.astype(jnp.bfloat16)
    grad_up = grad_up.astype(jnp.bfloat16)
    grad_h3 = branch_sum(matmul_nn(grad_gate, wm_gate) + matmul_nn(grad_up, wm_up))
    _, norm_pull3 = jax.vjp(normed, x2, gain_float[2])
    part_x2, grad_gain3 = norm_pull3(grad_h3)
    grad_x2 = grad_y + part_x2
    mlp_totals = wide_total(
        [
            matmul_tn(grad_gate, rows_three),
            matmul_tn(grad_up, rows_three),
            matmul_tn(hidden, grad_mlp),
        ]
    )
    grad_cross = row_gather(grad_x2.astype(jnp.bfloat16))
    grad_cross_heads = split(project(grad_cross, wc_out))
    grad_cross_heads = jnp.where(
        token_valid[:, None, None], grad_cross_heads, jnp.zeros_like(grad_cross_heads)
    )
    gq_heads, gk_heads, gv_heads = attend_backward(
        cq, ck, cv, cross_ok, cross_lse, grad_cross_heads
    )
    grad_cq = gq_heads.reshape(group_rows, own_width).astype(jnp.bfloat16)
    grad_ck = gk_heads.reshape(mem_group, own_width).astype(jnp.bfloat16)
    grad_cv = gv_heads.reshape(mem_group, own_width).astype(jnp.bfloat16)
    grad_h2 = branch_sum(matmul_nn(grad_cq, wc_q))
    _, norm_pull2 = jax.vjp(normed, x1, gain_float[1])
    part_x1, grad_gain2 = norm_pull2(grad_h2)
    grad_x1 = grad_x2 + part_x1
    grad_self = row_gather(grad_x1.astype(jnp.bfloat16))
    grad_memory = branch_sum(matmul_nn(grad_ck, wc_k) + matmul_nn(grad_cv, wc_v)).astype(
        jnp.bfloat16
    )
    mid_totals = wide_total(
        [
            matmul_tn(self_heads, grad_self),
            matmul_tn(grad_cq, rows_two),
            matmul_tn(grad_ck, memory_all),
            matmul_tn(grad_cv, memory_all),
            matmul_tn(cross_heads, grad_cross),
        ]
    )
    grad_self_heads = split(project(grad_self, ws_out))
    gsq, gsk, gsv = (
        mat.reshape(group_rows, own_width).astype(jnp.bfloat16)
        for mat in attend_backward(sq, sk, sv, self_ok, self_lse, grad_self_heads)
    )
    in_totals = wide_total(
        [matmul_tn(gsq, rows_one), matmul_tn(gsk, rows_one), matmul_tn(gsv, rows_one)]
    )
    grad_h1 = branch_sum(matmul_nn(gsq, ws_q) + matmul_nn(gsk, ws_k) + matmul_nn(gsv, ws_v))
    _, norm_pull1 = jax.vjp(normed, tok_float, gain_float[0])
    part_x, grad_gain1 = norm_pull1(grad_h1)
    grad_tokens = (grad_x1 + part_x).astype(jnp.bfloat16)
    gain_terms = jnp.stack([grad_gain1, grad_gain2, grad_gain3])
    return (output, grad_tokens, grad_memory, gain_terms, in_totals, mid_totals, mlp_totals)


def per_device_general(
    tokens,
    memory,
    item_len,
    item_kind,
    norm_gains,
    w_self_in,
    w_self_out,
    w_cross_q,
    w_cross_kv,
    w_cross_out,
    w_mlp_in,
    w_mlp_out,
    cotangent,
):
    tok_rows = tokens.shape[0]
    narrow_size = lax.axis_size("narrow")
    group_rows = tok_rows * narrow_size
    mem_group = memory.shape[0] * narrow_size
    lengths = item_len[0]
    item_count = lengths.shape[0]
    patch_rows = mem_group // item_count
    positions = jnp.arange(group_rows, dtype=jnp.int32)
    segment, token_valid, weight = token_info(lengths, item_kind[0], positions, item_count)
    local_weight = lax.dynamic_slice_in_dim(weight, lax.axis_index("narrow") * tok_rows, tok_rows)
    self_ok = (segment[:, None] == segment[None, :]) & (positions[None, :] <= positions[:, None])
    mem_item = jnp.arange(mem_group, dtype=jnp.int32) // patch_rows
    cross_ok = mem_item[None, :] == jnp.minimum(segment, item_count - 1)[:, None]
    valid_float = token_valid.astype(jnp.float32)
    masks = (segment, token_valid, valid_float, local_weight, self_ok, cross_ok)
    gain_float = norm_gains.astype(jnp.float32)
    weights = (w_self_in, w_self_out, w_cross_q, w_cross_kv, w_cross_out, w_mlp_in, w_mlp_out)
    output, grad_tokens, grad_memory, gain_terms, in_totals, mid_totals, mlp_totals = tensor_pass(
        tokens, memory, gain_float, weights, cotangent, masks
    )
    gain_shard = lax.psum_scatter(gain_terms, "narrow", scatter_dimension=1, tiled=True)
    gain_total = lax.psum(gain_shard, "wide")
    return (
        output,
        grad_tokens,
        grad_memory,
        gain_total,
        jnp.stack(in_totals, axis=1),
        mid_totals[0],
        mid_totals[1],
        jnp.stack([mid_totals[2], mid_totals[3]], axis=1),
        mid_totals[4],
        jnp.stack([mlp_totals[0], mlp_totals[1]], axis=1),
        mlp_totals[2],
    )


CORE, XDIM, YDIM = 1, 2, 4
PLANE = 8


def flip(value, bit):
    return lax.ppermute(value, "wide", [(i, i ^ bit) for i in range(PLANE)])


def unspread(piece):
    axes = ("wide", "narrow")
    first, second, _ = spread_tables(lax.axis_size("wide"), lax.axis_size("narrow"))
    piece = lax.ppermute(piece, axes, [(b, a) for a, b in second])
    return lax.ppermute(piece, axes, [(b, a) for a, b in first])


def after(value, *others):
    return lax.optimization_barrier((value,) + others)[0]


def low(value):
    return jax.tree.map(lambda part: part.astype(jnp.bfloat16), value)


def plus(kept, moved):
    return kept.astype(jnp.float32) + moved.astype(jnp.float32)


def side_pieces(shard):
    return [shard, flip(shard, XDIM), flip(shard, YDIM)]


def corner_pieces(sides):
    half = sides[0].shape[-2] // 2
    return sides + [flip(sides[1][..., :half, :], YDIM), flip(sides[2][..., half:, :], XDIM)]


def chip_pieces(shard):
    return corner_pieces(side_pieces(shard))


def plane_gather(shard):
    own = jnp.concatenate(chip_pieces(shard), axis=0)
    return (own, flip(own, CORE))


def plane_scatter(kept, sent):
    return scatter_end(*scatter_start(kept, sent))


def scatter_start(kept, sent):
    chip = low(plus(kept, flip(low(sent), CORE)))
    lead, rows, width = chip.shape[:-2], chip.shape[-2] // 4, chip.shape[-1]
    half = rows // 2
    view = jnp.moveaxis(chip.reshape(lead + (2, 2, rows, width)), (-4, -3), (0, 1))
    part_a, part_b = view[..., :half, :], view[..., half:, :]
    part_a = plus(part_a[:, 0], flip(part_a[:, 1], XDIM))
    part_b = plus(part_b[0], flip(part_b[1], YDIM))
    return (part_a, part_b)


def scatter_end(part_a, part_b):
    done_a = plus(part_a[0], flip(low(part_a[1]), YDIM))
    done_b = plus(part_b[0], flip(low(part_b[1]), XDIM))
    return jnp.concatenate([done_a, done_b], axis=-2)


def group_attend(queries, keys_all, values_all, allowed):
    scores = jnp.einsum(
        "gqhd,gkhd->ghqk", queries, keys_all, preferred_element_type=jnp.float32
    ) * HEAD_DIM ** (-0.5)
    scores = jnp.where(allowed[:, None], scores, NEGATIVE)
    row_top = jnp.max(scores, axis=3, keepdims=True)
    exp_scores = jnp.exp(scores - row_top)
    denom_sum = jnp.sum(exp_scores, axis=3, keepdims=True)
    soft_probs = low(exp_scores / denom_sum)
    result = jnp.einsum(
        "ghqk,gkhd->gqhd", soft_probs, values_all, preferred_element_type=jnp.float32
    )
    return (result, row_top + jnp.log(denom_sum))


def group_attend_back(queries, keys_all, values_all, allowed, log_sums, grad_out):
    score_scale = HEAD_DIM ** (-0.5)
    scores = (
        jnp.einsum("gqhd,gkhd->ghqk", queries, keys_all, preferred_element_type=jnp.float32)
        * score_scale
    )
    scores = jnp.where(allowed[:, None], scores, NEGATIVE)
    soft_probs = jnp.exp(scores - log_sums)
    grad_probs = jnp.einsum(
        "gqhd,gkhd->ghqk", grad_out, values_all, preferred_element_type=jnp.float32
    )
    row_inner = jnp.sum(soft_probs * grad_probs, axis=3, keepdims=True)
    grad_scores = low(soft_probs * (grad_probs - row_inner))
    grad_query = (
        jnp.einsum("ghqk,gkhd->gqhd", grad_scores, keys_all, preferred_element_type=jnp.float32)
        * score_scale
    )
    grad_keys = (
        jnp.einsum("ghqk,gqhd->gkhd", grad_scores, queries, preferred_element_type=jnp.float32)
        * score_scale
    )
    grad_values = jnp.einsum(
        "ghqk,gqhd->gkhd", low(soft_probs), grad_out, preferred_element_type=jnp.float32
    )
    return (grad_query, grad_keys, grad_values)


def narrow_full(stacked):
    kinds, rows, width = stacked.shape
    full = lax.all_gather(stacked.reshape(kinds * rows, width), "narrow", axis=0, tiled=False)
    full = full.reshape(-1, kinds, rows, width)
    return [full[:, kind].reshape(-1, width) for kind in range(kinds)]


def narrow_total(term):
    return lax.psum_scatter(low(term), "narrow", scatter_dimension=0, tiled=True)


PIECE_FLIPS = (0, 2, 5, 7, 1, 3, 4, 6)


def place_body(spots, *refs, plan, source_count):
    sources, outs = refs[:source_count], refs[source_count:]
    step, part = pl.program_id(0), pl.program_id(1)

    def write(source):
        for out, kinds in zip(outs, plan):
            if len(kinds) == 1:
                out[...] = source[kinds[0]].astype(jnp.float32)
            elif len(kinds) == 2:
                for slot, kind in enumerate(kinds):
                    out[:, slot, :] = source[kind].astype(jnp.float32)
            else:
                for slot, kind in enumerate(kinds):
                    out[slot] = source[kind].astype(jnp.float32)

    for number, source in enumerate(sources):
        which, spot = number // 5, number % 5
        if spot < 3:
            hit = step == 4 * which + spot
        else:
            hit = (step == 4 * which + 3) & (part == spot - 3)

        @pl.when(hit)
        def _(source=source):
            write(source)


def core_pieces(chip):
    return chip + [flip(piece, CORE) for piece in chip]


def placed(sources, spot_zero, plan):
    kinds, rows, width = sources[0].shape
    half = rows // 2
    spots = spot_zero ^ jnp.asarray(PIECE_FLIPS, jnp.int32)

    def source_spec(number):
        which, spot = number // 5, number % 5
        if spot >= 3:
            return pl.BlockSpec((kinds, half, width), lambda step, part, spots: (0, 0, 0))
        mine = 4 * which + spot

        def index(step, part, spots):
            return (0, jnp.where(step == mine, part, jnp.where(step < mine, 0, 1)), 0)

        return pl.BlockSpec((kinds, half, width), index)

    out_specs, out_shapes = [], []
    for group in plan:
        count = len(group)
        if count == 1:
            block, shape = (half, width), (PLANE * rows, width)
            index = lambda step, part, spots: (2 * spots[step] + part, 0)
        elif count == 2:
            block, shape = (half, 2, width), (PLANE * rows, 2, width)
            index = lambda step, part, spots: (2 * spots[step] + part, 0, 0)
        else:
            block, shape = (count, half, width), (count, PLANE * rows, width)
            index = lambda step, part, spots: (0, 2 * spots[step] + part, 0)
        out_specs.append(pl.BlockSpec(block, index))
        out_shapes.append(jax.ShapeDtypeStruct(shape, jnp.float32))
    body = lambda *refs: place_body(*refs, plan=plan, source_count=len(sources))
    return pl.pallas_call(
        body,
        grid_spec=pltpu.PrefetchScalarGridSpec(
            num_scalar_prefetch=1,
            grid=(PLANE, 2),
            in_specs=[source_spec(number) for number in range(len(sources))],
            out_specs=out_specs,
        ),
        out_shape=out_shapes,
        compiler_params=pltpu.CompilerParams(
            dimension_semantics=("arbitrary", "arbitrary"), vmem_limit_bytes=56 * 1024 * 1024
        ),
        name="place",
    )(spots, *sources)


def laid_body(spots, source, *outs, plan):
    for out, kinds in zip(outs, plan):
        if len(kinds) == 1:
            out[...] = source[0, kinds[0]].astype(jnp.float32)
        else:
            for slot, kind in enumerate(kinds):
                value = source[0, kind].astype(jnp.float32)
                if len(kinds) == 2:
                    out[:, slot, :] = value
                else:
                    out[slot] = value


def laid(moved, plan):
    kinds, rows, width = moved.shape
    half = rows // 2
    full = lax.all_gather(moved.reshape(kinds * rows, width), "wide", axis=0, tiled=False)
    full = full.reshape(PLANE, kinds, rows, width)
    _, _, spots = spread_tables(lax.axis_size("wide"), lax.axis_size("narrow"))
    order = jnp.asarray(spots, jnp.int32)[lax.axis_index("narrow")]
    out_specs, out_shapes = [], []
    for group in plan:
        count = len(group)
        if count == 1:
            block, shape = (half, width), (PLANE * rows, width)
            index = lambda step, part, spots: (2 * step + part, 0)
        elif count == 2:
            block, shape = (half, 2, width), (PLANE * rows, 2, width)
            index = lambda step, part, spots: (2 * step + part, 0, 0)
        else:
            block, shape = (count, half, width), (count, PLANE * rows, width)
            index = lambda step, part, spots: (0, 2 * step + part, 0)
        out_specs.append(pl.BlockSpec(block, index))
        out_shapes.append(jax.ShapeDtypeStruct(shape, jnp.float32))
    source_spec = pl.BlockSpec(
        (1, kinds, half, width), lambda step, part, spots: (spots[step], 0, part, 0)
    )
    return pl.pallas_call(
        lambda *refs: laid_body(*refs, plan=plan),
        grid_spec=pltpu.PrefetchScalarGridSpec(
            num_scalar_prefetch=1, grid=(PLANE, 2), in_specs=[source_spec], out_specs=out_specs
        ),
        out_shape=out_shapes,
        compiler_params=pltpu.CompilerParams(
            dimension_semantics=("arbitrary", "arbitrary"), vmem_limit_bytes=32 * 1024 * 1024
        ),
        name="laid",
    )(order, full)


def wide_full(stacked):
    kinds, rows, width = stacked.shape
    full = lax.all_gather(stacked.reshape(kinds * rows, width), "wide", axis=0, tiled=False)
    full = full.reshape(-1, kinds, rows, width)
    return [full[:, kind].reshape(-1, width) for kind in range(kinds)]


def per_device(
    tokens,
    memory,
    item_len,
    item_kind,
    norm_gains,
    w_self_in,
    w_self_out,
    w_cross_q,
    w_cross_kv,
    w_cross_out,
    w_mlp_in,
    w_mlp_out,
    cotangent,
):
    tok_rows, width = tokens.shape
    mem_rows = memory.shape[0]
    item_count = item_len.shape[1]
    gain = norm_gains.astype(jnp.float32)
    tokens_here = spread(tokens)
    ws_q, ws_k, ws_v = narrow_full(after(w_self_in.swapaxes(0, 1), tokens_here))
    x = tokens_here.astype(jnp.float32)
    h1 = low(normed(x, gain[0]))
    rows_one = plane_gather(h1)
    ws_out, wc_q = narrow_full(after(jnp.stack([w_self_out, w_cross_q]), ws_q))
    wc_k, wc_v = narrow_full(after(w_cross_kv.swapaxes(0, 1), ws_out))
    (wc_out,) = narrow_full(after(w_cross_out[None], wc_k))
    wm_gate, wm_up = wide_full(after(w_mlp_in.swapaxes(0, 1), wc_out))
    memory_here = level_hop(after(plane_hop(memory), tokens_here))
    memory_all = plane_gather(after(memory_here, rows_one[0]))
    cotangent_here = level_hop(after(plane_hop(cotangent), memory_here))

    me, level = lax.axis_index("wide"), lax.axis_index("narrow")
    differ = (me >> 1) ^ level
    side, upper = differ >> 1, differ & 1
    quarter = 2 * upper + ((me & 1) ^ side)
    spot_zero = 4 * side + quarter
    info_own = spread(jnp.concatenate([item_len, item_kind], axis=1))
    info = jnp.stack([info_own[0], flip(info_own, YDIM)[0]], axis=0)
    order = jnp.asarray([0, 2, 1, 3], jnp.int32)
    quarters = jnp.stack([quarter ^ order, quarter ^ 1 ^ order], axis=0)
    positions = (
        quarters[:, :, None] * tok_rows + jnp.arange(tok_rows, dtype=jnp.int32)
    ).reshape(2, -1)
    segment, token_valid, weight = jax.vmap(token_info, in_axes=(0, 0, 0, None))(
        info[:, :item_count], info[:, item_count:], positions, item_count
    )
    local_weight = weight[0, :tok_rows]
    self_ok = (segment[:, :, None] == segment[:, None, :]) & (
        positions[:, None, :] <= positions[:, :, None]
    )
    patch_rows = mem_rows * (PLANE // 2) // item_count
    mem_item = (
        (quarters[:, :, None] * mem_rows + jnp.arange(mem_rows, dtype=jnp.int32)) // patch_rows
    ).reshape(2, -1)
    cross_ok = mem_item[:, None, :] == jnp.minimum(segment, item_count - 1)[:, :, None]
    valid_float = token_valid.astype(jnp.float32)

    own_width = ws_out.shape[0]
    heads_here = own_width // HEAD_DIM

    def project(rows, mat):
        parts = [low(matmul_nt(part, mat)).reshape(2, -1, heads_here, HEAD_DIM) for part in rows]
        return jnp.concatenate(parts, axis=1)

    def merge(mat):
        count = mat.shape[1] // 2
        return tuple(
            low(part.reshape(-1, own_width)) for part in (mat[:, :count], mat[:, count:])
        )

    def spread_out(terms):
        parts = [sum(matmul_nn(mat[part], weight) for mat, weight in terms) for part in (0, 1)]
        return plane_scatter(*parts)

    def weight_sum(mats, rows):
        return narrow_total(matmul_tn(mats[0], rows[0]) + matmul_tn(mats[1], rows[1]))

    sq, sk, sv = (project(rows_one, mat) for mat in (ws_q, ws_k, ws_v))
    self_result, self_lse = group_attend(sq, sk, sv, self_ok)
    self_heads = merge(self_result)
    self_heads, cotangent_here = lax.optimization_barrier((self_heads, cotangent_here))
    x1 = x + spread_out([(self_heads, ws_out)])
    h2 = low(normed(x1, gain[1]))
    rows_two = plane_gather(h2)
    ck, cv = (project(memory_all, mat) for mat in (wc_k, wc_v))
    cq = project(rows_two, wc_q)
    cross_result, cross_lse = group_attend(cq, ck, cv, cross_ok)
    cross_heads = merge(cross_result * valid_float[:, :, None, None])
    x2 = x1 + spread_out([(cross_heads, wc_out)])
    h3 = low(normed(x2, gain[2]))
    grad_y = cotangent_here.astype(jnp.float32) * local_weight[:, None]
    grad_mlp = row_gather(after(low(grad_y), wm_gate))
    rows_three = row_gather(after(h3, grad_mlp))
    (wm_out,) = wide_full(after(w_mlp_out[None], rows_three))
    gate = matmul_nt(rows_three, wm_gate)
    up = matmul_nt(rows_three, wm_up)
    hidden = low(jax.nn.gelu(gate, approximate=True) * up)
    grad_hidden = matmul_nt(grad_mlp, wm_out)
    _, gelu_pull = jax.vjp(
        lambda gate_part, up_part: jax.nn.gelu(gate_part, approximate=True) * up_part, gate, up
    )
    grad_gate, grad_up = gelu_pull(grad_hidden)
    grad_gate, grad_up = low(grad_gate), low(grad_up)
    grad_h3 = branch_sum(matmul_nn(grad_gate, wm_gate) + matmul_nn(grad_up, wm_up))
    mlp_terms = ((grad_gate, rows_three), (grad_up, rows_three), (hidden, grad_mlp))
    mlp_packed = jnp.stack(
        [
            low(matmul_tn(mat, rows)).reshape(PLANE, -1, width)
            for mat, rows in mlp_terms
        ],
        axis=1,
    ).reshape(-1, width)
    mlp_packed, grad_h3 = lax.optimization_barrier((mlp_packed, grad_h3))
    mlp_sums = lax.psum_scatter(mlp_packed, "wide", scatter_dimension=0, tiled=True)
    mlp_sums = mlp_sums.reshape(3, -1, width)
    _, norm_pull3 = jax.vjp(normed, x2, gain[2])
    part_x2, grad_gain3 = norm_pull3(grad_h3)
    grad_x2 = grad_y + part_x2
    grad_cross = plane_gather(low(grad_x2))
    grad_cross_heads = project(grad_cross, wc_out)
    grad_cross_heads = jnp.where(
        token_valid[:, :, None, None], grad_cross_heads, jnp.zeros_like(grad_cross_heads)
    )
    grad_cq, grad_ck, grad_cv = (
        merge(mat)
        for mat in group_attend_back(cq, ck, cv, cross_ok, cross_lse, grad_cross_heads)
    )
    grad_h2 = spread_out([(grad_cq, wc_q)])
    _, norm_pull2 = jax.vjp(normed, x1, gain[1])
    part_x1, grad_gain2 = norm_pull2(grad_h2)
    grad_x1 = grad_x2 + part_x1
    grad_self = plane_gather(low(grad_x1))
    mlp_here = spread(mlp_sums)
    grad_self, mlp_here = lax.optimization_barrier((grad_self, mlp_here))
    mlp_totals = laid(mlp_here, ((0, 1), (2,)))
    memory_sums = low(
        spread_out([(after(grad_ck, grad_self[0]), wc_k), (after(grad_cv, grad_self[0]), wc_v)])
    )
    mid_here = spread(
        jnp.stack(
            [
                weight_sum(cross_heads, grad_cross),
                weight_sum(grad_cv, memory_all),
                weight_sum(grad_ck, memory_all),
                weight_sum(grad_cq, rows_two),
            ]
        )
    )
    self_out_sum = weight_sum(self_heads, grad_self)
    grad_self_heads = project(grad_self, ws_out)
    gsq, gsk, gsv = (
        merge(mat) for mat in group_attend_back(sq, sk, sv, self_ok, self_lse, grad_self_heads)
    )
    gsq, gsk, gsv, mid_here, memory_sums = lax.optimization_barrier(
        (gsq, gsk, gsv, mid_here, memory_sums)
    )
    grad_memory = unspread(memory_sums)
    in_sums = [weight_sum(term, rows_one) for term in (gsv, gsk, gsq)]
    branch_three = branch_sum(after(matmul_nn(hidden, wm_out), gsq))
    output = unspread(low(x2 + branch_three))
    mid_totals = placed(core_pieces(chip_pieces(mid_here)), spot_zero, ((3,), (2, 1), (0,)))
    last = jnp.stack([in_sums[2], in_sums[1], in_sums[0], self_out_sum])
    in_totals, out_totals = laid(spread(last), ((0, 1, 2), (3,)))
    grad_h1 = spread_out([(gsq, ws_q), (gsk, ws_k), (gsv, ws_v)])
    _, norm_pull1 = jax.vjp(normed, x, gain[0])
    part_x, grad_gain1 = norm_pull1(grad_h1)
    grad_tokens = unspread(low(grad_x1 + part_x))
    gain_terms = jnp.stack([grad_gain1, grad_gain2, grad_gain3])
    levels = jnp.sum(lax.all_gather(gain_terms, "narrow", axis=0, tiled=False), axis=0)
    own_gains = width // lax.axis_size("narrow")
    gain_own = lax.dynamic_slice_in_dim(levels, level * own_gains, own_gains, 1)
    gain_total = jnp.sum(lax.all_gather(gain_own, "wide", axis=0, tiled=False), axis=0)
    return (
        output,
        grad_tokens,
        grad_memory,
        gain_total,
        in_totals.swapaxes(0, 1),
        out_totals,
        *mid_totals,
        *mlp_totals,
    )


def solution(mesh):
    in_plane = (mesh.shape["wide"], mesh.shape["narrow"]) == (8, 4)
    return jax.shard_map(
        per_device if in_plane else per_device_general,
        mesh=mesh,
        in_specs=(
            P(("wide", "narrow"), None),
            P(("wide", "narrow"), None),
            P("wide", None),
            P("wide", None),
            P(),
            P(("wide", "narrow"), None, None),
            P(("wide", "narrow"), None),
            P(("wide", "narrow"), None),
            P(("wide", "narrow"), None, None),
            P(("wide", "narrow"), None),
            P(("wide", "narrow"), None, None),
            P(("wide", "narrow"), None),
            P(("wide", "narrow"), None),
        ),
        out_specs=(
            P(("wide", "narrow"), None),
            P(("wide", "narrow"), None),
            P(("wide", "narrow"), None),
            P(None, "narrow"),
            P("narrow", None, None),
            P("narrow", None),
            P("narrow", None),
            P("narrow", None, None),
            P("narrow", None),
            P("narrow", None, None),
            P("narrow", None),
        ),
        check_vma=False,
    )
```

```python
import jax
import jax.numpy as jnp
from jax import lax
from jax.experimental import pallas as pl
from jax.experimental.pallas import tpu as pltpu
from jax.sharding import PartitionSpec as P

HEAD_DIM = 128


EPSILON = 1e-06
ROBOT_WEIGHT = 2.0
NEGATIVE = -1e30


def normed(values, gain_row):
    factor = lax.rsqrt(jnp.mean(values * values, axis=-1, keepdims=True) + EPSILON)
    return values * factor * gain_row


def token_info(lengths, item_kinds, positions, item_count):
    item_ends = jnp.cumsum(lengths)
    segment = jnp.sum((positions[:, None] >= item_ends[None, :]).astype(jnp.int32), axis=1)
    token_valid = segment < item_count
    item_hit = segment[:, None] == jnp.arange(item_count, dtype=jnp.int32)[None, :]
    robot_flag = jnp.sum(jnp.where(item_hit, item_kinds[None, :], 0), axis=1)
    weight = jnp.where(token_valid, jnp.where(robot_flag == 1, ROBOT_WEIGHT, 1.0), 0.0).astype(
        jnp.float32
    )
    return (segment, token_valid, weight)


def attend_forward(queries, keys_all, values_all, allowed):
    scores = jnp.einsum(
        "qhd,khd->hqk", queries, keys_all, preferred_element_type=jnp.float32
    ) * HEAD_DIM ** (-0.5)
    scores = jnp.where(allowed[None], scores, NEGATIVE)
    row_top = jnp.max(scores, axis=2, keepdims=True)
    exp_scores = jnp.exp(scores - row_top)
    denom_sum = jnp.sum(exp_scores, axis=2, keepdims=True)
    soft_probs = (exp_scores / denom_sum).astype(jnp.bfloat16)
    result = jnp.einsum("hqk,khd->qhd", soft_probs, values_all, preferred_element_type=jnp.float32)
    return (result, row_top + jnp.log(denom_sum))


def attend_backward(queries, keys_all, values_all, allowed, log_sums, grad_out):
    score_scale = HEAD_DIM ** (-0.5)
    scores = (
        jnp.einsum("qhd,khd->hqk", queries, keys_all, preferred_element_type=jnp.float32)
        * score_scale
    )
    scores = jnp.where(allowed[None], scores, NEGATIVE)
    soft_probs = jnp.exp(scores - log_sums)
    grad_probs = jnp.einsum(
        "qhd,khd->hqk", grad_out, values_all, preferred_element_type=jnp.float32
    )
    row_inner = jnp.sum(soft_probs * grad_probs, axis=2, keepdims=True)
    grad_scores = (soft_probs * (grad_probs - row_inner)).astype(jnp.bfloat16)
    grad_query = (
        jnp.einsum("hqk,khd->qhd", grad_scores, keys_all, preferred_element_type=jnp.float32)
        * score_scale
    )
    grad_keys = (
        jnp.einsum("hqk,qhd->khd", grad_scores, queries, preferred_element_type=jnp.float32)
        * score_scale
    )
    grad_values = jnp.einsum(
        "hqk,qhd->khd",
        soft_probs.astype(jnp.bfloat16),
        grad_out,
        preferred_element_type=jnp.float32,
    )
    return (grad_query, grad_keys, grad_values)


def spread_tables(wide, narrow):
    total = wide * narrow
    ratio = wide // narrow
    if (wide, narrow) == (8, 4):
        first, second, spots = [], [], [[0] * wide for _ in range(narrow)]
        for block in range(total):
            w, n = divmod(block, narrow)
            q, c = divmod(w, ratio)
            z1, z0 = divmod(n, 2)
            spot = 2 * (q ^ (2 * c + z1)) + (z0 ^ c)
            first.append((block, spot * narrow + n))
            second.append((spot * narrow + n, spot * narrow + q))
            spots[q][block - q * wide] = spot
        return (first, second, spots)
    direct = []
    for block in range(total):
        n, w = divmod(block, wide)
        direct.append((block, w * narrow + n))
    return (direct, None, None)


def spread(piece):
    first, second, _ = spread_tables(lax.axis_size("wide"), lax.axis_size("narrow"))
    piece = hop(piece, first)
    if second is not None:
        piece = hop(piece, second)
    return piece


def hop(piece, pairs):
    narrow = lax.axis_size("narrow")
    stay = [0] * (lax.axis_size("wide") * narrow)
    for source, target in pairs:
        stay[source] = int(source == target)
    here = lax.axis_index("wide") * narrow + lax.axis_index("narrow")
    moved = lax.ppermute(
        piece, ("wide", "narrow"), [pair for pair in pairs if pair[0] != pair[1]]
    )
    return jnp.where(jnp.asarray(stay, jnp.int32)[here] == 1, piece, moved)


def plane_hop(piece):
    return hop(piece, spread_tables(lax.axis_size("wide"), lax.axis_size("narrow"))[0])


def level_hop(piece):
    return hop(piece, spread_tables(lax.axis_size("wide"), lax.axis_size("narrow"))[1])


def wide_gather(pieces):
    rows, width = pieces[0].shape
    moved = spread(jnp.concatenate(pieces, axis=0))
    full = lax.all_gather(moved, "wide", axis=0, tiled=False)
    full = full.reshape(-1, len(pieces), rows, width)
    return tuple(full[:, kind].reshape(-1, width) for kind in range(len(pieces)))


def wide_total(terms):
    wide_count = lax.axis_size("wide")
    width = terms[0].shape[1]
    parts = [term.astype(jnp.bfloat16).reshape(wide_count, -1, width) for term in terms]
    packed = jnp.concatenate(parts, axis=1)
    rows = packed.shape[1]
    shard = lax.psum_scatter(
        packed.reshape(wide_count * rows, width), "wide", scatter_dimension=0, tiled=True
    )
    full = lax.all_gather(shard, "wide", axis=0, tiled=False)
    _, _, spots = spread_tables(wide_count, lax.axis_size("narrow"))
    if spots is not None:
        order = jnp.asarray(spots, jnp.int32)[lax.axis_index("narrow")]
        full = jnp.concatenate(
            [lax.dynamic_slice_in_dim(full, order[j], 1, 0) for j in range(wide_count)], axis=0
        )
    full = full.reshape(wide_count, len(terms), -1, width)
    return [
        full[:, kind].reshape(-1, width).astype(jnp.float32) for kind in range(len(terms))
    ]


def row_gather(local_rows):
    return lax.all_gather(local_rows, "narrow", axis=0, tiled=True)


def branch_sum(partial_rows):
    return lax.psum_scatter(
        partial_rows.astype(jnp.bfloat16), "narrow", scatter_dimension=0, tiled=True
    ).astype(jnp.float32)


def matmul_nt(a, b):
    return lax.dot_general(a, b, (((1,), (1,)), ((), ())), preferred_element_type=jnp.float32)


def matmul_nn(a, b):
    return lax.dot_general(a, b, (((1,), (0,)), ((), ())), preferred_element_type=jnp.float32)


def matmul_tn(a, b):
    return lax.dot_general(a, b, (((0,), (0,)), ((), ())), preferred_element_type=jnp.float32)


def tensor_pass(tokens, memory, gain_float, weights, cotangent, masks):
    segment, token_valid, valid_float, local_weight, self_ok, cross_ok = masks
    tok_rows = tokens.shape[0]
    group_rows = tok_rows * lax.axis_size("narrow")
    mem_group = memory.shape[0] * lax.axis_size("narrow")
    w_self_in, w_self_out, w_cross_q, w_cross_kv, w_cross_out, w_mlp_in, w_mlp_out = weights
    tok_float = tokens.astype(jnp.float32)
    h1 = normed(tok_float, gain_float[0]).astype(jnp.bfloat16)
    rows_one = row_gather(h1)
    ws_q, ws_k, ws_v = wide_gather([w_self_in[:, 0], w_self_in[:, 1], w_self_in[:, 2]])
    ws_out, wc_q, wc_k, wc_v, wc_out = wide_gather(
        [w_self_out, w_cross_q, w_cross_kv[:, 0], w_cross_kv[:, 1], w_cross_out]
    )
    wm_gate, wm_up, wm_out = wide_gather([w_mlp_in[:, 0], w_mlp_in[:, 1], w_mlp_out])
    memory_all = row_gather(memory)
    grad_y = cotangent.astype(jnp.float32) * local_weight[:, None]
    grad_mlp = row_gather(grad_y.astype(jnp.bfloat16))
    own_width = ws_out.shape[0]
    heads_here = own_width // HEAD_DIM

    def split(mat):
        return mat.reshape(mat.shape[0], heads_here, HEAD_DIM)

    def project(rows, mat):
        return matmul_nt(rows, mat).astype(jnp.bfloat16)

    sq, sk, sv = (split(project(rows_one, mat)) for mat in (ws_q, ws_k, ws_v))
    self_result, self_lse = attend_forward(sq, sk, sv, self_ok)
    self_heads = self_result.reshape(group_rows, own_width).astype(jnp.bfloat16)
    x1 = tok_float + branch_sum(matmul_nn(self_heads, ws_out))
    h2 = normed(x1, gain_float[1]).astype(jnp.bfloat16)
    rows_two = row_gather(h2)
    ck, cv = (split(project(memory_all, mat)) for mat in (wc_k, wc_v))
    cq = split(project(rows_two, wc_q))
    cross_result, cross_lse = attend_forward(cq, ck, cv, cross_ok)
    cross_heads = (
        (cross_result * valid_float[:, None, None])
        .reshape(group_rows, own_width)
        .astype(jnp.bfloat16)
    )
    x2 = x1 + branch_sum(matmul_nn(cross_heads, wc_out))
    h3 = normed(x2, gain_float[2]).astype(jnp.bfloat16)
    rows_three = row_gather(h3)
    gate = matmul_nt(rows_three, wm_gate)
    up = matmul_nt(rows_three, wm_up)
    hidden = (jax.nn.gelu(gate, approximate=True) * up).astype(jnp.bfloat16)
    output = (x2 + branch_sum(matmul_nn(hidden, wm_out))).astype(jnp.bfloat16)
    grad_hidden = matmul_nt(grad_mlp, wm_out)
    _, gelu_pull = jax.vjp(
        lambda gate_part, up_part: jax.nn.gelu(gate_part, approximate=True) * up_part, gate, up
    )
    grad_gate, grad_up = gelu_pull(grad_hidden)
    grad_gate = grad_gate.astype(jnp.bfloat16)
    grad_up = grad_up.astype(jnp.bfloat16)
    grad_h3 = branch_sum(matmul_nn(grad_gate, wm_gate) + matmul_nn(grad_up, wm_up))
    _, norm_pull3 = jax.vjp(normed, x2, gain_float[2])
    part_x2, grad_gain3 = norm_pull3(grad_h3)
    grad_x2 = grad_y + part_x2
    mlp_totals = wide_total(
        [
            matmul_tn(grad_gate, rows_three),
            matmul_tn(grad_up, rows_three),
            matmul_tn(hidden, grad_mlp),
        ]
    )
    grad_cross = row_gather(grad_x2.astype(jnp.bfloat16))
    grad_cross_heads = split(project(grad_cross, wc_out))
    grad_cross_heads = jnp.where(
        token_valid[:, None, None], grad_cross_heads, jnp.zeros_like(grad_cross_heads)
    )
    gq_heads, gk_heads, gv_heads = attend_backward(
        cq, ck, cv, cross_ok, cross_lse, grad_cross_heads
    )
    grad_cq = gq_heads.reshape(group_rows, own_width).astype(jnp.bfloat16)
    grad_ck = gk_heads.reshape(mem_group, own_width).astype(jnp.bfloat16)
    grad_cv = gv_heads.reshape(mem_group, own_width).astype(jnp.bfloat16)
    grad_h2 = branch_sum(matmul_nn(grad_cq, wc_q))
    _, norm_pull2 = jax.vjp(normed, x1, gain_float[1])
    part_x1, grad_gain2 = norm_pull2(grad_h2)
    grad_x1 = grad_x2 + part_x1
    grad_self = row_gather(grad_x1.astype(jnp.bfloat16))
    grad_memory = branch_sum(matmul_nn(grad_ck, wc_k) + matmul_nn(grad_cv, wc_v)).astype(
        jnp.bfloat16
    )
    mid_totals = wide_total(
        [
            matmul_tn(self_heads, grad_self),
            matmul_tn(grad_cq, rows_two),
            matmul_tn(grad_ck, memory_all),
            matmul_tn(grad_cv, memory_all),
            matmul_tn(cross_heads, grad_cross),
        ]
    )
    grad_self_heads = split(project(grad_self, ws_out))
    gsq, gsk, gsv = (
        mat.reshape(group_rows, own_width).astype(jnp.bfloat16)
        for mat in attend_backward(sq, sk, sv, self_ok, self_lse, grad_self_heads)
    )
    in_totals = wide_total(
        [matmul_tn(gsq, rows_one), matmul_tn(gsk, rows_one), matmul_tn(gsv, rows_one)]
    )
    grad_h1 = branch_sum(matmul_nn(gsq, ws_q) + matmul_nn(gsk, ws_k) + matmul_nn(gsv, ws_v))
    _, norm_pull1 = jax.vjp(normed, tok_float, gain_float[0])
    part_x, grad_gain1 = norm_pull1(grad_h1)
    grad_tokens = (grad_x1 + part_x).astype(jnp.bfloat16)
    gain_terms = jnp.stack([grad_gain1, grad_gain2, grad_gain3])
    return (output, grad_tokens, grad_memory, gain_terms, in_totals, mid_totals, mlp_totals)


def per_device_general(
    tokens,
    memory,
    item_len,
    item_kind,
    norm_gains,
    w_self_in,
    w_self_out,
    w_cross_q,
    w_cross_kv,
    w_cross_out,
    w_mlp_in,
    w_mlp_out,
    cotangent,
):
    tok_rows = tokens.shape[0]
    narrow_size = lax.axis_size("narrow")
    group_rows = tok_rows * narrow_size
    mem_group = memory.shape[0] * narrow_size
    lengths = item_len[0]
    item_count = lengths.shape[0]
    patch_rows = mem_group // item_count
    positions = jnp.arange(group_rows, dtype=jnp.int32)
    segment, token_valid, weight = token_info(lengths, item_kind[0], positions, item_count)
    local_weight = lax.dynamic_slice_in_dim(weight, lax.axis_index("narrow") * tok_rows, tok_rows)
    self_ok = (segment[:, None] == segment[None, :]) & (positions[None, :] <= positions[:, None])
    mem_item = jnp.arange(mem_group, dtype=jnp.int32) // patch_rows
    cross_ok = mem_item[None, :] == jnp.minimum(segment, item_count - 1)[:, None]
    valid_float = token_valid.astype(jnp.float32)
    masks = (segment, token_valid, valid_float, local_weight, self_ok, cross_ok)
    gain_float = norm_gains.astype(jnp.float32)
    weights = (w_self_in, w_self_out, w_cross_q, w_cross_kv, w_cross_out, w_mlp_in, w_mlp_out)
    output, grad_tokens, grad_memory, gain_terms, in_totals, mid_totals, mlp_totals = tensor_pass(
        tokens, memory, gain_float, weights, cotangent, masks
    )
    gain_shard = lax.psum_scatter(gain_terms, "narrow", scatter_dimension=1, tiled=True)
    gain_total = lax.psum(gain_shard, "wide")
    return (
        output,
        grad_tokens,
        grad_memory,
        gain_total,
        jnp.stack(in_totals, axis=1),
        mid_totals[0],
        mid_totals[1],
        jnp.stack([mid_totals[2], mid_totals[3]], axis=1),
        mid_totals[4],
        jnp.stack([mlp_totals[0], mlp_totals[1]], axis=1),
        mlp_totals[2],
    )


CORE, XDIM, YDIM = 1, 2, 4
PLANE = 8


def flip(value, bit):
    return lax.ppermute(value, "wide", [(i, i ^ bit) for i in range(PLANE)])


def unspread(piece):
    first, second, _ = spread_tables(lax.axis_size("wide"), lax.axis_size("narrow"))
    piece = hop(piece, [(b, a) for a, b in second])
    return hop(piece, [(b, a) for a, b in first])


def after(value, *others):
    return lax.optimization_barrier((value,) + others)[0]


def low(value):
    return jax.tree.map(lambda part: part.astype(jnp.bfloat16), value)


def plus(kept, moved):
    return kept.astype(jnp.float32) + moved.astype(jnp.float32)


def side_pieces(shard):
    return [shard, flip(shard, XDIM), flip(shard, YDIM)]


def corner_pieces(sides):
    half = sides[0].shape[-2] // 2
    return sides + [flip(sides[1][..., :half, :], YDIM), flip(sides[2][..., half:, :], XDIM)]


def chip_pieces(shard):
    return corner_pieces(side_pieces(shard))


def plane_gather(shard):
    own = jnp.concatenate(chip_pieces(shard), axis=0)
    return (own, flip(own, CORE))


def plane_scatter(kept, sent):
    return scatter_end(*scatter_start(kept, sent))


def scatter_start(kept, sent):
    chip = low(plus(kept, flip(low(sent), CORE)))
    lead, rows, width = chip.shape[:-2], chip.shape[-2] // 4, chip.shape[-1]
    half = rows // 2
    view = jnp.moveaxis(chip.reshape(lead + (2, 2, rows, width)), (-4, -3), (0, 1))
    part_a, part_b = view[..., :half, :], view[..., half:, :]
    part_a = plus(part_a[:, 0], flip(part_a[:, 1], XDIM))
    part_b = plus(part_b[0], flip(part_b[1], YDIM))
    return (part_a, part_b)


def scatter_end(part_a, part_b):
    done_a = plus(part_a[0], flip(low(part_a[1]), YDIM))
    done_b = plus(part_b[0], flip(low(part_b[1]), XDIM))
    return jnp.concatenate([done_a, done_b], axis=-2)


def group_attend(queries, keys_all, values_all, allowed):
    scores = jnp.einsum(
        "gqhd,gkhd->ghqk", queries, keys_all, preferred_element_type=jnp.float32
    ) * HEAD_DIM ** (-0.5)
    scores = jnp.where(allowed[:, None], scores, NEGATIVE)
    row_top = jnp.max(scores, axis=3, keepdims=True)
    exp_scores = jnp.exp(scores - row_top)
    denom_sum = jnp.sum(exp_scores, axis=3, keepdims=True)
    soft_probs = low(exp_scores / denom_sum)
    result = jnp.einsum(
        "ghqk,gkhd->gqhd", soft_probs, values_all, preferred_element_type=jnp.float32
    )
    return (result, row_top + jnp.log(denom_sum))


def group_attend_back(queries, keys_all, values_all, allowed, log_sums, grad_out):
    score_scale = HEAD_DIM ** (-0.5)
    scores = (
        jnp.einsum("gqhd,gkhd->ghqk", queries, keys_all, preferred_element_type=jnp.float32)
        * score_scale
    )
    scores = jnp.where(allowed[:, None], scores, NEGATIVE)
    soft_probs = jnp.exp(scores - log_sums)
    grad_probs = jnp.einsum(
        "gqhd,gkhd->ghqk", grad_out, values_all, preferred_element_type=jnp.float32
    )
    row_inner = jnp.sum(soft_probs * grad_probs, axis=3, keepdims=True)
    grad_scores = low(soft_probs * (grad_probs - row_inner))
    grad_query = (
        jnp.einsum("ghqk,gkhd->gqhd", grad_scores, keys_all, preferred_element_type=jnp.float32)
        * score_scale
    )
    grad_keys = (
        jnp.einsum("ghqk,gqhd->gkhd", grad_scores, queries, preferred_element_type=jnp.float32)
        * score_scale
    )
    grad_values = jnp.einsum(
        "ghqk,gqhd->gkhd", low(soft_probs), grad_out, preferred_element_type=jnp.float32
    )
    return (grad_query, grad_keys, grad_values)


def narrow_full(stacked):
    kinds, rows, width = stacked.shape
    full = lax.all_gather(stacked.reshape(kinds * rows, width), "narrow", axis=0, tiled=False)
    full = full.reshape(-1, kinds, rows, width)
    return [full[:, kind].reshape(-1, width) for kind in range(kinds)]


def narrow_total(term):
    return lax.psum_scatter(low(term), "narrow", scatter_dimension=0, tiled=True)


PIECE_FLIPS = (0, 2, 5, 7, 1, 3, 4, 6)
WIDE_FLIPS = (0, 2, 4, 6, 1, 3, 5, 7)


def place_body(spots, *refs, plan, source_count):
    sources, outs = refs[:source_count], refs[source_count:]
    step, part = pl.program_id(0), pl.program_id(1)

    def write(source):
        for out, kinds in zip(outs, plan):
            if len(kinds) == 1:
                out[...] = source[kinds[0]].astype(out.dtype)
            elif len(kinds) == 2:
                for slot, kind in enumerate(kinds):
                    out[:, slot, :] = source[kind].astype(out.dtype)
            else:
                for slot, kind in enumerate(kinds):
                    out[slot] = source[kind].astype(out.dtype)

    for number, source in enumerate(sources):
        which, spot = number // 5, number % 5
        if spot < 3:
            hit = step == 4 * which + spot
        else:
            hit = (step == 4 * which + 3) & (part == spot - 3)

        @pl.when(hit)
        def _(source=source):
            write(source)


def core_pieces(chip):
    return chip + [flip(piece, CORE) for piece in chip]


def placed(sources, spot_zero, plan, flips=PIECE_FLIPS, kind=jnp.float32):
    kinds, rows, width = sources[0].shape
    half = rows // 2
    spots = spot_zero ^ jnp.asarray(flips, jnp.int32)

    def source_spec(number):
        which, spot = number // 5, number % 5
        if spot >= 3:
            return pl.BlockSpec((kinds, half, width), lambda step, part, spots: (0, 0, 0))
        mine = 4 * which + spot

        def index(step, part, spots):
            return (0, jnp.where(step == mine, part, jnp.where(step < mine, 0, 1)), 0)

        return pl.BlockSpec((kinds, half, width), index)

    out_specs, out_shapes = [], []
    for group in plan:
        count = len(group)
        if count == 1:
            block, shape = (half, width), (PLANE * rows, width)
            index = lambda step, part, spots: (2 * spots[step] + part, 0)
        elif count == 2:
            block, shape = (half, 2, width), (PLANE * rows, 2, width)
            index = lambda step, part, spots: (2 * spots[step] + part, 0, 0)
        else:
            block, shape = (count, half, width), (count, PLANE * rows, width)
            index = lambda step, part, spots: (0, 2 * spots[step] + part, 0)
        out_specs.append(pl.BlockSpec(block, index))
        out_shapes.append(jax.ShapeDtypeStruct(shape, kind))
    body = lambda *refs: place_body(*refs, plan=plan, source_count=len(sources))
    return pl.pallas_call(
        body,
        grid_spec=pltpu.PrefetchScalarGridSpec(
            num_scalar_prefetch=1,
            grid=(PLANE, 2),
            in_specs=[source_spec(number) for number in range(len(sources))],
            out_specs=out_specs,
        ),
        out_shape=out_shapes,
        compiler_params=pltpu.CompilerParams(
            dimension_semantics=("arbitrary", "arbitrary"), vmem_limit_bytes=56 * 1024 * 1024
        ),
        name="place",
    )(spots, *sources)


def per_device(
    tokens,
    memory,
    item_len,
    item_kind,
    norm_gains,
    w_self_in,
    w_self_out,
    w_cross_q,
    w_cross_kv,
    w_cross_out,
    w_mlp_in,
    w_mlp_out,
    cotangent,
):
    tok_rows, width = tokens.shape
    mem_rows = memory.shape[0]
    item_count = item_len.shape[1]
    gain = norm_gains.astype(jnp.float32)
    tokens_hop = plane_hop(tokens)
    mlp_shard = jnp.concatenate([w_mlp_in.swapaxes(0, 1), w_mlp_out[None]], axis=0)
    mlp_sides = side_pieces(after(mlp_shard, tokens_hop))
    tokens_here = level_hop(tokens_hop)
    ws_q, ws_k, ws_v = narrow_full(after(w_self_in.swapaxes(0, 1), tokens_here))
    x = tokens_here.astype(jnp.float32)
    h1 = low(normed(x, gain[0]))
    rows_one = plane_gather(h1)
    ws_out, wc_q = narrow_full(after(jnp.stack([w_self_out, w_cross_q]), ws_q))
    wc_k, wc_v = narrow_full(after(w_cross_kv.swapaxes(0, 1), ws_out))
    (wc_out,) = narrow_full(after(w_cross_out[None], wc_k))
    mlp_chip = corner_pieces(
        [mlp_sides[0], *lax.optimization_barrier((*mlp_sides[1:], rows_one[1]))[:2]]
    )
    memory_here = level_hop(after(plane_hop(memory), tokens_here))
    cotangent_here = level_hop(after(plane_hop(cotangent), memory_here))

    me, level = lax.axis_index("wide"), lax.axis_index("narrow")
    differ = (me >> 1) ^ level
    side, upper = differ >> 1, differ & 1
    quarter = 2 * upper + ((me & 1) ^ side)
    spot_zero = 4 * side + quarter
    info_own = spread(jnp.concatenate([item_len, item_kind], axis=1))
    info = jnp.stack([info_own[0], flip(info_own, YDIM)[0]], axis=0)
    order = jnp.asarray([0, 2, 1, 3], jnp.int32)
    quarters = jnp.stack([quarter ^ order, quarter ^ 1 ^ order], axis=0)
    positions = (
        quarters[:, :, None] * tok_rows + jnp.arange(tok_rows, dtype=jnp.int32)
    ).reshape(2, -1)
    segment, token_valid, weight = jax.vmap(token_info, in_axes=(0, 0, 0, None))(
        info[:, :item_count], info[:, item_count:], positions, item_count
    )
    local_weight = weight[0, :tok_rows]
    self_ok = (segment[:, :, None] == segment[:, None, :]) & (
        positions[:, None, :] <= positions[:, :, None]
    )
    patch_rows = mem_rows * (PLANE // 2) // item_count
    mem_item = (
        (quarters[:, :, None] * mem_rows + jnp.arange(mem_rows, dtype=jnp.int32)) // patch_rows
    ).reshape(2, -1)
    cross_ok = mem_item[:, None, :] == jnp.minimum(segment, item_count - 1)[:, :, None]
    valid_float = token_valid.astype(jnp.float32)

    own_width = ws_out.shape[0]
    heads_here = own_width // HEAD_DIM

    def project(rows, mat):
        parts = [low(matmul_nt(part, mat)).reshape(2, -1, heads_here, HEAD_DIM) for part in rows]
        return jnp.concatenate(parts, axis=1)

    def merge(mat):
        count = mat.shape[1] // 2
        return tuple(
            low(part.reshape(-1, own_width)) for part in (mat[:, :count], mat[:, count:])
        )

    def spread_out(terms):
        parts = [sum(matmul_nn(mat[part], weight) for mat, weight in terms) for part in (0, 1)]
        return plane_scatter(*parts)

    def weight_sum(mats, rows):
        return narrow_total(matmul_tn(mats[0], rows[0]) + matmul_tn(mats[1], rows[1]))

    sq, sk, sv = (project(rows_one, mat) for mat in (ws_q, ws_k, ws_v))
    self_result, self_lse = group_attend(sq, sk, sv, self_ok)
    self_heads = merge(self_result)
    self_heads, mlp_chip = lax.optimization_barrier((self_heads, mlp_chip))
    x1 = x + spread_out([(self_heads, ws_out)])
    h2 = low(normed(x1, gain[1]))
    h2, cotangent_here, memory_here = lax.optimization_barrier((h2, cotangent_here, memory_here))
    memory_all = plane_gather(memory_here)
    rows_two = plane_gather(h2)
    ck, cv = (project(memory_all, mat) for mat in (wc_k, wc_v))
    cq = project(rows_two, wc_q)
    cross_result, cross_lse = group_attend(cq, ck, cv, cross_ok)
    cross_heads = merge(cross_result * valid_float[:, :, None, None])
    grad_y = cotangent_here.astype(jnp.float32) * local_weight[:, None]
    grad_mlp = row_gather(after(low(grad_y), wc_out))
    cross_heads, grad_mlp = lax.optimization_barrier((cross_heads, grad_mlp))
    x2 = x1 + spread_out([(cross_heads, wc_out)])
    h3 = low(normed(x2, gain[2]))
    rows_three = row_gather(h3)
    wm_gate, wm_up, wm_out = placed(
        core_pieces(mlp_chip), me, ((0,), (1,), (2,)), WIDE_FLIPS, jnp.bfloat16
    )
    gate = matmul_nt(rows_three, wm_gate)
    up = matmul_nt(rows_three, wm_up)
    hidden = low(jax.nn.gelu(gate, approximate=True) * up)
    grad_hidden = matmul_nt(grad_mlp, wm_out)
    _, gelu_pull = jax.vjp(
        lambda gate_part, up_part: jax.nn.gelu(gate_part, approximate=True) * up_part, gate, up
    )
    grad_gate, grad_up = gelu_pull(grad_hidden)
    grad_gate, grad_up = low(grad_gate), low(grad_up)
    grad_h3 = branch_sum(matmul_nn(grad_gate, wm_gate) + matmul_nn(grad_up, wm_up))
    mlp_terms = ((grad_gate, rows_three), (grad_up, rows_three), (hidden, grad_mlp))
    mlp_packed = jnp.stack(
        [
            low(matmul_tn(mat, rows)).reshape(PLANE, -1, width)
            for mat, rows in mlp_terms
        ],
        axis=1,
    ).reshape(-1, width)
    mlp_packed, grad_h3 = lax.optimization_barrier((mlp_packed, grad_h3))
    mlp_sums = lax.psum_scatter(mlp_packed, "wide", scatter_dimension=0, tiled=True)
    mlp_sums = mlp_sums.reshape(3, -1, width)
    _, norm_pull3 = jax.vjp(normed, x2, gain[2])
    part_x2, grad_gain3 = norm_pull3(grad_h3)
    grad_x2 = grad_y + part_x2
    grad_cross = plane_gather(low(grad_x2))
    grad_cross_heads = project(grad_cross, wc_out)
    grad_cross_heads = jnp.where(
        token_valid[:, :, None, None], grad_cross_heads, jnp.zeros_like(grad_cross_heads)
    )
    grad_cq, grad_ck, grad_cv = (
        merge(mat)
        for mat in group_attend_back(cq, ck, cv, cross_ok, cross_lse, grad_cross_heads)
    )
    grad_h2 = spread_out([(grad_cq, wc_q)])
    _, norm_pull2 = jax.vjp(normed, x1, gain[1])
    part_x1, grad_gain2 = norm_pull2(grad_h2)
    grad_x1 = grad_x2 + part_x1
    grad_x1, mlp_sums = lax.optimization_barrier((grad_x1, mlp_sums))
    grad_self = plane_gather(low(grad_x1))
    memory_sides = scatter_start(
        *(
            matmul_nn(grad_ck[part], wc_k) + matmul_nn(grad_cv[part], wc_v)
            for part in (0, 1)
        )
    )
    mlp_here = spread(mlp_sums)
    mid_sums = jnp.stack(
        [
            weight_sum(cross_heads, grad_cross),
            weight_sum(grad_cv, memory_all),
            weight_sum(grad_ck, memory_all),
            weight_sum(grad_cq, rows_two),
        ]
    )
    self_out_sum = weight_sum(self_heads, grad_self)
    grad_self_heads = project(grad_self, ws_out)
    grad_self_heads, memory_sides = lax.optimization_barrier((grad_self_heads, memory_sides))
    memory_sums = low(scatter_end(*memory_sides))
    gsq, gsk, gsv = (
        merge(mat) for mat in group_attend_back(sq, sk, sv, self_ok, self_lse, grad_self_heads)
    )
    gsq, gsk, gsv, mlp_here, memory_sums = lax.optimization_barrier(
        (gsq, gsk, gsv, mlp_here, memory_sums)
    )
    grad_memory = unspread(memory_sums)

    def weight_part(mats, rows):
        return low(matmul_tn(mats[0], rows[0]) + matmul_tn(mats[1], rows[1]))

    in_parts = [weight_part(term, rows_one) for term in (gsv, gsk, gsq)]
    in_parts, mlp_here = lax.optimization_barrier((in_parts, mlp_here))
    in_sums = [narrow_total(part) for part in in_parts]
    mlp_pieces = core_pieces(chip_pieces(mlp_here))
    grad_h1 = spread_out([(gsq, ws_q), (gsk, ws_k), (gsv, ws_v)])
    _, norm_pull1 = jax.vjp(normed, x, gain[0])
    part_x, grad_gain1 = norm_pull1(grad_h1)
    grad_x = low(grad_x1 + part_x)
    gain_terms = jnp.stack([grad_gain1, grad_gain2, grad_gain3])
    levels = jnp.sum(lax.all_gather(gain_terms, "narrow", axis=0, tiled=False), axis=0)
    own_gains = width // lax.axis_size("narrow")
    gain_own = lax.dynamic_slice_in_dim(levels, level * own_gains, own_gains, 1)
    gain_total = jnp.sum(lax.all_gather(gain_own, "wide", axis=0, tiled=False), axis=0)
    mid_sides = side_pieces(spread(after(mid_sums, grad_x, *mlp_pieces[1:3])))
    last = jnp.stack([in_sums[2], in_sums[1], in_sums[0], self_out_sum])
    last, mlp_pieces, mid_sides, grad_x, gain_total = lax.optimization_barrier(
        (last, mlp_pieces, mid_sides, grad_x, gain_total)
    )
    grad_tokens = unspread(grad_x)
    mid_pieces = core_pieces(corner_pieces(mid_sides))
    mlp_totals = placed(mlp_pieces, spot_zero, ((0, 1), (2,)))
    last_hop, mlp_totals = lax.optimization_barrier((plane_hop(last), mlp_totals))
    last_sides = side_pieces(level_hop(last_hop))
    last_sides, mid_pieces = lax.optimization_barrier((last_sides, mid_pieces))
    mid_totals = placed(mid_pieces, spot_zero, ((3,), (2, 1), (0,)))
    last_chip = corner_pieces(last_sides)
    last_chip, mid_totals = lax.optimization_barrier((last_chip, mid_totals))
    in_totals, out_totals = placed(core_pieces(last_chip), spot_zero, ((0, 1, 2), (3,)))
    branch_three = branch_sum(after(matmul_nn(hidden, wm_out), in_parts[2]))
    output = unspread(low(x2 + branch_three))
    return (
        output,
        grad_tokens,
        grad_memory,
        gain_total,
        in_totals.swapaxes(0, 1),
        out_totals,
        *mid_totals,
        *mlp_totals,
    )


def solution(mesh):
    in_plane = (mesh.shape["wide"], mesh.shape["narrow"]) == (8, 4)
    return jax.shard_map(
        per_device if in_plane else per_device_general,
        mesh=mesh,
        in_specs=(
            P(("wide", "narrow"), None),
            P(("wide", "narrow"), None),
            P("wide", None),
            P("wide", None),
            P(),
            P(("wide", "narrow"), None, None),
            P(("wide", "narrow"), None),
            P(("wide", "narrow"), None),
            P(("wide", "narrow"), None, None),
            P(("wide", "narrow"), None),
            P(("wide", "narrow"), None, None),
            P(("wide", "narrow"), None),
            P(("wide", "narrow"), None),
        ),
        out_specs=(
            P(("wide", "narrow"), None),
            P(("wide", "narrow"), None),
            P(("wide", "narrow"), None),
            P(None, "narrow"),
            P("narrow", None, None),
            P("narrow", None),
            P("narrow", None),
            P("narrow", None, None),
            P("narrow", None),
            P("narrow", None, None),
            P("narrow", None),
        ),
        check_vma=False,
    )
```

```python
import jax
import jax.numpy as jnp
from jax import lax
from jax.experimental import pallas as pl
from jax.experimental.pallas import tpu as pltpu
from jax.sharding import PartitionSpec as P

HEAD_DIM = 128


EPSILON = 1e-06
ROBOT_WEIGHT = 2.0
NEGATIVE = -1e30


def normed(values, gain_row):
    factor = lax.rsqrt(jnp.mean(values * values, axis=-1, keepdims=True) + EPSILON)
    return values * factor * gain_row


def token_info(lengths, item_kinds, positions, item_count):
    item_ends = jnp.cumsum(lengths)
    segment = jnp.sum((positions[:, None] >= item_ends[None, :]).astype(jnp.int32), axis=1)
    token_valid = segment < item_count
    item_hit = segment[:, None] == jnp.arange(item_count, dtype=jnp.int32)[None, :]
    robot_flag = jnp.sum(jnp.where(item_hit, item_kinds[None, :], 0), axis=1)
    weight = jnp.where(token_valid, jnp.where(robot_flag == 1, ROBOT_WEIGHT, 1.0), 0.0).astype(
        jnp.float32
    )
    return (segment, token_valid, weight)


def attend_forward(queries, keys_all, values_all, allowed):
    scores = jnp.einsum(
        "qhd,khd->hqk", queries, keys_all, preferred_element_type=jnp.float32
    ) * HEAD_DIM ** (-0.5)
    scores = jnp.where(allowed[None], scores, NEGATIVE)
    row_top = jnp.max(scores, axis=2, keepdims=True)
    exp_scores = jnp.exp(scores - row_top)
    denom_sum = jnp.sum(exp_scores, axis=2, keepdims=True)
    soft_probs = (exp_scores / denom_sum).astype(jnp.bfloat16)
    result = jnp.einsum("hqk,khd->qhd", soft_probs, values_all, preferred_element_type=jnp.float32)
    return (result, row_top + jnp.log(denom_sum))


def attend_backward(queries, keys_all, values_all, allowed, log_sums, grad_out):
    score_scale = HEAD_DIM ** (-0.5)
    scores = (
        jnp.einsum("qhd,khd->hqk", queries, keys_all, preferred_element_type=jnp.float32)
        * score_scale
    )
    scores = jnp.where(allowed[None], scores, NEGATIVE)
    soft_probs = jnp.exp(scores - log_sums)
    grad_probs = jnp.einsum(
        "qhd,khd->hqk", grad_out, values_all, preferred_element_type=jnp.float32
    )
    row_inner = jnp.sum(soft_probs * grad_probs, axis=2, keepdims=True)
    grad_scores = (soft_probs * (grad_probs - row_inner)).astype(jnp.bfloat16)
    grad_query = (
        jnp.einsum("hqk,khd->qhd", grad_scores, keys_all, preferred_element_type=jnp.float32)
        * score_scale
    )
    grad_keys = (
        jnp.einsum("hqk,qhd->khd", grad_scores, queries, preferred_element_type=jnp.float32)
        * score_scale
    )
    grad_values = jnp.einsum(
        "hqk,qhd->khd",
        soft_probs.astype(jnp.bfloat16),
        grad_out,
        preferred_element_type=jnp.float32,
    )
    return (grad_query, grad_keys, grad_values)


def spread_tables(wide, narrow):
    total = wide * narrow
    ratio = wide // narrow
    if (wide, narrow) == (8, 4):
        first, second, spots = [], [], [[0] * wide for _ in range(narrow)]
        for block in range(total):
            w, n = divmod(block, narrow)
            q, c = divmod(w, ratio)
            z1, z0 = divmod(n, 2)
            spot = 2 * (q ^ (2 * c + z1)) + (z0 ^ c)
            first.append((block, spot * narrow + n))
            second.append((spot * narrow + n, spot * narrow + q))
            spots[q][block - q * wide] = spot
        return (first, second, spots)
    direct = []
    for block in range(total):
        n, w = divmod(block, wide)
        direct.append((block, w * narrow + n))
    return (direct, None, None)


def spread(piece):
    first, second, _ = spread_tables(lax.axis_size("wide"), lax.axis_size("narrow"))
    piece = hop(piece, first)
    if second is not None:
        piece = hop(piece, second)
    return piece


def hop(piece, pairs):
    narrow = lax.axis_size("narrow")
    stay = [0] * (lax.axis_size("wide") * narrow)
    for source, target in pairs:
        stay[source] = int(source == target)
    here = lax.axis_index("wide") * narrow + lax.axis_index("narrow")
    moved = lax.ppermute(
        piece, ("wide", "narrow"), [pair for pair in pairs if pair[0] != pair[1]]
    )
    return jnp.where(jnp.asarray(stay, jnp.int32)[here] == 1, piece, moved)


def plane_hop(piece):
    return hop(piece, spread_tables(lax.axis_size("wide"), lax.axis_size("narrow"))[0])


def level_hop(piece):
    return hop(piece, spread_tables(lax.axis_size("wide"), lax.axis_size("narrow"))[1])


def wide_gather(pieces):
    rows, width = pieces[0].shape
    moved = spread(jnp.concatenate(pieces, axis=0))
    full = lax.all_gather(moved, "wide", axis=0, tiled=False)
    full = full.reshape(-1, len(pieces), rows, width)
    return tuple(full[:, kind].reshape(-1, width) for kind in range(len(pieces)))


def wide_total(terms):
    wide_count = lax.axis_size("wide")
    width = terms[0].shape[1]
    parts = [term.astype(jnp.bfloat16).reshape(wide_count, -1, width) for term in terms]
    packed = jnp.concatenate(parts, axis=1)
    rows = packed.shape[1]
    shard = lax.psum_scatter(
        packed.reshape(wide_count * rows, width), "wide", scatter_dimension=0, tiled=True
    )
    full = lax.all_gather(shard, "wide", axis=0, tiled=False)
    _, _, spots = spread_tables(wide_count, lax.axis_size("narrow"))
    if spots is not None:
        order = jnp.asarray(spots, jnp.int32)[lax.axis_index("narrow")]
        full = jnp.concatenate(
            [lax.dynamic_slice_in_dim(full, order[j], 1, 0) for j in range(wide_count)], axis=0
        )
    full = full.reshape(wide_count, len(terms), -1, width)
    return [
        full[:, kind].reshape(-1, width).astype(jnp.float32) for kind in range(len(terms))
    ]


def row_gather(local_rows):
    return lax.all_gather(local_rows, "narrow", axis=0, tiled=True)


def branch_sum(partial_rows):
    return lax.psum_scatter(
        partial_rows.astype(jnp.bfloat16), "narrow", scatter_dimension=0, tiled=True
    ).astype(jnp.float32)


def matmul_nt(a, b):
    return lax.dot_general(a, b, (((1,), (1,)), ((), ())), preferred_element_type=jnp.float32)


def matmul_nn(a, b):
    return lax.dot_general(a, b, (((1,), (0,)), ((), ())), preferred_element_type=jnp.float32)


def matmul_tn(a, b):
    return lax.dot_general(a, b, (((0,), (0,)), ((), ())), preferred_element_type=jnp.float32)


def tensor_pass(tokens, memory, gain_float, weights, cotangent, masks):
    segment, token_valid, valid_float, local_weight, self_ok, cross_ok = masks
    tok_rows = tokens.shape[0]
    group_rows = tok_rows * lax.axis_size("narrow")
    mem_group = memory.shape[0] * lax.axis_size("narrow")
    w_self_in, w_self_out, w_cross_q, w_cross_kv, w_cross_out, w_mlp_in, w_mlp_out = weights
    tok_float = tokens.astype(jnp.float32)
    h1 = normed(tok_float, gain_float[0]).astype(jnp.bfloat16)
    rows_one = row_gather(h1)
    ws_q, ws_k, ws_v = wide_gather([w_self_in[:, 0], w_self_in[:, 1], w_self_in[:, 2]])
    ws_out, wc_q, wc_k, wc_v, wc_out = wide_gather(
        [w_self_out, w_cross_q, w_cross_kv[:, 0], w_cross_kv[:, 1], w_cross_out]
    )
    wm_gate, wm_up, wm_out = wide_gather([w_mlp_in[:, 0], w_mlp_in[:, 1], w_mlp_out])
    memory_all = row_gather(memory)
    grad_y = cotangent.astype(jnp.float32) * local_weight[:, None]
    grad_mlp = row_gather(grad_y.astype(jnp.bfloat16))
    own_width = ws_out.shape[0]
    heads_here = own_width // HEAD_DIM

    def split(mat):
        return mat.reshape(mat.shape[0], heads_here, HEAD_DIM)

    def project(rows, mat):
        return matmul_nt(rows, mat).astype(jnp.bfloat16)

    sq, sk, sv = (split(project(rows_one, mat)) for mat in (ws_q, ws_k, ws_v))
    self_result, self_lse = attend_forward(sq, sk, sv, self_ok)
    self_heads = self_result.reshape(group_rows, own_width).astype(jnp.bfloat16)
    x1 = tok_float + branch_sum(matmul_nn(self_heads, ws_out))
    h2 = normed(x1, gain_float[1]).astype(jnp.bfloat16)
    rows_two = row_gather(h2)
    ck, cv = (split(project(memory_all, mat)) for mat in (wc_k, wc_v))
    cq = split(project(rows_two, wc_q))
    cross_result, cross_lse = attend_forward(cq, ck, cv, cross_ok)
    cross_heads = (
        (cross_result * valid_float[:, None, None])
        .reshape(group_rows, own_width)
        .astype(jnp.bfloat16)
    )
    x2 = x1 + branch_sum(matmul_nn(cross_heads, wc_out))
    h3 = normed(x2, gain_float[2]).astype(jnp.bfloat16)
    rows_three = row_gather(h3)
    gate = matmul_nt(rows_three, wm_gate)
    up = matmul_nt(rows_three, wm_up)
    hidden = (jax.nn.gelu(gate, approximate=True) * up).astype(jnp.bfloat16)
    output = (x2 + branch_sum(matmul_nn(hidden, wm_out))).astype(jnp.bfloat16)
    grad_hidden = matmul_nt(grad_mlp, wm_out)
    _, gelu_pull = jax.vjp(
        lambda gate_part, up_part: jax.nn.gelu(gate_part, approximate=True) * up_part, gate, up
    )
    grad_gate, grad_up = gelu_pull(grad_hidden)
    grad_gate = grad_gate.astype(jnp.bfloat16)
    grad_up = grad_up.astype(jnp.bfloat16)
    grad_h3 = branch_sum(matmul_nn(grad_gate, wm_gate) + matmul_nn(grad_up, wm_up))
    _, norm_pull3 = jax.vjp(normed, x2, gain_float[2])
    part_x2, grad_gain3 = norm_pull3(grad_h3)
    grad_x2 = grad_y + part_x2
    mlp_totals = wide_total(
        [
            matmul_tn(grad_gate, rows_three),
            matmul_tn(grad_up, rows_three),
            matmul_tn(hidden, grad_mlp),
        ]
    )
    grad_cross = row_gather(grad_x2.astype(jnp.bfloat16))
    grad_cross_heads = split(project(grad_cross, wc_out))
    grad_cross_heads = jnp.where(
        token_valid[:, None, None], grad_cross_heads, jnp.zeros_like(grad_cross_heads)
    )
    gq_heads, gk_heads, gv_heads = attend_backward(
        cq, ck, cv, cross_ok, cross_lse, grad_cross_heads
    )
    grad_cq = gq_heads.reshape(group_rows, own_width).astype(jnp.bfloat16)
    grad_ck = gk_heads.reshape(mem_group, own_width).astype(jnp.bfloat16)
    grad_cv = gv_heads.reshape(mem_group, own_width).astype(jnp.bfloat16)
    grad_h2 = branch_sum(matmul_nn(grad_cq, wc_q))
    _, norm_pull2 = jax.vjp(normed, x1, gain_float[1])
    part_x1, grad_gain2 = norm_pull2(grad_h2)
    grad_x1 = grad_x2 + part_x1
    grad_self = row_gather(grad_x1.astype(jnp.bfloat16))
    grad_memory = branch_sum(matmul_nn(grad_ck, wc_k) + matmul_nn(grad_cv, wc_v)).astype(
        jnp.bfloat16
    )
    mid_totals = wide_total(
        [
            matmul_tn(self_heads, grad_self),
            matmul_tn(grad_cq, rows_two),
            matmul_tn(grad_ck, memory_all),
            matmul_tn(grad_cv, memory_all),
            matmul_tn(cross_heads, grad_cross),
        ]
    )
    grad_self_heads = split(project(grad_self, ws_out))
    gsq, gsk, gsv = (
        mat.reshape(group_rows, own_width).astype(jnp.bfloat16)
        for mat in attend_backward(sq, sk, sv, self_ok, self_lse, grad_self_heads)
    )
    in_totals = wide_total(
        [matmul_tn(gsq, rows_one), matmul_tn(gsk, rows_one), matmul_tn(gsv, rows_one)]
    )
    grad_h1 = branch_sum(matmul_nn(gsq, ws_q) + matmul_nn(gsk, ws_k) + matmul_nn(gsv, ws_v))
    _, norm_pull1 = jax.vjp(normed, tok_float, gain_float[0])
    part_x, grad_gain1 = norm_pull1(grad_h1)
    grad_tokens = (grad_x1 + part_x).astype(jnp.bfloat16)
    gain_terms = jnp.stack([grad_gain1, grad_gain2, grad_gain3])
    return (output, grad_tokens, grad_memory, gain_terms, in_totals, mid_totals, mlp_totals)


def per_device_general(
    tokens,
    memory,
    item_len,
    item_kind,
    norm_gains,
    w_self_in,
    w_self_out,
    w_cross_q,
    w_cross_kv,
    w_cross_out,
    w_mlp_in,
    w_mlp_out,
    cotangent,
):
    tok_rows = tokens.shape[0]
    narrow_size = lax.axis_size("narrow")
    group_rows = tok_rows * narrow_size
    mem_group = memory.shape[0] * narrow_size
    lengths = item_len[0]
    item_count = lengths.shape[0]
    patch_rows = mem_group // item_count
    positions = jnp.arange(group_rows, dtype=jnp.int32)
    segment, token_valid, weight = token_info(lengths, item_kind[0], positions, item_count)
    local_weight = lax.dynamic_slice_in_dim(weight, lax.axis_index("narrow") * tok_rows, tok_rows)
    self_ok = (segment[:, None] == segment[None, :]) & (positions[None, :] <= positions[:, None])
    mem_item = jnp.arange(mem_group, dtype=jnp.int32) // patch_rows
    cross_ok = mem_item[None, :] == jnp.minimum(segment, item_count - 1)[:, None]
    valid_float = token_valid.astype(jnp.float32)
    masks = (segment, token_valid, valid_float, local_weight, self_ok, cross_ok)
    gain_float = norm_gains.astype(jnp.float32)
    weights = (w_self_in, w_self_out, w_cross_q, w_cross_kv, w_cross_out, w_mlp_in, w_mlp_out)
    output, grad_tokens, grad_memory, gain_terms, in_totals, mid_totals, mlp_totals = tensor_pass(
        tokens, memory, gain_float, weights, cotangent, masks
    )
    gain_shard = lax.psum_scatter(gain_terms, "narrow", scatter_dimension=1, tiled=True)
    gain_total = lax.psum(gain_shard, "wide")
    return (
        output,
        grad_tokens,
        grad_memory,
        gain_total,
        jnp.stack(in_totals, axis=1),
        mid_totals[0],
        mid_totals[1],
        jnp.stack([mid_totals[2], mid_totals[3]], axis=1),
        mid_totals[4],
        jnp.stack([mlp_totals[0], mlp_totals[1]], axis=1),
        mlp_totals[2],
    )


CORE, XDIM, YDIM = 1, 2, 4
PLANE = 8


def flip(value, bit):
    return lax.ppermute(value, "wide", [(i, i ^ bit) for i in range(PLANE)])


def unspread(piece):
    first, second, _ = spread_tables(lax.axis_size("wide"), lax.axis_size("narrow"))
    piece = hop(piece, [(b, a) for a, b in second])
    return hop(piece, [(b, a) for a, b in first])


def after(value, *others):
    return lax.optimization_barrier((value,) + others)[0]


def low(value):
    return jax.tree.map(lambda part: part.astype(jnp.bfloat16), value)


def plus(kept, moved):
    return kept.astype(jnp.float32) + moved.astype(jnp.float32)


def side_pieces(shard):
    return [shard, flip(shard, XDIM), flip(shard, YDIM)]


def corner_pieces(sides):
    half = sides[0].shape[-2] // 2
    return sides + [flip(sides[1][..., :half, :], YDIM), flip(sides[2][..., half:, :], XDIM)]


def chip_pieces(shard):
    return corner_pieces(side_pieces(shard))


def plane_gather(shard):
    own = jnp.concatenate(chip_pieces(shard), axis=0)
    return (own, flip(own, CORE))


def plane_scatter(kept, sent):
    return scatter_end(*scatter_start(kept, sent))


def scatter_start(kept, sent):
    chip = low(plus(kept, flip(low(sent), CORE)))
    lead, rows, width = chip.shape[:-2], chip.shape[-2] // 4, chip.shape[-1]
    half = rows // 2
    view = jnp.moveaxis(chip.reshape(lead + (2, 2, rows, width)), (-4, -3), (0, 1))
    part_a, part_b = view[..., :half, :], view[..., half:, :]
    part_a = plus(part_a[:, 0], flip(part_a[:, 1], XDIM))
    part_b = plus(part_b[0], flip(part_b[1], YDIM))
    return (part_a, part_b)


def scatter_end(part_a, part_b):
    done_a = plus(part_a[0], flip(low(part_a[1]), YDIM))
    done_b = plus(part_b[0], flip(low(part_b[1]), XDIM))
    return jnp.concatenate([done_a, done_b], axis=-2)


def group_attend(queries, keys_all, values_all, allowed):
    scores = jnp.einsum(
        "gqhd,gkhd->ghqk", queries, keys_all, preferred_element_type=jnp.float32
    ) * HEAD_DIM ** (-0.5)
    scores = jnp.where(allowed[:, None], scores, NEGATIVE)
    row_top = jnp.max(scores, axis=3, keepdims=True)
    exp_scores = jnp.exp(scores - row_top)
    denom_sum = jnp.sum(exp_scores, axis=3, keepdims=True)
    soft_probs = low(exp_scores / denom_sum)
    result = jnp.einsum(
        "ghqk,gkhd->gqhd", soft_probs, values_all, preferred_element_type=jnp.float32
    )
    return (result, row_top + jnp.log(denom_sum))


def group_attend_back(queries, keys_all, values_all, allowed, log_sums, grad_out):
    score_scale = HEAD_DIM ** (-0.5)
    scores = (
        jnp.einsum("gqhd,gkhd->ghqk", queries, keys_all, preferred_element_type=jnp.float32)
        * score_scale
    )
    scores = jnp.where(allowed[:, None], scores, NEGATIVE)
    soft_probs = jnp.exp(scores - log_sums)
    grad_probs = jnp.einsum(
        "gqhd,gkhd->ghqk", grad_out, values_all, preferred_element_type=jnp.float32
    )
    row_inner = jnp.sum(soft_probs * grad_probs, axis=3, keepdims=True)
    grad_scores = low(soft_probs * (grad_probs - row_inner))
    grad_query = (
        jnp.einsum("ghqk,gkhd->gqhd", grad_scores, keys_all, preferred_element_type=jnp.float32)
        * score_scale
    )
    grad_keys = (
        jnp.einsum("ghqk,gqhd->gkhd", grad_scores, queries, preferred_element_type=jnp.float32)
        * score_scale
    )
    grad_values = jnp.einsum(
        "ghqk,gqhd->gkhd", low(soft_probs), grad_out, preferred_element_type=jnp.float32
    )
    return (grad_query, grad_keys, grad_values)


def narrow_full(stacked):
    kinds, rows, width = stacked.shape
    full = lax.all_gather(stacked.reshape(kinds * rows, width), "narrow", axis=0, tiled=False)
    full = full.reshape(-1, kinds, rows, width)
    return [full[:, kind].reshape(-1, width) for kind in range(kinds)]


def narrow_total(term):
    return lax.psum_scatter(low(term), "narrow", scatter_dimension=0, tiled=True)


PIECE_FLIPS = (0, 2, 5, 7, 1, 3, 4, 6)
WIDE_FLIPS = (0, 2, 4, 6, 1, 3, 5, 7)


def place_body(spots, *refs, plan, source_count):
    sources, outs = refs[:source_count], refs[source_count:]
    step, part = pl.program_id(0), pl.program_id(1)

    def write(source):
        for out, kinds in zip(outs, plan):
            if len(kinds) == 1:
                out[...] = source[kinds[0]].astype(out.dtype)
            elif len(kinds) == 2:
                for slot, kind in enumerate(kinds):
                    out[:, slot, :] = source[kind].astype(out.dtype)
            else:
                for slot, kind in enumerate(kinds):
                    out[slot] = source[kind].astype(out.dtype)

    for number, source in enumerate(sources):
        which, spot = number // 5, number % 5
        if spot < 3:
            hit = step == 4 * which + spot
        else:
            hit = (step == 4 * which + 3) & (part == spot - 3)

        @pl.when(hit)
        def _(source=source):
            write(source)


def core_pieces(chip):
    return chip + [flip(piece, CORE) for piece in chip]


def placed(sources, spot_zero, plan, flips=PIECE_FLIPS, kind=jnp.float32):
    kinds, rows, width = sources[0].shape
    half = rows // 2
    spots = spot_zero ^ jnp.asarray(flips, jnp.int32)

    def source_spec(number):
        which, spot = number // 5, number % 5
        if spot >= 3:
            return pl.BlockSpec((kinds, half, width), lambda step, part, spots: (0, 0, 0))
        mine = 4 * which + spot

        def index(step, part, spots):
            return (0, jnp.where(step == mine, part, jnp.where(step < mine, 0, 1)), 0)

        return pl.BlockSpec((kinds, half, width), index)

    out_specs, out_shapes = [], []
    for group in plan:
        count = len(group)
        if count == 1:
            block, shape = (half, width), (PLANE * rows, width)
            index = lambda step, part, spots: (2 * spots[step] + part, 0)
        elif count == 2:
            block, shape = (half, 2, width), (PLANE * rows, 2, width)
            index = lambda step, part, spots: (2 * spots[step] + part, 0, 0)
        else:
            block, shape = (count, half, width), (count, PLANE * rows, width)
            index = lambda step, part, spots: (0, 2 * spots[step] + part, 0)
        out_specs.append(pl.BlockSpec(block, index))
        out_shapes.append(jax.ShapeDtypeStruct(shape, kind))
    body = lambda *refs: place_body(*refs, plan=plan, source_count=len(sources))
    return pl.pallas_call(
        body,
        grid_spec=pltpu.PrefetchScalarGridSpec(
            num_scalar_prefetch=1,
            grid=(PLANE, 2),
            in_specs=[source_spec(number) for number in range(len(sources))],
            out_specs=out_specs,
        ),
        out_shape=out_shapes,
        compiler_params=pltpu.CompilerParams(
            dimension_semantics=("arbitrary", "arbitrary"), vmem_limit_bytes=56 * 1024 * 1024
        ),
        cost_estimate=pl.CostEstimate(
            flops=0,
            transcendentals=0,
            bytes_accessed=PLANE * kinds * rows * width * (2 + jnp.dtype(kind).itemsize),
        ),
        name="place",
    )(spots, *sources)


def per_device(
    tokens,
    memory,
    item_len,
    item_kind,
    norm_gains,
    w_self_in,
    w_self_out,
    w_cross_q,
    w_cross_kv,
    w_cross_out,
    w_mlp_in,
    w_mlp_out,
    cotangent,
):
    tok_rows, width = tokens.shape
    mem_rows = memory.shape[0]
    item_count = item_len.shape[1]
    gain = norm_gains.astype(jnp.float32)
    tokens_hop = plane_hop(tokens)
    mlp_shard = jnp.concatenate([w_mlp_in.swapaxes(0, 1), w_mlp_out[None]], axis=0)
    info_own = spread(jnp.concatenate([item_len, item_kind], axis=1))
    info = jnp.stack([info_own[0], flip(info_own, YDIM)[0]], axis=0)
    mlp_sides = side_pieces(after(mlp_shard, tokens_hop, info))
    tokens_here = level_hop(tokens_hop)
    ws_q, ws_k, ws_v = narrow_full(after(w_self_in.swapaxes(0, 1), tokens_here))
    x = tokens_here.astype(jnp.float32)
    h1 = after(low(normed(x, gain[0])), info)
    rows_one = plane_gather(h1)
    ws_out, wc_q = narrow_full(after(jnp.stack([w_self_out, w_cross_q]), ws_q))
    wc_k, wc_v = narrow_full(after(w_cross_kv.swapaxes(0, 1), ws_out))
    (wc_out,) = narrow_full(after(w_cross_out[None], wc_k))
    rows_one, memory_hop, cotangent_hop = lax.optimization_barrier(
        (rows_one, plane_hop(memory), plane_hop(cotangent))
    )
    memory_here = level_hop(memory_hop)
    cotangent_here = level_hop(after(cotangent_hop, memory_here))

    me, level = lax.axis_index("wide"), lax.axis_index("narrow")
    differ = (me >> 1) ^ level
    side, upper = differ >> 1, differ & 1
    quarter = 2 * upper + ((me & 1) ^ side)
    spot_zero = 4 * side + quarter
    order = jnp.asarray([0, 2, 1, 3], jnp.int32)
    quarters = jnp.stack([quarter ^ order, quarter ^ 1 ^ order], axis=0)
    positions = (
        quarters[:, :, None] * tok_rows + jnp.arange(tok_rows, dtype=jnp.int32)
    ).reshape(2, -1)
    segment, token_valid, weight = jax.vmap(token_info, in_axes=(0, 0, 0, None))(
        info[:, :item_count], info[:, item_count:], positions, item_count
    )
    local_weight = weight[0, :tok_rows]
    self_ok = (segment[:, :, None] == segment[:, None, :]) & (
        positions[:, None, :] <= positions[:, :, None]
    )
    patch_rows = mem_rows * (PLANE // 2) // item_count
    mem_item = (
        (quarters[:, :, None] * mem_rows + jnp.arange(mem_rows, dtype=jnp.int32)) // patch_rows
    ).reshape(2, -1)
    cross_ok = mem_item[:, None, :] == jnp.minimum(segment, item_count - 1)[:, :, None]
    valid_float = token_valid.astype(jnp.float32)

    own_width = ws_out.shape[0]
    heads_here = own_width // HEAD_DIM

    def project(rows, mat):
        parts = [low(matmul_nt(part, mat)).reshape(2, -1, heads_here, HEAD_DIM) for part in rows]
        return jnp.concatenate(parts, axis=1)

    def merge(mat):
        count = mat.shape[1] // 2
        return tuple(
            low(part.reshape(-1, own_width)) for part in (mat[:, :count], mat[:, count:])
        )

    def spread_out(terms):
        parts = [sum(matmul_nn(mat[part], weight) for mat, weight in terms) for part in (0, 1)]
        return plane_scatter(*parts)

    def weight_part(mats, rows):
        return low(matmul_tn(mats[0], rows[0]) + matmul_tn(mats[1], rows[1]))

    def packed_total(parts):
        levels = lax.axis_size("narrow")
        packed = jnp.stack([part.reshape(levels, -1, width) for part in parts], axis=1)
        total = lax.psum_scatter(
            packed.reshape(-1, width), "narrow", scatter_dimension=0, tiled=True
        )
        return total.reshape(len(parts), -1, width)

    sq, sk, sv = (project(rows_one, mat) for mat in (ws_q, ws_k, ws_v))
    self_result, self_lse = group_attend(sq, sk, sv, self_ok)
    self_heads = merge(self_result)
    self_heads, mlp_sides, memory_here = lax.optimization_barrier(
        (self_heads, mlp_sides, memory_here)
    )
    x1 = x + spread_out([(self_heads, ws_out)])
    h2 = low(normed(x1, gain[1]))
    memory_all = plane_gather(after(memory_here, h2))
    rows_two, cotangent_here = lax.optimization_barrier((plane_gather(h2), cotangent_here))
    ck, cv = (project(memory_all, mat) for mat in (wc_k, wc_v))
    cq = project(rows_two, wc_q)
    cross_result, cross_lse = group_attend(cq, ck, cv, cross_ok)
    cross_heads = merge(cross_result * valid_float[:, :, None, None])
    grad_y = cotangent_here.astype(jnp.float32) * local_weight[:, None]
    grad_mlp = row_gather(after(low(grad_y), wc_out))
    mlp_chip = corner_pieces(lax.optimization_barrier((mlp_sides, memory_all[0]))[0])
    cross_heads, grad_mlp, mlp_chip = lax.optimization_barrier((cross_heads, grad_mlp, mlp_chip))
    x2 = x1 + spread_out([(cross_heads, wc_out)])
    h3 = low(normed(x2, gain[2]))
    rows_three = row_gather(h3)
    wm_gate, wm_up, wm_out = placed(
        core_pieces(mlp_chip), me, ((0,), (1,), (2,)), WIDE_FLIPS, jnp.bfloat16
    )
    gate = matmul_nt(rows_three, wm_gate)
    up = matmul_nt(rows_three, wm_up)
    hidden = low(jax.nn.gelu(gate, approximate=True) * up)
    grad_hidden = matmul_nt(grad_mlp, wm_out)
    _, gelu_pull = jax.vjp(
        lambda gate_part, up_part: jax.nn.gelu(gate_part, approximate=True) * up_part, gate, up
    )
    grad_gate, grad_up = gelu_pull(grad_hidden)
    grad_gate, grad_up = low(grad_gate), low(grad_up)
    grad_h3 = branch_sum(matmul_nn(grad_gate, wm_gate) + matmul_nn(grad_up, wm_up))
    mlp_terms = ((grad_gate, rows_three), (grad_up, rows_three), (hidden, grad_mlp))
    mlp_packed = jnp.stack(
        [
            low(matmul_tn(mat, rows)).reshape(PLANE, -1, width)
            for mat, rows in mlp_terms
        ],
        axis=1,
    ).reshape(-1, width)
    mlp_packed, grad_h3 = lax.optimization_barrier((mlp_packed, grad_h3))
    mlp_sums = lax.psum_scatter(mlp_packed, "wide", scatter_dimension=0, tiled=True)
    mlp_sums = mlp_sums.reshape(3, -1, width)
    _, norm_pull3 = jax.vjp(normed, x2, gain[2])
    part_x2, grad_gain3 = norm_pull3(grad_h3)
    grad_x2 = grad_y + part_x2
    grad_cross = plane_gather(low(grad_x2))
    grad_cross_heads = project(grad_cross, wc_out)
    grad_cross_heads = jnp.where(
        token_valid[:, :, None, None], grad_cross_heads, jnp.zeros_like(grad_cross_heads)
    )
    grad_cq, grad_ck, grad_cv = (
        merge(mat)
        for mat in group_attend_back(cq, ck, cv, cross_ok, cross_lse, grad_cross_heads)
    )
    grad_h2 = spread_out([(grad_cq, wc_q)])
    _, norm_pull2 = jax.vjp(normed, x1, gain[1])
    part_x1, grad_gain2 = norm_pull2(grad_h2)
    grad_x1 = grad_x2 + part_x1
    grad_x1, mlp_sums = lax.optimization_barrier((grad_x1, mlp_sums))
    grad_self = plane_gather(low(grad_x1))
    memory_parts = [
        low(matmul_nn(grad_ck[part], wc_k) + matmul_nn(grad_cv[part], wc_v)) for part in (0, 1)
    ]
    mlp_here = spread(mlp_sums)
    mid_parts = [
        weight_part(cross_heads, grad_cross),
        weight_part(grad_cv, memory_all),
        weight_part(grad_ck, memory_all),
        weight_part(grad_cq, rows_two),
    ]
    mid_sums = packed_total(mid_parts)
    self_out_part = weight_part(self_heads, grad_self)
    grad_self_heads = project(grad_self, ws_out)
    gsq, gsk, gsv = (
        merge(mat) for mat in group_attend_back(sq, sk, sv, self_ok, self_lse, grad_self_heads)
    )
    gsq, gsk, gsv, mlp_here, memory_parts = lax.optimization_barrier(
        (gsq, gsk, gsv, mlp_here, memory_parts)
    )

    last_parts = [weight_part(term, rows_one) for term in (gsq, gsk, gsv)] + [self_out_part]
    last_parts, mlp_here = lax.optimization_barrier((last_parts, mlp_here))
    last = packed_total(last_parts)
    mlp_sides = side_pieces(mlp_here)
    grad_h1 = spread_out([(gsq, ws_q), (gsk, ws_k), (gsv, ws_v)])
    _, norm_pull1 = jax.vjp(normed, x, gain[0])
    part_x, grad_gain1 = norm_pull1(grad_h1)
    grad_x = low(grad_x1 + part_x)
    gain_terms = jnp.stack([grad_gain1, grad_gain2, grad_gain3])
    for bit in (1, 2):
        pairs = [(i, i ^ bit) for i in range(lax.axis_size("narrow"))]
        gain_terms = gain_terms + lax.ppermute(gain_terms, "narrow", pairs)
    for bit in (CORE, XDIM, YDIM):
        gain_terms = gain_terms + flip(gain_terms, bit)
    own_gains = width // lax.axis_size("narrow")
    gain_total = lax.dynamic_slice_in_dim(gain_terms, level * own_gains, own_gains, 1)
    group_hop = plane_hop(jnp.concatenate([last, mid_sums], axis=0))
    memory_sums = low(plane_scatter(memory_parts[0], after(memory_parts[1], mlp_sides[1])))
    mlp_sides, group_hop, grad_x, memory_sums = lax.optimization_barrier(
        (mlp_sides, group_hop, grad_x, memory_sums)
    )
    mlp_chip = corner_pieces(mlp_sides)
    group_here = level_hop(group_hop)
    mlp_chip, group_here = lax.optimization_barrier((mlp_chip, group_here))
    grad_memory = unspread(memory_sums)
    mlp_pieces = core_pieces(mlp_chip)
    group_sides = side_pieces(group_here)
    group_sides, mlp_pieces = lax.optimization_barrier((group_sides, mlp_pieces))
    mlp_totals = placed(mlp_pieces, spot_zero, ((0, 1), (2,)))
    group_chip = corner_pieces(group_sides)
    group_chip, mlp_totals = lax.optimization_barrier((group_chip, mlp_totals))
    in_totals, *other_totals = placed(
        core_pieces(group_chip), spot_zero, ((0, 1, 2), (3,), (7,), (6, 5), (4,))
    )
    grad_tokens = unspread(grad_x)
    branch_three = branch_sum(after(matmul_nn(hidden, wm_out), group_here))
    output = unspread(low(x2 + branch_three))
    return (
        output,
        grad_tokens,
        grad_memory,
        gain_total,
        in_totals.swapaxes(0, 1),
        *other_totals,
        *mlp_totals,
    )


def solution(mesh):
    in_plane = (mesh.shape["wide"], mesh.shape["narrow"]) == (8, 4)
    return jax.shard_map(
        per_device if in_plane else per_device_general,
        mesh=mesh,
        in_specs=(
            P(("wide", "narrow"), None),
            P(("wide", "narrow"), None),
            P("wide", None),
            P("wide", None),
            P(),
            P(("wide", "narrow"), None, None),
            P(("wide", "narrow"), None),
            P(("wide", "narrow"), None),
            P(("wide", "narrow"), None, None),
            P(("wide", "narrow"), None),
            P(("wide", "narrow"), None, None),
            P(("wide", "narrow"), None),
            P(("wide", "narrow"), None),
        ),
        out_specs=(
            P(("wide", "narrow"), None),
            P(("wide", "narrow"), None),
            P(("wide", "narrow"), None),
            P(None, "narrow"),
            P("narrow", None, None),
            P("narrow", None),
            P("narrow", None),
            P("narrow", None, None),
            P("narrow", None),
            P("narrow", None, None),
            P("narrow", None),
        ),
        check_vma=False,
    )
```

```python
import jax
import jax.numpy as jnp
from jax import lax
from jax.experimental import pallas as pl
from jax.experimental.pallas import tpu as pltpu
from jax.sharding import PartitionSpec as P

HEAD_DIM = 128


EPSILON = 1e-06
ROBOT_WEIGHT = 2.0
NEGATIVE = -1e30


def normed(values, gain_row):
    factor = lax.rsqrt(jnp.mean(values * values, axis=-1, keepdims=True) + EPSILON)
    return values * factor * gain_row


def token_info(lengths, item_kinds, positions, item_count):
    item_ends = jnp.cumsum(lengths)
    segment = jnp.sum((positions[:, None] >= item_ends[None, :]).astype(jnp.int32), axis=1)
    token_valid = segment < item_count
    item_hit = segment[:, None] == jnp.arange(item_count, dtype=jnp.int32)[None, :]
    robot_flag = jnp.sum(jnp.where(item_hit, item_kinds[None, :], 0), axis=1)
    weight = jnp.where(token_valid, jnp.where(robot_flag == 1, ROBOT_WEIGHT, 1.0), 0.0).astype(
        jnp.float32
    )
    return (segment, token_valid, weight)


def attend_forward(queries, keys_all, values_all, allowed):
    scores = jnp.einsum(
        "qhd,khd->hqk", queries, keys_all, preferred_element_type=jnp.float32
    ) * HEAD_DIM ** (-0.5)
    scores = jnp.where(allowed[None], scores, NEGATIVE)
    row_top = jnp.max(scores, axis=2, keepdims=True)
    exp_scores = jnp.exp(scores - row_top)
    denom_sum = jnp.sum(exp_scores, axis=2, keepdims=True)
    soft_probs = (exp_scores / denom_sum).astype(jnp.bfloat16)
    result = jnp.einsum("hqk,khd->qhd", soft_probs, values_all, preferred_element_type=jnp.float32)
    return (result, row_top + jnp.log(denom_sum))


def attend_backward(queries, keys_all, values_all, allowed, log_sums, grad_out):
    score_scale = HEAD_DIM ** (-0.5)
    scores = (
        jnp.einsum("qhd,khd->hqk", queries, keys_all, preferred_element_type=jnp.float32)
        * score_scale
    )
    scores = jnp.where(allowed[None], scores, NEGATIVE)
    soft_probs = jnp.exp(scores - log_sums)
    grad_probs = jnp.einsum(
        "qhd,khd->hqk", grad_out, values_all, preferred_element_type=jnp.float32
    )
    row_inner = jnp.sum(soft_probs * grad_probs, axis=2, keepdims=True)
    grad_scores = (soft_probs * (grad_probs - row_inner)).astype(jnp.bfloat16)
    grad_query = (
        jnp.einsum("hqk,khd->qhd", grad_scores, keys_all, preferred_element_type=jnp.float32)
        * score_scale
    )
    grad_keys = (
        jnp.einsum("hqk,qhd->khd", grad_scores, queries, preferred_element_type=jnp.float32)
        * score_scale
    )
    grad_values = jnp.einsum(
        "hqk,qhd->khd",
        soft_probs.astype(jnp.bfloat16),
        grad_out,
        preferred_element_type=jnp.float32,
    )
    return (grad_query, grad_keys, grad_values)


def spread_tables(wide, narrow):
    total = wide * narrow
    ratio = wide // narrow
    if (wide, narrow) == (8, 4):
        first, second, spots = [], [], [[0] * wide for _ in range(narrow)]
        for block in range(total):
            w, n = divmod(block, narrow)
            q, c = divmod(w, ratio)
            z1, z0 = divmod(n, 2)
            spot = 2 * (q ^ (2 * c + z1)) + (z0 ^ c)
            first.append((block, spot * narrow + n))
            second.append((spot * narrow + n, spot * narrow + q))
            spots[q][block - q * wide] = spot
        return (first, second, spots)
    direct = []
    for block in range(total):
        n, w = divmod(block, wide)
        direct.append((block, w * narrow + n))
    return (direct, None, None)


def spread(piece):
    first, second, _ = spread_tables(lax.axis_size("wide"), lax.axis_size("narrow"))
    piece = hop(piece, first)
    if second is not None:
        piece = hop(piece, second)
    return piece


def hop(piece, pairs):
    narrow = lax.axis_size("narrow")
    stay = [0] * (lax.axis_size("wide") * narrow)
    for source, target in pairs:
        stay[source] = int(source == target)
    here = lax.axis_index("wide") * narrow + lax.axis_index("narrow")
    moved = lax.ppermute(
        piece, ("wide", "narrow"), [pair for pair in pairs if pair[0] != pair[1]]
    )
    return jnp.where(jnp.asarray(stay, jnp.int32)[here] == 1, piece, moved)


def plane_hop(piece):
    return hop(piece, spread_tables(lax.axis_size("wide"), lax.axis_size("narrow"))[0])


def level_hop(piece):
    return hop(piece, spread_tables(lax.axis_size("wide"), lax.axis_size("narrow"))[1])


def wide_gather(pieces):
    rows, width = pieces[0].shape
    moved = spread(jnp.concatenate(pieces, axis=0))
    full = lax.all_gather(moved, "wide", axis=0, tiled=False)
    full = full.reshape(-1, len(pieces), rows, width)
    return tuple(full[:, kind].reshape(-1, width) for kind in range(len(pieces)))


def wide_total(terms):
    wide_count = lax.axis_size("wide")
    width = terms[0].shape[1]
    parts = [term.astype(jnp.bfloat16).reshape(wide_count, -1, width) for term in terms]
    packed = jnp.concatenate(parts, axis=1)
    rows = packed.shape[1]
    shard = lax.psum_scatter(
        packed.reshape(wide_count * rows, width), "wide", scatter_dimension=0, tiled=True
    )
    full = lax.all_gather(shard, "wide", axis=0, tiled=False)
    _, _, spots = spread_tables(wide_count, lax.axis_size("narrow"))
    if spots is not None:
        order = jnp.asarray(spots, jnp.int32)[lax.axis_index("narrow")]
        full = jnp.concatenate(
            [lax.dynamic_slice_in_dim(full, order[j], 1, 0) for j in range(wide_count)], axis=0
        )
    full = full.reshape(wide_count, len(terms), -1, width)
    return [
        full[:, kind].reshape(-1, width).astype(jnp.float32) for kind in range(len(terms))
    ]


def row_gather(local_rows):
    return lax.all_gather(local_rows, "narrow", axis=0, tiled=True)


def branch_sum(partial_rows):
    return lax.psum_scatter(
        partial_rows.astype(jnp.bfloat16), "narrow", scatter_dimension=0, tiled=True
    ).astype(jnp.float32)


def matmul_nt(a, b):
    return lax.dot_general(a, b, (((1,), (1,)), ((), ())), preferred_element_type=jnp.float32)


def matmul_nn(a, b):
    return lax.dot_general(a, b, (((1,), (0,)), ((), ())), preferred_element_type=jnp.float32)


def matmul_tn(a, b):
    return lax.dot_general(a, b, (((0,), (0,)), ((), ())), preferred_element_type=jnp.float32)


def tensor_pass(tokens, memory, gain_float, weights, cotangent, masks):
    segment, token_valid, valid_float, local_weight, self_ok, cross_ok = masks
    tok_rows = tokens.shape[0]
    group_rows = tok_rows * lax.axis_size("narrow")
    mem_group = memory.shape[0] * lax.axis_size("narrow")
    w_self_in, w_self_out, w_cross_q, w_cross_kv, w_cross_out, w_mlp_in, w_mlp_out = weights
    tok_float = tokens.astype(jnp.float32)
    h1 = normed(tok_float, gain_float[0]).astype(jnp.bfloat16)
    rows_one = row_gather(h1)
    ws_q, ws_k, ws_v = wide_gather([w_self_in[:, 0], w_self_in[:, 1], w_self_in[:, 2]])
    ws_out, wc_q, wc_k, wc_v, wc_out = wide_gather(
        [w_self_out, w_cross_q, w_cross_kv[:, 0], w_cross_kv[:, 1], w_cross_out]
    )
    wm_gate, wm_up, wm_out = wide_gather([w_mlp_in[:, 0], w_mlp_in[:, 1], w_mlp_out])
    memory_all = row_gather(memory)
    grad_y = cotangent.astype(jnp.float32) * local_weight[:, None]
    grad_mlp = row_gather(grad_y.astype(jnp.bfloat16))
    own_width = ws_out.shape[0]
    heads_here = own_width // HEAD_DIM

    def split(mat):
        return mat.reshape(mat.shape[0], heads_here, HEAD_DIM)

    def project(rows, mat):
        return matmul_nt(rows, mat).astype(jnp.bfloat16)

    sq, sk, sv = (split(project(rows_one, mat)) for mat in (ws_q, ws_k, ws_v))
    self_result, self_lse = attend_forward(sq, sk, sv, self_ok)
    self_heads = self_result.reshape(group_rows, own_width).astype(jnp.bfloat16)
    x1 = tok_float + branch_sum(matmul_nn(self_heads, ws_out))
    h2 = normed(x1, gain_float[1]).astype(jnp.bfloat16)
    rows_two = row_gather(h2)
    ck, cv = (split(project(memory_all, mat)) for mat in (wc_k, wc_v))
    cq = split(project(rows_two, wc_q))
    cross_result, cross_lse = attend_forward(cq, ck, cv, cross_ok)
    cross_heads = (
        (cross_result * valid_float[:, None, None])
        .reshape(group_rows, own_width)
        .astype(jnp.bfloat16)
    )
    x2 = x1 + branch_sum(matmul_nn(cross_heads, wc_out))
    h3 = normed(x2, gain_float[2]).astype(jnp.bfloat16)
    rows_three = row_gather(h3)
    gate = matmul_nt(rows_three, wm_gate)
    up = matmul_nt(rows_three, wm_up)
    hidden = (jax.nn.gelu(gate, approximate=True) * up).astype(jnp.bfloat16)
    output = (x2 + branch_sum(matmul_nn(hidden, wm_out))).astype(jnp.bfloat16)
    grad_hidden = matmul_nt(grad_mlp, wm_out)
    _, gelu_pull = jax.vjp(
        lambda gate_part, up_part: jax.nn.gelu(gate_part, approximate=True) * up_part, gate, up
    )
    grad_gate, grad_up = gelu_pull(grad_hidden)
    grad_gate = grad_gate.astype(jnp.bfloat16)
    grad_up = grad_up.astype(jnp.bfloat16)
    grad_h3 = branch_sum(matmul_nn(grad_gate, wm_gate) + matmul_nn(grad_up, wm_up))
    _, norm_pull3 = jax.vjp(normed, x2, gain_float[2])
    part_x2, grad_gain3 = norm_pull3(grad_h3)
    grad_x2 = grad_y + part_x2
    mlp_totals = wide_total(
        [
            matmul_tn(grad_gate, rows_three),
            matmul_tn(grad_up, rows_three),
            matmul_tn(hidden, grad_mlp),
        ]
    )
    grad_cross = row_gather(grad_x2.astype(jnp.bfloat16))
    grad_cross_heads = split(project(grad_cross, wc_out))
    grad_cross_heads = jnp.where(
        token_valid[:, None, None], grad_cross_heads, jnp.zeros_like(grad_cross_heads)
    )
    gq_heads, gk_heads, gv_heads = attend_backward(
        cq, ck, cv, cross_ok, cross_lse, grad_cross_heads
    )
    grad_cq = gq_heads.reshape(group_rows, own_width).astype(jnp.bfloat16)
    grad_ck = gk_heads.reshape(mem_group, own_width).astype(jnp.bfloat16)
    grad_cv = gv_heads.reshape(mem_group, own_width).astype(jnp.bfloat16)
    grad_h2 = branch_sum(matmul_nn(grad_cq, wc_q))
    _, norm_pull2 = jax.vjp(normed, x1, gain_float[1])
    part_x1, grad_gain2 = norm_pull2(grad_h2)
    grad_x1 = grad_x2 + part_x1
    grad_self = row_gather(grad_x1.astype(jnp.bfloat16))
    grad_memory = branch_sum(matmul_nn(grad_ck, wc_k) + matmul_nn(grad_cv, wc_v)).astype(
        jnp.bfloat16
    )
    mid_totals = wide_total(
        [
            matmul_tn(self_heads, grad_self),
            matmul_tn(grad_cq, rows_two),
            matmul_tn(grad_ck, memory_all),
            matmul_tn(grad_cv, memory_all),
            matmul_tn(cross_heads, grad_cross),
        ]
    )
    grad_self_heads = split(project(grad_self, ws_out))
    gsq, gsk, gsv = (
        mat.reshape(group_rows, own_width).astype(jnp.bfloat16)
        for mat in attend_backward(sq, sk, sv, self_ok, self_lse, grad_self_heads)
    )
    in_totals = wide_total(
        [matmul_tn(gsq, rows_one), matmul_tn(gsk, rows_one), matmul_tn(gsv, rows_one)]
    )
    grad_h1 = branch_sum(matmul_nn(gsq, ws_q) + matmul_nn(gsk, ws_k) + matmul_nn(gsv, ws_v))
    _, norm_pull1 = jax.vjp(normed, tok_float, gain_float[0])
    part_x, grad_gain1 = norm_pull1(grad_h1)
    grad_tokens = (grad_x1 + part_x).astype(jnp.bfloat16)
    gain_terms = jnp.stack([grad_gain1, grad_gain2, grad_gain3])
    return (output, grad_tokens, grad_memory, gain_terms, in_totals, mid_totals, mlp_totals)


def per_device_general(
    tokens,
    memory,
    item_len,
    item_kind,
    norm_gains,
    w_self_in,
    w_self_out,
    w_cross_q,
    w_cross_kv,
    w_cross_out,
    w_mlp_in,
    w_mlp_out,
    cotangent,
):
    tok_rows = tokens.shape[0]
    narrow_size = lax.axis_size("narrow")
    group_rows = tok_rows * narrow_size
    mem_group = memory.shape[0] * narrow_size
    lengths = item_len[0]
    item_count = lengths.shape[0]
    patch_rows = mem_group // item_count
    positions = jnp.arange(group_rows, dtype=jnp.int32)
    segment, token_valid, weight = token_info(lengths, item_kind[0], positions, item_count)
    local_weight = lax.dynamic_slice_in_dim(weight, lax.axis_index("narrow") * tok_rows, tok_rows)
    self_ok = (segment[:, None] == segment[None, :]) & (positions[None, :] <= positions[:, None])
    mem_item = jnp.arange(mem_group, dtype=jnp.int32) // patch_rows
    cross_ok = mem_item[None, :] == jnp.minimum(segment, item_count - 1)[:, None]
    valid_float = token_valid.astype(jnp.float32)
    masks = (segment, token_valid, valid_float, local_weight, self_ok, cross_ok)
    gain_float = norm_gains.astype(jnp.float32)
    weights = (w_self_in, w_self_out, w_cross_q, w_cross_kv, w_cross_out, w_mlp_in, w_mlp_out)
    output, grad_tokens, grad_memory, gain_terms, in_totals, mid_totals, mlp_totals = tensor_pass(
        tokens, memory, gain_float, weights, cotangent, masks
    )
    gain_shard = lax.psum_scatter(gain_terms, "narrow", scatter_dimension=1, tiled=True)
    gain_total = lax.psum(gain_shard, "wide")
    return (
        output,
        grad_tokens,
        grad_memory,
        gain_total,
        jnp.stack(in_totals, axis=1),
        mid_totals[0],
        mid_totals[1],
        jnp.stack([mid_totals[2], mid_totals[3]], axis=1),
        mid_totals[4],
        jnp.stack([mlp_totals[0], mlp_totals[1]], axis=1),
        mlp_totals[2],
    )


CORE, XDIM, YDIM = 1, 2, 4
PLANE = 8


def flip(value, bit):
    return lax.ppermute(value, "wide", [(i, i ^ bit) for i in range(PLANE)])


def unspread(piece):
    first, second, _ = spread_tables(lax.axis_size("wide"), lax.axis_size("narrow"))
    piece = hop(piece, [(b, a) for a, b in second])
    return hop(piece, [(b, a) for a, b in first])


def after(value, *others):
    return lax.optimization_barrier((value,) + others)[0]


def low(value):
    return jax.tree.map(lambda part: part.astype(jnp.bfloat16), value)


def plus(kept, moved):
    return kept.astype(jnp.float32) + moved.astype(jnp.float32)


def side_pieces(shard):
    return [shard, flip(shard, XDIM), flip(shard, YDIM)]


def corner_pieces(sides):
    half = sides[0].shape[-2] // 2
    return sides + [flip(sides[1][..., :half, :], YDIM), flip(sides[2][..., half:, :], XDIM)]


def chip_pieces(shard):
    return corner_pieces(side_pieces(shard))


def plane_gather(shard):
    own = jnp.concatenate(chip_pieces(shard), axis=0)
    return (own, flip(own, CORE))


def plane_scatter(kept, sent):
    return scatter_end(*scatter_start(kept, sent))


def scatter_start(kept, sent):
    chip = low(plus(kept, flip(low(sent), CORE)))
    lead, rows, width = chip.shape[:-2], chip.shape[-2] // 4, chip.shape[-1]
    half = rows // 2
    view = jnp.moveaxis(chip.reshape(lead + (2, 2, rows, width)), (-4, -3), (0, 1))
    part_a, part_b = view[..., :half, :], view[..., half:, :]
    part_a = plus(part_a[:, 0], flip(part_a[:, 1], XDIM))
    part_b = plus(part_b[0], flip(part_b[1], YDIM))
    return (part_a, part_b)


def scatter_end(part_a, part_b):
    done_a = plus(part_a[0], flip(low(part_a[1]), YDIM))
    done_b = plus(part_b[0], flip(low(part_b[1]), XDIM))
    return jnp.concatenate([done_a, done_b], axis=-2)


def group_attend(queries, keys_all, values_all, allowed):
    scores = jnp.einsum(
        "gqhd,gkhd->ghqk", queries, keys_all, preferred_element_type=jnp.float32
    ) * HEAD_DIM ** (-0.5)
    scores = jnp.where(allowed[:, None], scores, NEGATIVE)
    row_top = jnp.max(scores, axis=3, keepdims=True)
    exp_scores = jnp.exp(scores - row_top)
    denom_sum = jnp.sum(exp_scores, axis=3, keepdims=True)
    soft_probs = low(exp_scores / denom_sum)
    result = jnp.einsum(
        "ghqk,gkhd->gqhd", soft_probs, values_all, preferred_element_type=jnp.float32
    )
    return (result, row_top + jnp.log(denom_sum))


def group_attend_back(queries, keys_all, values_all, allowed, log_sums, grad_out):
    score_scale = HEAD_DIM ** (-0.5)
    scores = (
        jnp.einsum("gqhd,gkhd->ghqk", queries, keys_all, preferred_element_type=jnp.float32)
        * score_scale
    )
    scores = jnp.where(allowed[:, None], scores, NEGATIVE)
    soft_probs = jnp.exp(scores - log_sums)
    grad_probs = jnp.einsum(
        "gqhd,gkhd->ghqk", grad_out, values_all, preferred_element_type=jnp.float32
    )
    row_inner = jnp.sum(soft_probs * grad_probs, axis=3, keepdims=True)
    grad_scores = low(soft_probs * (grad_probs - row_inner))
    grad_query = (
        jnp.einsum("ghqk,gkhd->gqhd", grad_scores, keys_all, preferred_element_type=jnp.float32)
        * score_scale
    )
    grad_keys = (
        jnp.einsum("ghqk,gqhd->gkhd", grad_scores, queries, preferred_element_type=jnp.float32)
        * score_scale
    )
    grad_values = jnp.einsum(
        "ghqk,gqhd->gkhd", low(soft_probs), grad_out, preferred_element_type=jnp.float32
    )
    return (grad_query, grad_keys, grad_values)


def narrow_full(stacked):
    kinds, rows, width = stacked.shape
    full = lax.all_gather(stacked.reshape(kinds * rows, width), "narrow", axis=0, tiled=False)
    full = full.reshape(-1, kinds, rows, width)
    return [full[:, kind].reshape(-1, width) for kind in range(kinds)]


def narrow_total(term):
    return lax.psum_scatter(low(term), "narrow", scatter_dimension=0, tiled=True)


PIECE_FLIPS = (0, 2, 5, 7, 1, 3, 4, 6)
WIDE_FLIPS = (0, 2, 4, 6, 1, 3, 5, 7)


def place_body(spots, *refs, plan, source_count):
    sources, outs = refs[:source_count], refs[source_count:]
    step, part = pl.program_id(0), pl.program_id(1)

    def write(source):
        for out, kinds in zip(outs, plan):
            if len(kinds) == 1:
                out[...] = source[kinds[0]].astype(out.dtype)
            elif len(kinds) == 2:
                for slot, kind in enumerate(kinds):
                    out[:, slot, :] = source[kind].astype(out.dtype)
            else:
                for slot, kind in enumerate(kinds):
                    out[slot] = source[kind].astype(out.dtype)

    for number, source in enumerate(sources):
        which, spot = number // 5, number % 5
        if spot < 3:
            hit = step == 4 * which + spot
        else:
            hit = (step == 4 * which + 3) & (part == spot - 3)

        @pl.when(hit)
        def _(source=source):
            write(source)


def core_pieces(chip):
    return chip + [flip(piece, CORE) for piece in chip]


def placed(sources, spot_zero, plan, flips=PIECE_FLIPS, kind=jnp.float32):
    kinds, rows, width = sources[0].shape
    half = rows // 2
    spots = spot_zero ^ jnp.asarray(flips, jnp.int32)

    def source_spec(number):
        which, spot = number // 5, number % 5
        if spot >= 3:
            return pl.BlockSpec((kinds, half, width), lambda step, part, spots: (0, 0, 0))
        mine = 4 * which + spot

        def index(step, part, spots):
            return (0, jnp.where(step == mine, part, jnp.where(step < mine, 0, 1)), 0)

        return pl.BlockSpec((kinds, half, width), index)

    out_specs, out_shapes = [], []
    for group in plan:
        count = len(group)
        if count == 1:
            block, shape = (half, width), (PLANE * rows, width)
            index = lambda step, part, spots: (2 * spots[step] + part, 0)
        elif count == 2:
            block, shape = (half, 2, width), (PLANE * rows, 2, width)
            index = lambda step, part, spots: (2 * spots[step] + part, 0, 0)
        else:
            block, shape = (count, half, width), (count, PLANE * rows, width)
            index = lambda step, part, spots: (0, 2 * spots[step] + part, 0)
        out_specs.append(pl.BlockSpec(block, index))
        out_shapes.append(jax.ShapeDtypeStruct(shape, kind))
    body = lambda *refs: place_body(*refs, plan=plan, source_count=len(sources))
    return pl.pallas_call(
        body,
        grid_spec=pltpu.PrefetchScalarGridSpec(
            num_scalar_prefetch=1,
            grid=(PLANE, 2),
            in_specs=[source_spec(number) for number in range(len(sources))],
            out_specs=out_specs,
        ),
        out_shape=out_shapes,
        compiler_params=pltpu.CompilerParams(
            dimension_semantics=("arbitrary", "arbitrary"), vmem_limit_bytes=56 * 1024 * 1024
        ),
        cost_estimate=pl.CostEstimate(
            flops=0,
            transcendentals=0,
            bytes_accessed=PLANE * kinds * rows * width * (2 + jnp.dtype(kind).itemsize),
        ),
        name="place",
    )(spots, *sources)


def per_device(
    tokens,
    memory,
    item_len,
    item_kind,
    norm_gains,
    w_self_in,
    w_self_out,
    w_cross_q,
    w_cross_kv,
    w_cross_out,
    w_mlp_in,
    w_mlp_out,
    cotangent,
):
    tok_rows, width = tokens.shape
    mem_rows = memory.shape[0]
    item_count = item_len.shape[1]
    gain = norm_gains.astype(jnp.float32)
    tokens_hop = plane_hop(tokens)
    mlp_shard = jnp.concatenate([w_mlp_in.swapaxes(0, 1), w_mlp_out[None]], axis=0)
    info_own = spread(jnp.concatenate([item_len, item_kind], axis=1))
    info = jnp.stack([info_own[0], flip(info_own, YDIM)[0]], axis=0)
    tokens_here = level_hop(tokens_hop)
    ws_q, ws_k, ws_v = narrow_full(after(w_self_in.swapaxes(0, 1), tokens_here))
    x = tokens_here.astype(jnp.float32)
    h1 = after(low(normed(x, gain[0])), info)
    rows_one = plane_gather(h1)
    mlp_sides = side_pieces(after(mlp_shard, ws_q))
    ws_out, wc_q = narrow_full(after(jnp.stack([w_self_out, w_cross_q]), ws_q))
    wc_k, wc_v = narrow_full(after(w_cross_kv.swapaxes(0, 1), ws_out))
    (wc_out,) = narrow_full(after(w_cross_out[None], wc_k))
    rows_one, memory_hop, cotangent_hop = lax.optimization_barrier(
        (rows_one, plane_hop(memory), plane_hop(cotangent))
    )
    memory_here = level_hop(memory_hop)
    cotangent_here = level_hop(after(cotangent_hop, memory_here))

    me, level = lax.axis_index("wide"), lax.axis_index("narrow")
    differ = (me >> 1) ^ level
    side, upper = differ >> 1, differ & 1
    quarter = 2 * upper + ((me & 1) ^ side)
    spot_zero = 4 * side + quarter
    order = jnp.asarray([0, 2, 1, 3], jnp.int32)
    quarters = jnp.stack([quarter ^ order, quarter ^ 1 ^ order], axis=0)
    positions = (
        quarters[:, :, None] * tok_rows + jnp.arange(tok_rows, dtype=jnp.int32)
    ).reshape(2, -1)
    segment, token_valid, weight = jax.vmap(token_info, in_axes=(0, 0, 0, None))(
        info[:, :item_count], info[:, item_count:], positions, item_count
    )
    local_weight = weight[0, :tok_rows]
    self_ok = (segment[:, :, None] == segment[:, None, :]) & (
        positions[:, None, :] <= positions[:, :, None]
    )
    patch_rows = mem_rows * (PLANE // 2) // item_count
    mem_item = (
        (quarters[:, :, None] * mem_rows + jnp.arange(mem_rows, dtype=jnp.int32)) // patch_rows
    ).reshape(2, -1)
    cross_ok = mem_item[:, None, :] == jnp.minimum(segment, item_count - 1)[:, :, None]
    valid_float = token_valid.astype(jnp.float32)

    own_width = ws_out.shape[0]
    heads_here = own_width // HEAD_DIM

    def project(rows, mat):
        parts = [low(matmul_nt(part, mat)).reshape(2, -1, heads_here, HEAD_DIM) for part in rows]
        return jnp.concatenate(parts, axis=1)

    def merge(mat):
        count = mat.shape[1] // 2
        return tuple(
            low(part.reshape(-1, own_width)) for part in (mat[:, :count], mat[:, count:])
        )

    def spread_out(terms):
        parts = [sum(matmul_nn(mat[part], weight) for mat, weight in terms) for part in (0, 1)]
        return plane_scatter(*parts)

    def weight_part(mats, rows):
        return low(matmul_tn(mats[0], rows[0]) + matmul_tn(mats[1], rows[1]))

    def packed_total(parts):
        levels = lax.axis_size("narrow")
        packed = jnp.stack([part.reshape(levels, -1, width) for part in parts], axis=1)
        total = lax.psum_scatter(
            packed.reshape(-1, width), "narrow", scatter_dimension=0, tiled=True
        )
        return total.reshape(len(parts), -1, width)

    sq, sk, sv = (project(rows_one, mat) for mat in (ws_q, ws_k, ws_v))
    self_result, self_lse = group_attend(sq, sk, sv, self_ok)
    self_heads = merge(self_result)
    self_heads, mlp_sides, memory_here = lax.optimization_barrier(
        (self_heads, mlp_sides, memory_here)
    )
    x1 = x + spread_out([(self_heads, ws_out)])
    h2 = low(normed(x1, gain[1]))
    memory_all = plane_gather(after(memory_here, h2))
    rows_two, cotangent_here = lax.optimization_barrier((plane_gather(h2), cotangent_here))
    ck, cv = (project(memory_all, mat) for mat in (wc_k, wc_v))
    cq = project(rows_two, wc_q)
    cross_result, cross_lse = group_attend(cq, ck, cv, cross_ok)
    cross_heads = merge(cross_result * valid_float[:, :, None, None])
    grad_y = cotangent_here.astype(jnp.float32) * local_weight[:, None]
    grad_mlp = row_gather(after(low(grad_y), wc_out))
    mlp_chip = corner_pieces(lax.optimization_barrier((mlp_sides, memory_all[0]))[0])
    cross_heads, grad_mlp, mlp_chip = lax.optimization_barrier((cross_heads, grad_mlp, mlp_chip))
    x2 = x1 + spread_out([(cross_heads, wc_out)])
    h3 = low(normed(x2, gain[2]))
    rows_three = row_gather(h3)
    wm_gate, wm_up, wm_out = placed(
        core_pieces(mlp_chip), me, ((0,), (1,), (2,)), WIDE_FLIPS, jnp.bfloat16
    )
    gate = matmul_nt(rows_three, wm_gate)
    up = matmul_nt(rows_three, wm_up)
    hidden = low(jax.nn.gelu(gate, approximate=True) * up)
    grad_hidden = matmul_nt(grad_mlp, wm_out)
    _, gelu_pull = jax.vjp(
        lambda gate_part, up_part: jax.nn.gelu(gate_part, approximate=True) * up_part, gate, up
    )
    grad_gate, grad_up = gelu_pull(grad_hidden)
    grad_gate, grad_up = low(grad_gate), low(grad_up)
    grad_h3 = branch_sum(matmul_nn(grad_gate, wm_gate) + matmul_nn(grad_up, wm_up))
    mlp_terms = ((grad_gate, rows_three), (grad_up, rows_three), (hidden, grad_mlp))
    mlp_packed = jnp.stack(
        [
            low(matmul_tn(mat, rows)).reshape(PLANE, -1, width)
            for mat, rows in mlp_terms
        ],
        axis=1,
    ).reshape(-1, width)
    mlp_packed, grad_h3 = lax.optimization_barrier((mlp_packed, grad_h3))
    mlp_sums = lax.psum_scatter(mlp_packed, "wide", scatter_dimension=0, tiled=True)
    mlp_sums = mlp_sums.reshape(3, -1, width)
    _, norm_pull3 = jax.vjp(normed, x2, gain[2])
    part_x2, grad_gain3 = norm_pull3(grad_h3)
    grad_x2 = grad_y + part_x2
    grad_cross = plane_gather(low(grad_x2))
    grad_cross_heads = project(grad_cross, wc_out)
    grad_cross_heads = jnp.where(
        token_valid[:, :, None, None], grad_cross_heads, jnp.zeros_like(grad_cross_heads)
    )
    grad_cq, grad_ck, grad_cv = (
        merge(mat)
        for mat in group_attend_back(cq, ck, cv, cross_ok, cross_lse, grad_cross_heads)
    )
    grad_h2 = spread_out([(grad_cq, wc_q)])
    _, norm_pull2 = jax.vjp(normed, x1, gain[1])
    part_x1, grad_gain2 = norm_pull2(grad_h2)
    grad_x1 = grad_x2 + part_x1
    grad_x1, mlp_sums = lax.optimization_barrier((grad_x1, mlp_sums))
    grad_self = plane_gather(low(grad_x1))
    memory_parts = [
        low(matmul_nn(grad_ck[part], wc_k) + matmul_nn(grad_cv[part], wc_v)) for part in (0, 1)
    ]
    mlp_here = spread(mlp_sums)
    mid_parts = [
        weight_part(cross_heads, grad_cross),
        weight_part(grad_cv, memory_all),
        weight_part(grad_ck, memory_all),
        weight_part(grad_cq, rows_two),
    ]
    mid_sums = packed_total(mid_parts)
    self_out_part = weight_part(self_heads, grad_self)
    grad_self_heads = project(grad_self, ws_out)
    gsq, gsk, gsv = (
        merge(mat) for mat in group_attend_back(sq, sk, sv, self_ok, self_lse, grad_self_heads)
    )
    gsq, gsk, gsv, memory_parts = lax.optimization_barrier((gsq, gsk, gsv, memory_parts))

    last_parts = [weight_part(term, rows_one) for term in (gsq, gsk, gsv)] + [self_out_part]
    last_parts, mlp_here = lax.optimization_barrier((last_parts, mlp_here))
    last = packed_total(last_parts)
    mlp_sides = side_pieces(mlp_here)
    grad_h1 = spread_out([(gsq, ws_q), (gsk, ws_k), (gsv, ws_v)])
    _, norm_pull1 = jax.vjp(normed, x, gain[0])
    part_x, grad_gain1 = norm_pull1(grad_h1)
    grad_x = low(grad_x1 + part_x)
    gain_terms = jnp.stack([grad_gain1, grad_gain2, grad_gain3])
    for bit in (1, 2):
        pairs = [(i, i ^ bit) for i in range(lax.axis_size("narrow"))]
        gain_terms = gain_terms + lax.ppermute(gain_terms, "narrow", pairs)
    for bit in (CORE, XDIM, YDIM):
        gain_terms = gain_terms + flip(gain_terms, bit)
    own_gains = width // lax.axis_size("narrow")
    gain_total = lax.dynamic_slice_in_dim(gain_terms, level * own_gains, own_gains, 1)
    group_hop = plane_hop(jnp.concatenate([last, mid_sums], axis=0))
    memory_sums = low(plane_scatter(memory_parts[0], memory_parts[1]))
    mlp_sides, group_hop, grad_x, memory_sums = lax.optimization_barrier(
        (mlp_sides, group_hop, grad_x, memory_sums)
    )
    mlp_chip = corner_pieces(mlp_sides)
    group_here = level_hop(group_hop)
    mlp_chip, group_here = lax.optimization_barrier((mlp_chip, group_here))
    grad_memory = unspread(memory_sums)
    mlp_pieces = core_pieces(mlp_chip)
    group_sides = side_pieces(group_here)
    group_sides, mlp_pieces = lax.optimization_barrier((group_sides, mlp_pieces))
    mlp_totals = placed(mlp_pieces, spot_zero, ((0, 1), (2,)))
    group_chip = corner_pieces(group_sides)
    group_chip, mlp_totals = lax.optimization_barrier((group_chip, mlp_totals))
    in_totals, *other_totals = placed(
        core_pieces(group_chip), spot_zero, ((0, 1, 2), (3,), (7,), (6, 5), (4,))
    )
    grad_tokens = unspread(grad_x)
    branch_three = branch_sum(after(matmul_nn(hidden, wm_out), group_here))
    output = unspread(low(x2 + branch_three))
    return (
        output,
        grad_tokens,
        grad_memory,
        gain_total,
        in_totals.swapaxes(0, 1),
        *other_totals,
        *mlp_totals,
    )


def solution(mesh):
    in_plane = (mesh.shape["wide"], mesh.shape["narrow"]) == (8, 4)
    return jax.shard_map(
        per_device if in_plane else per_device_general,
        mesh=mesh,
        in_specs=(
            P(("wide", "narrow"), None),
            P(("wide", "narrow"), None),
            P("wide", None),
            P("wide", None),
            P(),
            P(("wide", "narrow"), None, None),
            P(("wide", "narrow"), None),
            P(("wide", "narrow"), None),
            P(("wide", "narrow"), None, None),
            P(("wide", "narrow"), None),
            P(("wide", "narrow"), None, None),
            P(("wide", "narrow"), None),
            P(("wide", "narrow"), None),
        ),
        out_specs=(
            P(("wide", "narrow"), None),
            P(("wide", "narrow"), None),
            P(("wide", "narrow"), None),
            P(None, "narrow"),
            P("narrow", None, None),
            P("narrow", None),
            P("narrow", None),
            P("narrow", None, None),
            P("narrow", None),
            P("narrow", None, None),
            P("narrow", None),
        ),
        check_vma=False,
    )
```

```python
import jax
import jax.numpy as jnp
from jax import lax
from jax.experimental import pallas as pl
from jax.experimental.pallas import tpu as pltpu
from jax.sharding import PartitionSpec as P

HEAD_DIM = 128


EPSILON = 1e-06
ROBOT_WEIGHT = 2.0
NEGATIVE = -1e30


def normed(values, gain_row):
    factor = lax.rsqrt(jnp.mean(values * values, axis=-1, keepdims=True) + EPSILON)
    return values * factor * gain_row


def token_info(lengths, item_kinds, positions, item_count):
    item_ends = jnp.cumsum(lengths)
    segment = jnp.sum((positions[:, None] >= item_ends[None, :]).astype(jnp.int32), axis=1)
    token_valid = segment < item_count
    item_hit = segment[:, None] == jnp.arange(item_count, dtype=jnp.int32)[None, :]
    robot_flag = jnp.sum(jnp.where(item_hit, item_kinds[None, :], 0), axis=1)
    weight = jnp.where(token_valid, jnp.where(robot_flag == 1, ROBOT_WEIGHT, 1.0), 0.0).astype(
        jnp.float32
    )
    return (segment, token_valid, weight)


def attend_forward(queries, keys_all, values_all, allowed):
    scores = jnp.einsum(
        "qhd,khd->hqk", queries, keys_all, preferred_element_type=jnp.float32
    ) * HEAD_DIM ** (-0.5)
    scores = jnp.where(allowed[None], scores, NEGATIVE)
    row_top = jnp.max(scores, axis=2, keepdims=True)
    exp_scores = jnp.exp(scores - row_top)
    denom_sum = jnp.sum(exp_scores, axis=2, keepdims=True)
    soft_probs = (exp_scores / denom_sum).astype(jnp.bfloat16)
    result = jnp.einsum("hqk,khd->qhd", soft_probs, values_all, preferred_element_type=jnp.float32)
    return (result, row_top + jnp.log(denom_sum))


def attend_backward(queries, keys_all, values_all, allowed, log_sums, grad_out):
    score_scale = HEAD_DIM ** (-0.5)
    scores = (
        jnp.einsum("qhd,khd->hqk", queries, keys_all, preferred_element_type=jnp.float32)
        * score_scale
    )
    scores = jnp.where(allowed[None], scores, NEGATIVE)
    soft_probs = jnp.exp(scores - log_sums)
    grad_probs = jnp.einsum(
        "qhd,khd->hqk", grad_out, values_all, preferred_element_type=jnp.float32
    )
    row_inner = jnp.sum(soft_probs * grad_probs, axis=2, keepdims=True)
    grad_scores = (soft_probs * (grad_probs - row_inner)).astype(jnp.bfloat16)
    grad_query = (
        jnp.einsum("hqk,khd->qhd", grad_scores, keys_all, preferred_element_type=jnp.float32)
        * score_scale
    )
    grad_keys = (
        jnp.einsum("hqk,qhd->khd", grad_scores, queries, preferred_element_type=jnp.float32)
        * score_scale
    )
    grad_values = jnp.einsum(
        "hqk,qhd->khd",
        soft_probs.astype(jnp.bfloat16),
        grad_out,
        preferred_element_type=jnp.float32,
    )
    return (grad_query, grad_keys, grad_values)


def spread_tables(wide, narrow):
    total = wide * narrow
    ratio = wide // narrow
    if (wide, narrow) == (8, 4):
        first, second, spots = [], [], [[0] * wide for _ in range(narrow)]
        for block in range(total):
            w, n = divmod(block, narrow)
            q, c = divmod(w, ratio)
            z1, z0 = divmod(n, 2)
            spot = 2 * (q ^ (2 * c + z1)) + (z0 ^ c)
            first.append((block, spot * narrow + n))
            second.append((spot * narrow + n, spot * narrow + q))
            spots[q][block - q * wide] = spot
        return (first, second, spots)
    direct = []
    for block in range(total):
        n, w = divmod(block, wide)
        direct.append((block, w * narrow + n))
    return (direct, None, None)


def spread(piece):
    first, second, _ = spread_tables(lax.axis_size("wide"), lax.axis_size("narrow"))
    piece = hop(piece, first)
    if second is not None:
        piece = hop(piece, second)
    return piece


def hop(piece, pairs):
    narrow = lax.axis_size("narrow")
    stay = [0] * (lax.axis_size("wide") * narrow)
    for source, target in pairs:
        stay[source] = int(source == target)
    here = lax.axis_index("wide") * narrow + lax.axis_index("narrow")
    moved = lax.ppermute(
        piece, ("wide", "narrow"), [pair for pair in pairs if pair[0] != pair[1]]
    )
    return jnp.where(jnp.asarray(stay, jnp.int32)[here] == 1, piece, moved)


def plane_hop(piece):
    return hop(piece, spread_tables(lax.axis_size("wide"), lax.axis_size("narrow"))[0])


def level_hop(piece):
    return hop(piece, spread_tables(lax.axis_size("wide"), lax.axis_size("narrow"))[1])


def wide_gather(pieces):
    rows, width = pieces[0].shape
    moved = spread(jnp.concatenate(pieces, axis=0))
    full = lax.all_gather(moved, "wide", axis=0, tiled=False)
    full = full.reshape(-1, len(pieces), rows, width)
    return tuple(full[:, kind].reshape(-1, width) for kind in range(len(pieces)))


def wide_total(terms):
    wide_count = lax.axis_size("wide")
    width = terms[0].shape[1]
    parts = [term.astype(jnp.bfloat16).reshape(wide_count, -1, width) for term in terms]
    packed = jnp.concatenate(parts, axis=1)
    rows = packed.shape[1]
    shard = lax.psum_scatter(
        packed.reshape(wide_count * rows, width), "wide", scatter_dimension=0, tiled=True
    )
    full = lax.all_gather(shard, "wide", axis=0, tiled=False)
    _, _, spots = spread_tables(wide_count, lax.axis_size("narrow"))
    if spots is not None:
        order = jnp.asarray(spots, jnp.int32)[lax.axis_index("narrow")]
        full = jnp.concatenate(
            [lax.dynamic_slice_in_dim(full, order[j], 1, 0) for j in range(wide_count)], axis=0
        )
    full = full.reshape(wide_count, len(terms), -1, width)
    return [
        full[:, kind].reshape(-1, width).astype(jnp.float32) for kind in range(len(terms))
    ]


def row_gather(local_rows):
    return lax.all_gather(local_rows, "narrow", axis=0, tiled=True)


def branch_sum(partial_rows):
    return lax.psum_scatter(
        partial_rows.astype(jnp.bfloat16), "narrow", scatter_dimension=0, tiled=True
    ).astype(jnp.float32)


def matmul_nt(a, b):
    return lax.dot_general(a, b, (((1,), (1,)), ((), ())), preferred_element_type=jnp.float32)


def matmul_nn(a, b):
    return lax.dot_general(a, b, (((1,), (0,)), ((), ())), preferred_element_type=jnp.float32)


def matmul_tn(a, b):
    return lax.dot_general(a, b, (((0,), (0,)), ((), ())), preferred_element_type=jnp.float32)


def tensor_pass(tokens, memory, gain_float, weights, cotangent, masks):
    segment, token_valid, valid_float, local_weight, self_ok, cross_ok = masks
    tok_rows = tokens.shape[0]
    group_rows = tok_rows * lax.axis_size("narrow")
    mem_group = memory.shape[0] * lax.axis_size("narrow")
    w_self_in, w_self_out, w_cross_q, w_cross_kv, w_cross_out, w_mlp_in, w_mlp_out = weights
    tok_float = tokens.astype(jnp.float32)
    h1 = normed(tok_float, gain_float[0]).astype(jnp.bfloat16)
    rows_one = row_gather(h1)
    ws_q, ws_k, ws_v = wide_gather([w_self_in[:, 0], w_self_in[:, 1], w_self_in[:, 2]])
    ws_out, wc_q, wc_k, wc_v, wc_out = wide_gather(
        [w_self_out, w_cross_q, w_cross_kv[:, 0], w_cross_kv[:, 1], w_cross_out]
    )
    wm_gate, wm_up, wm_out = wide_gather([w_mlp_in[:, 0], w_mlp_in[:, 1], w_mlp_out])
    memory_all = row_gather(memory)
    grad_y = cotangent.astype(jnp.float32) * local_weight[:, None]
    grad_mlp = row_gather(grad_y.astype(jnp.bfloat16))
    own_width = ws_out.shape[0]
    heads_here = own_width // HEAD_DIM

    def split(mat):
        return mat.reshape(mat.shape[0], heads_here, HEAD_DIM)

    def project(rows, mat):
        return matmul_nt(rows, mat).astype(jnp.bfloat16)

    sq, sk, sv = (split(project(rows_one, mat)) for mat in (ws_q, ws_k, ws_v))
    self_result, self_lse = attend_forward(sq, sk, sv, self_ok)
    self_heads = self_result.reshape(group_rows, own_width).astype(jnp.bfloat16)
    x1 = tok_float + branch_sum(matmul_nn(self_heads, ws_out))
    h2 = normed(x1, gain_float[1]).astype(jnp.bfloat16)
    rows_two = row_gather(h2)
    ck, cv = (split(project(memory_all, mat)) for mat in (wc_k, wc_v))
    cq = split(project(rows_two, wc_q))
    cross_result, cross_lse = attend_forward(cq, ck, cv, cross_ok)
    cross_heads = (
        (cross_result * valid_float[:, None, None])
        .reshape(group_rows, own_width)
        .astype(jnp.bfloat16)
    )
    x2 = x1 + branch_sum(matmul_nn(cross_heads, wc_out))
    h3 = normed(x2, gain_float[2]).astype(jnp.bfloat16)
    rows_three = row_gather(h3)
    gate = matmul_nt(rows_three, wm_gate)
    up = matmul_nt(rows_three, wm_up)
    hidden = (jax.nn.gelu(gate, approximate=True) * up).astype(jnp.bfloat16)
    output = (x2 + branch_sum(matmul_nn(hidden, wm_out))).astype(jnp.bfloat16)
    grad_hidden = matmul_nt(grad_mlp, wm_out)
    _, gelu_pull = jax.vjp(
        lambda gate_part, up_part: jax.nn.gelu(gate_part, approximate=True) * up_part, gate, up
    )
    grad_gate, grad_up = gelu_pull(grad_hidden)
    grad_gate = grad_gate.astype(jnp.bfloat16)
    grad_up = grad_up.astype(jnp.bfloat16)
    grad_h3 = branch_sum(matmul_nn(grad_gate, wm_gate) + matmul_nn(grad_up, wm_up))
    _, norm_pull3 = jax.vjp(normed, x2, gain_float[2])
    part_x2, grad_gain3 = norm_pull3(grad_h3)
    grad_x2 = grad_y + part_x2
    mlp_totals = wide_total(
        [
            matmul_tn(grad_gate, rows_three),
            matmul_tn(grad_up, rows_three),
            matmul_tn(hidden, grad_mlp),
        ]
    )
    grad_cross = row_gather(grad_x2.astype(jnp.bfloat16))
    grad_cross_heads = split(project(grad_cross, wc_out))
    grad_cross_heads = jnp.where(
        token_valid[:, None, None], grad_cross_heads, jnp.zeros_like(grad_cross_heads)
    )
    gq_heads, gk_heads, gv_heads = attend_backward(
        cq, ck, cv, cross_ok, cross_lse, grad_cross_heads
    )
    grad_cq = gq_heads.reshape(group_rows, own_width).astype(jnp.bfloat16)
    grad_ck = gk_heads.reshape(mem_group, own_width).astype(jnp.bfloat16)
    grad_cv = gv_heads.reshape(mem_group, own_width).astype(jnp.bfloat16)
    grad_h2 = branch_sum(matmul_nn(grad_cq, wc_q))
    _, norm_pull2 = jax.vjp(normed, x1, gain_float[1])
    part_x1, grad_gain2 = norm_pull2(grad_h2)
    grad_x1 = grad_x2 + part_x1
    grad_self = row_gather(grad_x1.astype(jnp.bfloat16))
    grad_memory = branch_sum(matmul_nn(grad_ck, wc_k) + matmul_nn(grad_cv, wc_v)).astype(
        jnp.bfloat16
    )
    mid_totals = wide_total(
        [
            matmul_tn(self_heads, grad_self),
            matmul_tn(grad_cq, rows_two),
            matmul_tn(grad_ck, memory_all),
            matmul_tn(grad_cv, memory_all),
            matmul_tn(cross_heads, grad_cross),
        ]
    )
    grad_self_heads = split(project(grad_self, ws_out))
    gsq, gsk, gsv = (
        mat.reshape(group_rows, own_width).astype(jnp.bfloat16)
        for mat in attend_backward(sq, sk, sv, self_ok, self_lse, grad_self_heads)
    )
    in_totals = wide_total(
        [matmul_tn(gsq, rows_one), matmul_tn(gsk, rows_one), matmul_tn(gsv, rows_one)]
    )
    grad_h1 = branch_sum(matmul_nn(gsq, ws_q) + matmul_nn(gsk, ws_k) + matmul_nn(gsv, ws_v))
    _, norm_pull1 = jax.vjp(normed, tok_float, gain_float[0])
    part_x, grad_gain1 = norm_pull1(grad_h1)
    grad_tokens = (grad_x1 + part_x).astype(jnp.bfloat16)
    gain_terms = jnp.stack([grad_gain1, grad_gain2, grad_gain3])
    return (output, grad_tokens, grad_memory, gain_terms, in_totals, mid_totals, mlp_totals)


def per_device_general(
    tokens,
    memory,
    item_len,
    item_kind,
    norm_gains,
    w_self_in,
    w_self_out,
    w_cross_q,
    w_cross_kv,
    w_cross_out,
    w_mlp_in,
    w_mlp_out,
    cotangent,
):
    tok_rows = tokens.shape[0]
    narrow_size = lax.axis_size("narrow")
    group_rows = tok_rows * narrow_size
    mem_group = memory.shape[0] * narrow_size
    lengths = item_len[0]
    item_count = lengths.shape[0]
    patch_rows = mem_group // item_count
    positions = jnp.arange(group_rows, dtype=jnp.int32)
    segment, token_valid, weight = token_info(lengths, item_kind[0], positions, item_count)
    local_weight = lax.dynamic_slice_in_dim(weight, lax.axis_index("narrow") * tok_rows, tok_rows)
    self_ok = (segment[:, None] == segment[None, :]) & (positions[None, :] <= positions[:, None])
    mem_item = jnp.arange(mem_group, dtype=jnp.int32) // patch_rows
    cross_ok = mem_item[None, :] == jnp.minimum(segment, item_count - 1)[:, None]
    valid_float = token_valid.astype(jnp.float32)
    masks = (segment, token_valid, valid_float, local_weight, self_ok, cross_ok)
    gain_float = norm_gains.astype(jnp.float32)
    weights = (w_self_in, w_self_out, w_cross_q, w_cross_kv, w_cross_out, w_mlp_in, w_mlp_out)
    output, grad_tokens, grad_memory, gain_terms, in_totals, mid_totals, mlp_totals = tensor_pass(
        tokens, memory, gain_float, weights, cotangent, masks
    )
    gain_shard = lax.psum_scatter(gain_terms, "narrow", scatter_dimension=1, tiled=True)
    gain_total = lax.psum(gain_shard, "wide")
    return (
        output,
        grad_tokens,
        grad_memory,
        gain_total,
        jnp.stack(in_totals, axis=1),
        mid_totals[0],
        mid_totals[1],
        jnp.stack([mid_totals[2], mid_totals[3]], axis=1),
        mid_totals[4],
        jnp.stack([mlp_totals[0], mlp_totals[1]], axis=1),
        mlp_totals[2],
    )


CORE, XDIM, YDIM = 1, 2, 4
PLANE = 8


def flip(value, bit):
    return lax.ppermute(value, "wide", [(i, i ^ bit) for i in range(PLANE)])


def unspread(piece):
    first, second, _ = spread_tables(lax.axis_size("wide"), lax.axis_size("narrow"))
    piece = hop(piece, [(b, a) for a, b in second])
    return hop(piece, [(b, a) for a, b in first])


def after(value, *others):
    return lax.optimization_barrier((value,) + others)[0]


def low(value):
    return jax.tree.map(lambda part: part.astype(jnp.bfloat16), value)


def plus(kept, moved):
    return kept.astype(jnp.float32) + moved.astype(jnp.float32)


def side_pieces(shard):
    return [shard, flip(shard, XDIM), flip(shard, YDIM)]


def corner_pieces(sides):
    half = sides[0].shape[-2] // 2
    return sides + [flip(sides[1][..., :half, :], YDIM), flip(sides[2][..., half:, :], XDIM)]


def chip_pieces(shard):
    return corner_pieces(side_pieces(shard))


def plane_gather(shard):
    own = jnp.concatenate(chip_pieces(shard), axis=0)
    return (own, flip(own, CORE))


def plane_scatter(kept, sent):
    return scatter_end(*scatter_start(kept, sent))


def scatter_start(kept, sent):
    chip = low(plus(kept, flip(low(sent), CORE)))
    lead, rows, width = chip.shape[:-2], chip.shape[-2] // 4, chip.shape[-1]
    half = rows // 2
    view = jnp.moveaxis(chip.reshape(lead + (2, 2, rows, width)), (-4, -3), (0, 1))
    part_a, part_b = view[..., :half, :], view[..., half:, :]
    part_a = plus(part_a[:, 0], flip(part_a[:, 1], XDIM))
    part_b = plus(part_b[0], flip(part_b[1], YDIM))
    return (part_a, part_b)


def scatter_end(part_a, part_b):
    done_a = plus(part_a[0], flip(low(part_a[1]), YDIM))
    done_b = plus(part_b[0], flip(low(part_b[1]), XDIM))
    return jnp.concatenate([done_a, done_b], axis=-2)


def group_attend(queries, keys_all, values_all, allowed):
    scores = jnp.einsum(
        "gqhd,gkhd->ghqk", queries, keys_all, preferred_element_type=jnp.float32
    ) * HEAD_DIM ** (-0.5)
    scores = jnp.where(allowed[:, None], scores, NEGATIVE)
    row_top = jnp.max(scores, axis=3, keepdims=True)
    exp_scores = jnp.exp(scores - row_top)
    denom_sum = jnp.sum(exp_scores, axis=3, keepdims=True)
    soft_probs = low(exp_scores / denom_sum)
    result = jnp.einsum(
        "ghqk,gkhd->gqhd", soft_probs, values_all, preferred_element_type=jnp.float32
    )
    return (result, row_top + jnp.log(denom_sum))


def group_attend_back(queries, keys_all, values_all, allowed, log_sums, grad_out):
    score_scale = HEAD_DIM ** (-0.5)
    scores = (
        jnp.einsum("gqhd,gkhd->ghqk", queries, keys_all, preferred_element_type=jnp.float32)
        * score_scale
    )
    scores = jnp.where(allowed[:, None], scores, NEGATIVE)
    soft_probs = jnp.exp(scores - log_sums)
    grad_probs = jnp.einsum(
        "gqhd,gkhd->ghqk", grad_out, values_all, preferred_element_type=jnp.float32
    )
    row_inner = jnp.sum(soft_probs * grad_probs, axis=3, keepdims=True)
    grad_scores = low(soft_probs * (grad_probs - row_inner))
    grad_query = (
        jnp.einsum("ghqk,gkhd->gqhd", grad_scores, keys_all, preferred_element_type=jnp.float32)
        * score_scale
    )
    grad_keys = (
        jnp.einsum("ghqk,gqhd->gkhd", grad_scores, queries, preferred_element_type=jnp.float32)
        * score_scale
    )
    grad_values = jnp.einsum(
        "ghqk,gqhd->gkhd", low(soft_probs), grad_out, preferred_element_type=jnp.float32
    )
    return (grad_query, grad_keys, grad_values)


def narrow_full(stacked):
    kinds, rows, width = stacked.shape
    full = lax.all_gather(stacked.reshape(kinds * rows, width), "narrow", axis=0, tiled=False)
    full = full.reshape(-1, kinds, rows, width)
    return [full[:, kind].reshape(-1, width) for kind in range(kinds)]


def narrow_total(term):
    return lax.psum_scatter(low(term), "narrow", scatter_dimension=0, tiled=True)


PIECE_FLIPS = (0, 2, 5, 7, 1, 3, 4, 6)
WIDE_FLIPS = (0, 2, 4, 6, 1, 3, 5, 7)


def place_body(spots, *refs, plan, source_count):
    sources, outs = refs[:source_count], refs[source_count:]
    step, part = pl.program_id(0), pl.program_id(1)

    def write(source):
        for out, kinds in zip(outs, plan):
            if len(kinds) == 1:
                out[...] = source[kinds[0]].astype(out.dtype)
            elif len(kinds) == 2:
                for slot, kind in enumerate(kinds):
                    out[:, slot, :] = source[kind].astype(out.dtype)
            else:
                for slot, kind in enumerate(kinds):
                    out[slot] = source[kind].astype(out.dtype)

    for number, source in enumerate(sources):
        which, spot = number // 5, number % 5
        if spot < 3:
            hit = step == 4 * which + spot
        else:
            hit = (step == 4 * which + 3) & (part == spot - 3)

        @pl.when(hit)
        def _(source=source):
            write(source)


def core_pieces(chip):
    return chip + [flip(piece, CORE) for piece in chip]


def placed(sources, spot_zero, plan, flips=PIECE_FLIPS, kind=jnp.float32):
    kinds, rows, width = sources[0].shape
    half = rows // 2
    spots = spot_zero ^ jnp.asarray(flips, jnp.int32)

    def source_spec(number):
        which, spot = number // 5, number % 5
        if spot >= 3:
            return pl.BlockSpec((kinds, half, width), lambda step, part, spots: (0, 0, 0))
        mine = 4 * which + spot

        def index(step, part, spots):
            return (0, jnp.where(step == mine, part, jnp.where(step < mine, 0, 1)), 0)

        return pl.BlockSpec((kinds, half, width), index)

    out_specs, out_shapes = [], []
    for group in plan:
        count = len(group)
        if count == 1:
            block, shape = (half, width), (PLANE * rows, width)
            index = lambda step, part, spots: (2 * spots[step] + part, 0)
        elif count == 2:
            block, shape = (half, 2, width), (PLANE * rows, 2, width)
            index = lambda step, part, spots: (2 * spots[step] + part, 0, 0)
        else:
            block, shape = (count, half, width), (count, PLANE * rows, width)
            index = lambda step, part, spots: (0, 2 * spots[step] + part, 0)
        out_specs.append(pl.BlockSpec(block, index))
        out_shapes.append(jax.ShapeDtypeStruct(shape, kind))
    body = lambda *refs: place_body(*refs, plan=plan, source_count=len(sources))
    return pl.pallas_call(
        body,
        grid_spec=pltpu.PrefetchScalarGridSpec(
            num_scalar_prefetch=1,
            grid=(PLANE, 2),
            in_specs=[source_spec(number) for number in range(len(sources))],
            out_specs=out_specs,
        ),
        out_shape=out_shapes,
        compiler_params=pltpu.CompilerParams(
            dimension_semantics=("arbitrary", "arbitrary"), vmem_limit_bytes=56 * 1024 * 1024
        ),
        cost_estimate=pl.CostEstimate(
            flops=0,
            transcendentals=0,
            bytes_accessed=PLANE * kinds * rows * width * (2 + jnp.dtype(kind).itemsize),
        ),
        name="place",
    )(spots, *sources)


def per_device(
    tokens,
    memory,
    item_len,
    item_kind,
    norm_gains,
    w_self_in,
    w_self_out,
    w_cross_q,
    w_cross_kv,
    w_cross_out,
    w_mlp_in,
    w_mlp_out,
    cotangent,
):
    tok_rows, width = tokens.shape
    mem_rows = memory.shape[0]
    item_count = item_len.shape[1]
    gain = norm_gains.astype(jnp.float32)
    tokens_hop = plane_hop(tokens)
    mlp_shard = jnp.concatenate([w_mlp_in.swapaxes(0, 1), w_mlp_out[None]], axis=0)
    info_own = spread(jnp.concatenate([item_len, item_kind], axis=1))
    info = jnp.stack([info_own[0], flip(info_own, YDIM)[0]], axis=0)
    tokens_here = level_hop(tokens_hop)
    ws_q, ws_k, ws_v = narrow_full(after(w_self_in.swapaxes(0, 1), tokens_here))
    x = tokens_here.astype(jnp.float32)
    h1 = after(low(normed(x, gain[0])), info)
    rows_one = plane_gather(h1)
    ws_out, wc_q = narrow_full(after(jnp.stack([w_self_out, w_cross_q]), ws_q))
    wc_k, wc_v = narrow_full(after(w_cross_kv.swapaxes(0, 1), ws_out))
    (wc_out,) = narrow_full(after(w_cross_out[None], wc_k))
    rows_one, memory_hop, cotangent_hop = lax.optimization_barrier(
        (rows_one, plane_hop(memory), plane_hop(cotangent))
    )
    memory_here = level_hop(memory_hop)
    cotangent_here = level_hop(after(cotangent_hop, memory_here))

    me, level = lax.axis_index("wide"), lax.axis_index("narrow")
    differ = (me >> 1) ^ level
    side, upper = differ >> 1, differ & 1
    quarter = 2 * upper + ((me & 1) ^ side)
    spot_zero = 4 * side + quarter
    order = jnp.asarray([0, 2, 1, 3], jnp.int32)
    quarters = jnp.stack([quarter ^ order, quarter ^ 1 ^ order], axis=0)
    positions = (
        quarters[:, :, None] * tok_rows + jnp.arange(tok_rows, dtype=jnp.int32)
    ).reshape(2, -1)
    segment, token_valid, weight = jax.vmap(token_info, in_axes=(0, 0, 0, None))(
        info[:, :item_count], info[:, item_count:], positions, item_count
    )
    local_weight = weight[0, :tok_rows]
    self_ok = (segment[:, :, None] == segment[:, None, :]) & (
        positions[:, None, :] <= positions[:, :, None]
    )
    patch_rows = mem_rows * (PLANE // 2) // item_count
    mem_item = (
        (quarters[:, :, None] * mem_rows + jnp.arange(mem_rows, dtype=jnp.int32)) // patch_rows
    ).reshape(2, -1)
    cross_ok = mem_item[:, None, :] == jnp.minimum(segment, item_count - 1)[:, :, None]
    valid_float = token_valid.astype(jnp.float32)

    own_width = ws_out.shape[0]
    heads_here = own_width // HEAD_DIM

    def project(rows, mat):
        parts = [low(matmul_nt(part, mat)).reshape(2, -1, heads_here, HEAD_DIM) for part in rows]
        return jnp.concatenate(parts, axis=1)

    def merge(mat):
        count = mat.shape[1] // 2
        return tuple(
            low(part.reshape(-1, own_width)) for part in (mat[:, :count], mat[:, count:])
        )

    def spread_out(terms):
        parts = [sum(matmul_nn(mat[part], weight) for mat, weight in terms) for part in (0, 1)]
        return plane_scatter(*parts)

    def weight_part(mats, rows):
        return low(matmul_tn(mats[0], rows[0]) + matmul_tn(mats[1], rows[1]))

    def packed_total(parts):
        levels = lax.axis_size("narrow")
        packed = jnp.stack([part.reshape(levels, -1, width) for part in parts], axis=1)
        total = lax.psum_scatter(
            packed.reshape(-1, width), "narrow", scatter_dimension=0, tiled=True
        )
        return total.reshape(len(parts), -1, width)

    sq, sk, sv = (project(rows_one, mat) for mat in (ws_q, ws_k, ws_v))
    self_result, self_lse = group_attend(sq, sk, sv, self_ok)
    self_heads = merge(self_result)
    self_heads, memory_here = lax.optimization_barrier((self_heads, memory_here))
    x1 = x + spread_out([(self_heads, ws_out)])
    h2 = low(normed(x1, gain[1]))
    memory_all = plane_gather(after(memory_here, h2))
    rows_two, cotangent_here = lax.optimization_barrier((plane_gather(h2), cotangent_here))
    ck, cv = (project(memory_all, mat) for mat in (wc_k, wc_v))
    cq = project(rows_two, wc_q)
    cross_result, cross_lse = group_attend(cq, ck, cv, cross_ok)
    cross_heads = merge(cross_result * valid_float[:, :, None, None])
    grad_y = cotangent_here.astype(jnp.float32) * local_weight[:, None]
    grad_mlp = row_gather(after(low(grad_y), wc_out))
    mlp_chip = corner_pieces(side_pieces(after(mlp_shard, memory_all[0])))
    cross_heads, grad_mlp, mlp_chip = lax.optimization_barrier((cross_heads, grad_mlp, mlp_chip))
    x2 = x1 + spread_out([(cross_heads, wc_out)])
    h3 = low(normed(x2, gain[2]))
    rows_three = row_gather(h3)
    wm_gate, wm_up, wm_out = placed(
        core_pieces(mlp_chip), me, ((0,), (1,), (2,)), WIDE_FLIPS, jnp.bfloat16
    )
    gate = matmul_nt(rows_three, wm_gate)
    up = matmul_nt(rows_three, wm_up)
    hidden = low(jax.nn.gelu(gate, approximate=True) * up)
    grad_hidden = matmul_nt(grad_mlp, wm_out)
    _, gelu_pull = jax.vjp(
        lambda gate_part, up_part: jax.nn.gelu(gate_part, approximate=True) * up_part, gate, up
    )
    grad_gate, grad_up = gelu_pull(grad_hidden)
    grad_gate, grad_up = low(grad_gate), low(grad_up)
    grad_h3 = branch_sum(matmul_nn(grad_gate, wm_gate) + matmul_nn(grad_up, wm_up))
    mlp_terms = ((grad_gate, rows_three), (grad_up, rows_three), (hidden, grad_mlp))
    mlp_packed = jnp.stack(
        [
            low(matmul_tn(mat, rows)).reshape(PLANE, -1, width)
            for mat, rows in mlp_terms
        ],
        axis=1,
    ).reshape(-1, width)
    mlp_packed, grad_h3 = lax.optimization_barrier((mlp_packed, grad_h3))
    mlp_sums = lax.psum_scatter(mlp_packed, "wide", scatter_dimension=0, tiled=True)
    mlp_sums = mlp_sums.reshape(3, -1, width)
    _, norm_pull3 = jax.vjp(normed, x2, gain[2])
    part_x2, grad_gain3 = norm_pull3(grad_h3)
    grad_x2 = grad_y + part_x2
    grad_cross = plane_gather(low(grad_x2))
    grad_cross_heads = project(grad_cross, wc_out)
    grad_cross_heads = jnp.where(
        token_valid[:, :, None, None], grad_cross_heads, jnp.zeros_like(grad_cross_heads)
    )
    grad_cq, grad_ck, grad_cv = (
        merge(mat)
        for mat in group_attend_back(cq, ck, cv, cross_ok, cross_lse, grad_cross_heads)
    )
    grad_h2 = spread_out([(grad_cq, wc_q)])
    _, norm_pull2 = jax.vjp(normed, x1, gain[1])
    part_x1, grad_gain2 = norm_pull2(grad_h2)
    grad_x1 = grad_x2 + part_x1
    grad_x1, mlp_sums = lax.optimization_barrier((grad_x1, mlp_sums))
    grad_self = plane_gather(low(grad_x1))
    memory_parts = [
        low(matmul_nn(grad_ck[part], wc_k) + matmul_nn(grad_cv[part], wc_v)) for part in (0, 1)
    ]
    mlp_here = spread(mlp_sums)
    mid_parts = [
        weight_part(cross_heads, grad_cross),
        weight_part(grad_cv, memory_all),
        weight_part(grad_ck, memory_all),
        weight_part(grad_cq, rows_two),
    ]
    mid_sums = packed_total(mid_parts)
    self_out_part = weight_part(self_heads, grad_self)
    grad_self_heads = project(grad_self, ws_out)
    gsq, gsk, gsv = (
        merge(mat) for mat in group_attend_back(sq, sk, sv, self_ok, self_lse, grad_self_heads)
    )
    gsq, gsk, gsv, memory_parts = lax.optimization_barrier((gsq, gsk, gsv, memory_parts))

    last_parts = [weight_part(term, rows_one) for term in (gsq, gsk, gsv)] + [self_out_part]
    last_parts, mlp_here = lax.optimization_barrier((last_parts, mlp_here))
    last = packed_total(last_parts)
    mlp_sides = side_pieces(mlp_here)
    grad_h1 = spread_out([(gsq, ws_q), (gsk, ws_k), (gsv, ws_v)])
    _, norm_pull1 = jax.vjp(normed, x, gain[0])
    part_x, grad_gain1 = norm_pull1(grad_h1)
    grad_x = low(grad_x1 + part_x)
    gain_terms = jnp.stack([grad_gain1, grad_gain2, grad_gain3])
    for bit in (1, 2):
        pairs = [(i, i ^ bit) for i in range(lax.axis_size("narrow"))]
        gain_terms = gain_terms + lax.ppermute(gain_terms, "narrow", pairs)
    for bit in (CORE, XDIM, YDIM):
        gain_terms = gain_terms + flip(gain_terms, bit)
    own_gains = width // lax.axis_size("narrow")
    gain_total = lax.dynamic_slice_in_dim(gain_terms, level * own_gains, own_gains, 1)
    group_hop = plane_hop(jnp.concatenate([last, mid_sums], axis=0))
    memory_sums = low(plane_scatter(memory_parts[0], memory_parts[1]))
    mlp_sides, group_hop, grad_x, memory_sums = lax.optimization_barrier(
        (mlp_sides, group_hop, grad_x, memory_sums)
    )
    mlp_chip = corner_pieces(mlp_sides)
    group_here = level_hop(group_hop)
    mlp_chip, group_here = lax.optimization_barrier((mlp_chip, group_here))
    grad_memory = unspread(memory_sums)
    mlp_pieces = core_pieces(mlp_chip)
    group_sides = side_pieces(group_here)
    mlp_totals = placed(mlp_pieces, spot_zero, ((0, 1), (2,)))
    group_sides, mlp_totals = lax.optimization_barrier((group_sides, mlp_totals))
    group_chip = corner_pieces(group_sides)
    in_totals, *other_totals = placed(
        core_pieces(group_chip), spot_zero, ((0, 1, 2), (3,), (7,), (6, 5), (4,))
    )
    grad_tokens = unspread(grad_x)
    branch_three = branch_sum(after(matmul_nn(hidden, wm_out), group_here))
    output = unspread(low(x2 + branch_three))
    return (
        output,
        grad_tokens,
        grad_memory,
        gain_total,
        in_totals.swapaxes(0, 1),
        *other_totals,
        *mlp_totals,
    )


def solution(mesh):
    in_plane = (mesh.shape["wide"], mesh.shape["narrow"]) == (8, 4)
    return jax.shard_map(
        per_device if in_plane else per_device_general,
        mesh=mesh,
        in_specs=(
            P(("wide", "narrow"), None),
            P(("wide", "narrow"), None),
            P("wide", None),
            P("wide", None),
            P(),
            P(("wide", "narrow"), None, None),
            P(("wide", "narrow"), None),
            P(("wide", "narrow"), None),
            P(("wide", "narrow"), None, None),
            P(("wide", "narrow"), None),
            P(("wide", "narrow"), None, None),
            P(("wide", "narrow"), None),
            P(("wide", "narrow"), None),
        ),
        out_specs=(
            P(("wide", "narrow"), None),
            P(("wide", "narrow"), None),
            P(("wide", "narrow"), None),
            P(None, "narrow"),
            P("narrow", None, None),
            P("narrow", None),
            P("narrow", None),
            P("narrow", None, None),
            P("narrow", None),
            P("narrow", None, None),
            P("narrow", None),
        ),
        check_vma=False,
    )
```

```python
import jax
import jax.numpy as jnp
from jax import lax
from jax.experimental import pallas as pl
from jax.experimental.pallas import tpu as pltpu
from jax.sharding import PartitionSpec as P

HEAD_DIM = 128


EPSILON = 1e-06
ROBOT_WEIGHT = 2.0
NEGATIVE = -1e30


def normed(values, gain_row):
    factor = lax.rsqrt(jnp.mean(values * values, axis=-1, keepdims=True) + EPSILON)
    return values * factor * gain_row


def token_info(lengths, item_kinds, positions, item_count):
    item_ends = jnp.cumsum(lengths)
    segment = jnp.sum((positions[:, None] >= item_ends[None, :]).astype(jnp.int32), axis=1)
    token_valid = segment < item_count
    item_hit = segment[:, None] == jnp.arange(item_count, dtype=jnp.int32)[None, :]
    robot_flag = jnp.sum(jnp.where(item_hit, item_kinds[None, :], 0), axis=1)
    weight = jnp.where(token_valid, jnp.where(robot_flag == 1, ROBOT_WEIGHT, 1.0), 0.0).astype(
        jnp.float32
    )
    return (segment, token_valid, weight)


def attend_forward(queries, keys_all, values_all, allowed):
    scores = jnp.einsum(
        "qhd,khd->hqk", queries, keys_all, preferred_element_type=jnp.float32
    ) * HEAD_DIM ** (-0.5)
    scores = jnp.where(allowed[None], scores, NEGATIVE)
    row_top = jnp.max(scores, axis=2, keepdims=True)
    exp_scores = jnp.exp(scores - row_top)
    denom_sum = jnp.sum(exp_scores, axis=2, keepdims=True)
    soft_probs = (exp_scores / denom_sum).astype(jnp.bfloat16)
    result = jnp.einsum("hqk,khd->qhd", soft_probs, values_all, preferred_element_type=jnp.float32)
    return (result, row_top + jnp.log(denom_sum))


def attend_backward(queries, keys_all, values_all, allowed, log_sums, grad_out):
    score_scale = HEAD_DIM ** (-0.5)
    scores = (
        jnp.einsum("qhd,khd->hqk", queries, keys_all, preferred_element_type=jnp.float32)
        * score_scale
    )
    scores = jnp.where(allowed[None], scores, NEGATIVE)
    soft_probs = jnp.exp(scores - log_sums)
    grad_probs = jnp.einsum(
        "qhd,khd->hqk", grad_out, values_all, preferred_element_type=jnp.float32
    )
    row_inner = jnp.sum(soft_probs * grad_probs, axis=2, keepdims=True)
    grad_scores = (soft_probs * (grad_probs - row_inner)).astype(jnp.bfloat16)
    grad_query = (
        jnp.einsum("hqk,khd->qhd", grad_scores, keys_all, preferred_element_type=jnp.float32)
        * score_scale
    )
    grad_keys = (
        jnp.einsum("hqk,qhd->khd", grad_scores, queries, preferred_element_type=jnp.float32)
        * score_scale
    )
    grad_values = jnp.einsum(
        "hqk,qhd->khd",
        soft_probs.astype(jnp.bfloat16),
        grad_out,
        preferred_element_type=jnp.float32,
    )
    return (grad_query, grad_keys, grad_values)


def spread_tables(wide, narrow):
    total = wide * narrow
    ratio = wide // narrow
    if (wide, narrow) == (8, 4):
        first, second, spots = [], [], [[0] * wide for _ in range(narrow)]
        for block in range(total):
            w, n = divmod(block, narrow)
            q, c = divmod(w, ratio)
            z1, z0 = divmod(n, 2)
            spot = 2 * (q ^ (2 * c + z1)) + (z0 ^ c)
            first.append((block, spot * narrow + n))
            second.append((spot * narrow + n, spot * narrow + q))
            spots[q][block - q * wide] = spot
        return (first, second, spots)
    direct = []
    for block in range(total):
        n, w = divmod(block, wide)
        direct.append((block, w * narrow + n))
    return (direct, None, None)


def spread(piece):
    first, second, _ = spread_tables(lax.axis_size("wide"), lax.axis_size("narrow"))
    piece = hop(piece, first)
    if second is not None:
        piece = hop(piece, second)
    return piece


def hop(piece, pairs):
    narrow = lax.axis_size("narrow")
    stay = [0] * (lax.axis_size("wide") * narrow)
    for source, target in pairs:
        stay[source] = int(source == target)
    here = lax.axis_index("wide") * narrow + lax.axis_index("narrow")
    moved = lax.ppermute(
        piece, ("wide", "narrow"), [pair for pair in pairs if pair[0] != pair[1]]
    )
    return jnp.where(jnp.asarray(stay, jnp.int32)[here] == 1, piece, moved)


def plane_hop(piece):
    return hop(piece, spread_tables(lax.axis_size("wide"), lax.axis_size("narrow"))[0])


def level_hop(piece):
    return hop(piece, spread_tables(lax.axis_size("wide"), lax.axis_size("narrow"))[1])


def wide_gather(pieces):
    rows, width = pieces[0].shape
    moved = spread(jnp.concatenate(pieces, axis=0))
    full = lax.all_gather(moved, "wide", axis=0, tiled=False)
    full = full.reshape(-1, len(pieces), rows, width)
    return tuple(full[:, kind].reshape(-1, width) for kind in range(len(pieces)))


def wide_total(terms):
    wide_count = lax.axis_size("wide")
    width = terms[0].shape[1]
    parts = [term.astype(jnp.bfloat16).reshape(wide_count, -1, width) for term in terms]
    packed = jnp.concatenate(parts, axis=1)
    rows = packed.shape[1]
    shard = lax.psum_scatter(
        packed.reshape(wide_count * rows, width), "wide", scatter_dimension=0, tiled=True
    )
    full = lax.all_gather(shard, "wide", axis=0, tiled=False)
    _, _, spots = spread_tables(wide_count, lax.axis_size("narrow"))
    if spots is not None:
        order = jnp.asarray(spots, jnp.int32)[lax.axis_index("narrow")]
        full = jnp.concatenate(
            [lax.dynamic_slice_in_dim(full, order[j], 1, 0) for j in range(wide_count)], axis=0
        )
    full = full.reshape(wide_count, len(terms), -1, width)
    return [
        full[:, kind].reshape(-1, width).astype(jnp.float32) for kind in range(len(terms))
    ]


def row_gather(local_rows):
    return lax.all_gather(local_rows, "narrow", axis=0, tiled=True)


def branch_sum(partial_rows):
    return lax.psum_scatter(
        partial_rows.astype(jnp.bfloat16), "narrow", scatter_dimension=0, tiled=True
    ).astype(jnp.float32)


def matmul_nt(a, b):
    return lax.dot_general(a, b, (((1,), (1,)), ((), ())), preferred_element_type=jnp.float32)


def matmul_nn(a, b):
    return lax.dot_general(a, b, (((1,), (0,)), ((), ())), preferred_element_type=jnp.float32)


def matmul_tn(a, b):
    return lax.dot_general(a, b, (((0,), (0,)), ((), ())), preferred_element_type=jnp.float32)


def tensor_pass(tokens, memory, gain_float, weights, cotangent, masks):
    segment, token_valid, valid_float, local_weight, self_ok, cross_ok = masks
    tok_rows = tokens.shape[0]
    group_rows = tok_rows * lax.axis_size("narrow")
    mem_group = memory.shape[0] * lax.axis_size("narrow")
    w_self_in, w_self_out, w_cross_q, w_cross_kv, w_cross_out, w_mlp_in, w_mlp_out = weights
    tok_float = tokens.astype(jnp.float32)
    h1 = normed(tok_float, gain_float[0]).astype(jnp.bfloat16)
    rows_one = row_gather(h1)
    ws_q, ws_k, ws_v = wide_gather([w_self_in[:, 0], w_self_in[:, 1], w_self_in[:, 2]])
    ws_out, wc_q, wc_k, wc_v, wc_out = wide_gather(
        [w_self_out, w_cross_q, w_cross_kv[:, 0], w_cross_kv[:, 1], w_cross_out]
    )
    wm_gate, wm_up, wm_out = wide_gather([w_mlp_in[:, 0], w_mlp_in[:, 1], w_mlp_out])
    memory_all = row_gather(memory)
    grad_y = cotangent.astype(jnp.float32) * local_weight[:, None]
    grad_mlp = row_gather(grad_y.astype(jnp.bfloat16))
    own_width = ws_out.shape[0]
    heads_here = own_width // HEAD_DIM

    def split(mat):
        return mat.reshape(mat.shape[0], heads_here, HEAD_DIM)

    def project(rows, mat):
        return matmul_nt(rows, mat).astype(jnp.bfloat16)

    sq, sk, sv = (split(project(rows_one, mat)) for mat in (ws_q, ws_k, ws_v))
    self_result, self_lse = attend_forward(sq, sk, sv, self_ok)
    self_heads = self_result.reshape(group_rows, own_width).astype(jnp.bfloat16)
    x1 = tok_float + branch_sum(matmul_nn(self_heads, ws_out))
    h2 = normed(x1, gain_float[1]).astype(jnp.bfloat16)
    rows_two = row_gather(h2)
    ck, cv = (split(project(memory_all, mat)) for mat in (wc_k, wc_v))
    cq = split(project(rows_two, wc_q))
    cross_result, cross_lse = attend_forward(cq, ck, cv, cross_ok)
    cross_heads = (
        (cross_result * valid_float[:, None, None])
        .reshape(group_rows, own_width)
        .astype(jnp.bfloat16)
    )
    x2 = x1 + branch_sum(matmul_nn(cross_heads, wc_out))
    h3 = normed(x2, gain_float[2]).astype(jnp.bfloat16)
    rows_three = row_gather(h3)
    gate = matmul_nt(rows_three, wm_gate)
    up = matmul_nt(rows_three, wm_up)
    hidden = (jax.nn.gelu(gate, approximate=True) * up).astype(jnp.bfloat16)
    output = (x2 + branch_sum(matmul_nn(hidden, wm_out))).astype(jnp.bfloat16)
    grad_hidden = matmul_nt(grad_mlp, wm_out)
    _, gelu_pull = jax.vjp(
        lambda gate_part, up_part: jax.nn.gelu(gate_part, approximate=True) * up_part, gate, up
    )
    grad_gate, grad_up = gelu_pull(grad_hidden)
    grad_gate = grad_gate.astype(jnp.bfloat16)
    grad_up = grad_up.astype(jnp.bfloat16)
    grad_h3 = branch_sum(matmul_nn(grad_gate, wm_gate) + matmul_nn(grad_up, wm_up))
    _, norm_pull3 = jax.vjp(normed, x2, gain_float[2])
    part_x2, grad_gain3 = norm_pull3(grad_h3)
    grad_x2 = grad_y + part_x2
    mlp_totals = wide_total(
        [
            matmul_tn(grad_gate, rows_three),
            matmul_tn(grad_up, rows_three),
            matmul_tn(hidden, grad_mlp),
        ]
    )
    grad_cross = row_gather(grad_x2.astype(jnp.bfloat16))
    grad_cross_heads = split(project(grad_cross, wc_out))
    grad_cross_heads = jnp.where(
        token_valid[:, None, None], grad_cross_heads, jnp.zeros_like(grad_cross_heads)
    )
    gq_heads, gk_heads, gv_heads = attend_backward(
        cq, ck, cv, cross_ok, cross_lse, grad_cross_heads
    )
    grad_cq = gq_heads.reshape(group_rows, own_width).astype(jnp.bfloat16)
    grad_ck = gk_heads.reshape(mem_group, own_width).astype(jnp.bfloat16)
    grad_cv = gv_heads.reshape(mem_group, own_width).astype(jnp.bfloat16)
    grad_h2 = branch_sum(matmul_nn(grad_cq, wc_q))
    _, norm_pull2 = jax.vjp(normed, x1, gain_float[1])
    part_x1, grad_gain2 = norm_pull2(grad_h2)
    grad_x1 = grad_x2 + part_x1
    grad_self = row_gather(grad_x1.astype(jnp.bfloat16))
    grad_memory = branch_sum(matmul_nn(grad_ck, wc_k) + matmul_nn(grad_cv, wc_v)).astype(
        jnp.bfloat16
    )
    mid_totals = wide_total(
        [
            matmul_tn(self_heads, grad_self),
            matmul_tn(grad_cq, rows_two),
            matmul_tn(grad_ck, memory_all),
            matmul_tn(grad_cv, memory_all),
            matmul_tn(cross_heads, grad_cross),
        ]
    )
    grad_self_heads = split(project(grad_self, ws_out))
    gsq, gsk, gsv = (
        mat.reshape(group_rows, own_width).astype(jnp.bfloat16)
        for mat in attend_backward(sq, sk, sv, self_ok, self_lse, grad_self_heads)
    )
    in_totals = wide_total(
        [matmul_tn(gsq, rows_one), matmul_tn(gsk, rows_one), matmul_tn(gsv, rows_one)]
    )
    grad_h1 = branch_sum(matmul_nn(gsq, ws_q) + matmul_nn(gsk, ws_k) + matmul_nn(gsv, ws_v))
    _, norm_pull1 = jax.vjp(normed, tok_float, gain_float[0])
    part_x, grad_gain1 = norm_pull1(grad_h1)
    grad_tokens = (grad_x1 + part_x).astype(jnp.bfloat16)
    gain_terms = jnp.stack([grad_gain1, grad_gain2, grad_gain3])
    return (output, grad_tokens, grad_memory, gain_terms, in_totals, mid_totals, mlp_totals)


def per_device_general(
    tokens,
    memory,
    item_len,
    item_kind,
    norm_gains,
    w_self_in,
    w_self_out,
    w_cross_q,
    w_cross_kv,
    w_cross_out,
    w_mlp_in,
    w_mlp_out,
    cotangent,
):
    tok_rows = tokens.shape[0]
    narrow_size = lax.axis_size("narrow")
    group_rows = tok_rows * narrow_size
    mem_group = memory.shape[0] * narrow_size
    lengths = item_len[0]
    item_count = lengths.shape[0]
    patch_rows = mem_group // item_count
    positions = jnp.arange(group_rows, dtype=jnp.int32)
    segment, token_valid, weight = token_info(lengths, item_kind[0], positions, item_count)
    local_weight = lax.dynamic_slice_in_dim(weight, lax.axis_index("narrow") * tok_rows, tok_rows)
    self_ok = (segment[:, None] == segment[None, :]) & (positions[None, :] <= positions[:, None])
    mem_item = jnp.arange(mem_group, dtype=jnp.int32) // patch_rows
    cross_ok = mem_item[None, :] == jnp.minimum(segment, item_count - 1)[:, None]
    valid_float = token_valid.astype(jnp.float32)
    masks = (segment, token_valid, valid_float, local_weight, self_ok, cross_ok)
    gain_float = norm_gains.astype(jnp.float32)
    weights = (w_self_in, w_self_out, w_cross_q, w_cross_kv, w_cross_out, w_mlp_in, w_mlp_out)
    output, grad_tokens, grad_memory, gain_terms, in_totals, mid_totals, mlp_totals = tensor_pass(
        tokens, memory, gain_float, weights, cotangent, masks
    )
    gain_shard = lax.psum_scatter(gain_terms, "narrow", scatter_dimension=1, tiled=True)
    gain_total = lax.psum(gain_shard, "wide")
    return (
        output,
        grad_tokens,
        grad_memory,
        gain_total,
        jnp.stack(in_totals, axis=1),
        mid_totals[0],
        mid_totals[1],
        jnp.stack([mid_totals[2], mid_totals[3]], axis=1),
        mid_totals[4],
        jnp.stack([mlp_totals[0], mlp_totals[1]], axis=1),
        mlp_totals[2],
    )


CORE, XDIM, YDIM = 1, 2, 4
PLANE = 8


def flip(value, bit):
    return lax.ppermute(value, "wide", [(i, i ^ bit) for i in range(PLANE)])


def unspread(piece):
    first, second, _ = spread_tables(lax.axis_size("wide"), lax.axis_size("narrow"))
    piece = hop(piece, [(b, a) for a, b in second])
    return hop(piece, [(b, a) for a, b in first])


def after(value, *others):
    return lax.optimization_barrier((value,) + others)[0]


def low(value):
    return jax.tree.map(lambda part: part.astype(jnp.bfloat16), value)


def plus(kept, moved):
    return kept.astype(jnp.float32) + moved.astype(jnp.float32)


def side_pieces(shard):
    return [shard, flip(shard, XDIM), flip(shard, YDIM)]


def corner_pieces(sides):
    half = sides[0].shape[-2] // 2
    return sides + [flip(sides[1][..., :half, :], YDIM), flip(sides[2][..., half:, :], XDIM)]


def chip_pieces(shard):
    return corner_pieces(side_pieces(shard))


def plane_gather(shard):
    own = jnp.concatenate(chip_pieces(shard), axis=0)
    return (own, flip(own, CORE))


def plane_scatter(kept, sent):
    return scatter_end(*scatter_start(kept, sent))


def scatter_start(kept, sent):
    chip = low(plus(kept, flip(low(sent), CORE)))
    lead, rows, width = chip.shape[:-2], chip.shape[-2] // 4, chip.shape[-1]
    half = rows // 2
    view = jnp.moveaxis(chip.reshape(lead + (2, 2, rows, width)), (-4, -3), (0, 1))
    part_a, part_b = view[..., :half, :], view[..., half:, :]
    part_a = plus(part_a[:, 0], flip(part_a[:, 1], XDIM))
    part_b = plus(part_b[0], flip(part_b[1], YDIM))
    return (part_a, part_b)


def scatter_end(part_a, part_b):
    done_a = plus(part_a[0], flip(low(part_a[1]), YDIM))
    done_b = plus(part_b[0], flip(low(part_b[1]), XDIM))
    return jnp.concatenate([done_a, done_b], axis=-2)


def group_attend(queries, keys_all, values_all, allowed):
    scores = jnp.einsum(
        "gqhd,gkhd->ghqk", queries, keys_all, preferred_element_type=jnp.float32
    ) * HEAD_DIM ** (-0.5)
    scores = jnp.where(allowed[:, None], scores, NEGATIVE)
    row_top = jnp.max(scores, axis=3, keepdims=True)
    exp_scores = jnp.exp(scores - row_top)
    denom_sum = jnp.sum(exp_scores, axis=3, keepdims=True)
    soft_probs = low(exp_scores / denom_sum)
    result = jnp.einsum(
        "ghqk,gkhd->gqhd", soft_probs, values_all, preferred_element_type=jnp.float32
    )
    return (result, row_top + jnp.log(denom_sum))


def group_attend_back(queries, keys_all, values_all, allowed, log_sums, grad_out):
    score_scale = HEAD_DIM ** (-0.5)
    scores = (
        jnp.einsum("gqhd,gkhd->ghqk", queries, keys_all, preferred_element_type=jnp.float32)
        * score_scale
    )
    scores = jnp.where(allowed[:, None], scores, NEGATIVE)
    soft_probs = jnp.exp(scores - log_sums)
    grad_probs = jnp.einsum(
        "gqhd,gkhd->ghqk", grad_out, values_all, preferred_element_type=jnp.float32
    )
    row_inner = jnp.sum(soft_probs * grad_probs, axis=3, keepdims=True)
    grad_scores = low(soft_probs * (grad_probs - row_inner))
    grad_query = (
        jnp.einsum("ghqk,gkhd->gqhd", grad_scores, keys_all, preferred_element_type=jnp.float32)
        * score_scale
    )
    grad_keys = (
        jnp.einsum("ghqk,gqhd->gkhd", grad_scores, queries, preferred_element_type=jnp.float32)
        * score_scale
    )
    grad_values = jnp.einsum(
        "ghqk,gqhd->gkhd", low(soft_probs), grad_out, preferred_element_type=jnp.float32
    )
    return (grad_query, grad_keys, grad_values)


def narrow_full(stacked):
    kinds, rows, width = stacked.shape
    full = lax.all_gather(stacked.reshape(kinds * rows, width), "narrow", axis=0, tiled=False)
    full = full.reshape(-1, kinds, rows, width)
    return [full[:, kind].reshape(-1, width) for kind in range(kinds)]


def narrow_total(term):
    return lax.psum_scatter(low(term), "narrow", scatter_dimension=0, tiled=True)


PIECE_FLIPS = (0, 2, 5, 7, 1, 3, 4, 6)
WIDE_FLIPS = (0, 2, 4, 6, 1, 3, 5, 7)


def place_body(spots, *refs, plan, source_count):
    sources, outs = refs[:source_count], refs[source_count:]
    step, part = pl.program_id(0), pl.program_id(1)

    def write(source):
        for out, kinds in zip(outs, plan):
            if len(kinds) == 1:
                out[...] = source[kinds[0]].astype(out.dtype)
            elif len(kinds) == 2:
                for slot, kind in enumerate(kinds):
                    out[:, slot, :] = source[kind].astype(out.dtype)
            else:
                for slot, kind in enumerate(kinds):
                    out[slot] = source[kind].astype(out.dtype)

    for number, source in enumerate(sources):
        which, spot = number // 5, number % 5
        if spot < 3:
            hit = step == 4 * which + spot
        else:
            hit = (step == 4 * which + 3) & (part == spot - 3)

        @pl.when(hit)
        def _(source=source):
            write(source)


def core_pieces(chip):
    return chip + [flip(piece, CORE) for piece in chip]


def placed(sources, spot_zero, plan, flips=PIECE_FLIPS, kind=jnp.float32):
    kinds, rows, width = sources[0].shape
    half = rows // 2
    spots = spot_zero ^ jnp.asarray(flips, jnp.int32)

    def source_spec(number):
        which, spot = number // 5, number % 5
        if spot >= 3:
            return pl.BlockSpec((kinds, half, width), lambda step, part, spots: (0, 0, 0))
        mine = 4 * which + spot

        def index(step, part, spots):
            return (0, jnp.where(step == mine, part, jnp.where(step < mine, 0, 1)), 0)

        return pl.BlockSpec((kinds, half, width), index)

    out_specs, out_shapes = [], []
    for group in plan:
        count = len(group)
        if count == 1:
            block, shape = (half, width), (PLANE * rows, width)
            index = lambda step, part, spots: (2 * spots[step] + part, 0)
        elif count == 2:
            block, shape = (half, 2, width), (PLANE * rows, 2, width)
            index = lambda step, part, spots: (2 * spots[step] + part, 0, 0)
        else:
            block, shape = (count, half, width), (count, PLANE * rows, width)
            index = lambda step, part, spots: (0, 2 * spots[step] + part, 0)
        out_specs.append(pl.BlockSpec(block, index))
        out_shapes.append(jax.ShapeDtypeStruct(shape, kind))
    body = lambda *refs: place_body(*refs, plan=plan, source_count=len(sources))
    return pl.pallas_call(
        body,
        grid_spec=pltpu.PrefetchScalarGridSpec(
            num_scalar_prefetch=1,
            grid=(PLANE, 2),
            in_specs=[source_spec(number) for number in range(len(sources))],
            out_specs=out_specs,
        ),
        out_shape=out_shapes,
        compiler_params=pltpu.CompilerParams(
            dimension_semantics=("arbitrary", "arbitrary"), vmem_limit_bytes=56 * 1024 * 1024
        ),
        cost_estimate=pl.CostEstimate(
            flops=0,
            transcendentals=0,
            bytes_accessed=PLANE * kinds * rows * width * (2 + jnp.dtype(kind).itemsize),
        ),
        name="place",
    )(spots, *sources)


def per_device(
    tokens,
    memory,
    item_len,
    item_kind,
    norm_gains,
    w_self_in,
    w_self_out,
    w_cross_q,
    w_cross_kv,
    w_cross_out,
    w_mlp_in,
    w_mlp_out,
    cotangent,
):
    tok_rows, width = tokens.shape
    mem_rows = memory.shape[0]
    item_count = item_len.shape[1]
    gain = norm_gains.astype(jnp.float32)
    tokens_hop = plane_hop(tokens)
    mlp_shard = jnp.concatenate([w_mlp_in.swapaxes(0, 1), w_mlp_out[None]], axis=0)
    info_own = spread(jnp.concatenate([item_len, item_kind], axis=1))
    info = jnp.stack([info_own[0], flip(info_own, YDIM)[0]], axis=0)
    tokens_here = level_hop(tokens_hop)
    ws_q, ws_k, ws_v = narrow_full(after(w_self_in.swapaxes(0, 1), tokens_here))
    x = tokens_here.astype(jnp.float32)
    h1 = after(low(normed(x, gain[0])), info)
    rows_one = plane_gather(h1)
    mlp_sides = side_pieces(after(mlp_shard, ws_q))
    ws_out, wc_q = narrow_full(after(jnp.stack([w_self_out, w_cross_q]), ws_q))
    wc_k, wc_v = narrow_full(after(w_cross_kv.swapaxes(0, 1), ws_out))
    (wc_out,) = narrow_full(after(w_cross_out[None], wc_k))
    rows_one, memory_hop, cotangent_hop = lax.optimization_barrier(
        (rows_one, plane_hop(memory), plane_hop(cotangent))
    )
    memory_here = level_hop(memory_hop)
    cotangent_here = level_hop(after(cotangent_hop, memory_here))

    me, level = lax.axis_index("wide"), lax.axis_index("narrow")
    differ = (me >> 1) ^ level
    side, upper = differ >> 1, differ & 1
    quarter = 2 * upper + ((me & 1) ^ side)
    spot_zero = 4 * side + quarter
    order = jnp.asarray([0, 2, 1, 3], jnp.int32)
    quarters = jnp.stack([quarter ^ order, quarter ^ 1 ^ order], axis=0)
    positions = (
        quarters[:, :, None] * tok_rows + jnp.arange(tok_rows, dtype=jnp.int32)
    ).reshape(2, -1)
    segment, token_valid, weight = jax.vmap(token_info, in_axes=(0, 0, 0, None))(
        info[:, :item_count], info[:, item_count:], positions, item_count
    )
    local_weight = weight[0, :tok_rows]
    self_ok = (segment[:, :, None] == segment[:, None, :]) & (
        positions[:, None, :] <= positions[:, :, None]
    )
    patch_rows = mem_rows * (PLANE // 2) // item_count
    mem_item = (
        (quarters[:, :, None] * mem_rows + jnp.arange(mem_rows, dtype=jnp.int32)) // patch_rows
    ).reshape(2, -1)
    cross_ok = mem_item[:, None, :] == jnp.minimum(segment, item_count - 1)[:, :, None]
    valid_float = token_valid.astype(jnp.float32)

    own_width = ws_out.shape[0]
    heads_here = own_width // HEAD_DIM

    def project(rows, mat):
        parts = [low(matmul_nt(part, mat)).reshape(2, -1, heads_here, HEAD_DIM) for part in rows]
        return jnp.concatenate(parts, axis=1)

    def merge(mat):
        count = mat.shape[1] // 2
        return tuple(
            low(part.reshape(-1, own_width)) for part in (mat[:, :count], mat[:, count:])
        )

    def spread_out(terms):
        parts = [sum(matmul_nn(mat[part], weight) for mat, weight in terms) for part in (0, 1)]
        return plane_scatter(*parts)

    def weight_part(mats, rows):
        return low(matmul_tn(mats[0], rows[0]) + matmul_tn(mats[1], rows[1]))

    def packed_total(parts):
        levels = lax.axis_size("narrow")
        packed = jnp.stack([part.reshape(levels, -1, width) for part in parts], axis=1)
        total = lax.psum_scatter(
            packed.reshape(-1, width), "narrow", scatter_dimension=0, tiled=True
        )
        return total.reshape(len(parts), -1, width)

    sq, sk, sv = (project(rows_one, mat) for mat in (ws_q, ws_k, ws_v))
    self_result, self_lse = group_attend(sq, sk, sv, self_ok)
    self_heads = merge(self_result)
    self_heads, mlp_sides, memory_here = lax.optimization_barrier(
        (self_heads, mlp_sides, memory_here)
    )
    x1 = x + spread_out([(self_heads, ws_out)])
    h2 = low(normed(x1, gain[1]))
    memory_all = plane_gather(after(memory_here, h2))
    rows_two, cotangent_here = lax.optimization_barrier((plane_gather(h2), cotangent_here))
    ck, cv = (project(memory_all, mat) for mat in (wc_k, wc_v))
    cq = project(rows_two, wc_q)
    cross_result, cross_lse = group_attend(cq, ck, cv, cross_ok)
    cross_heads = merge(cross_result * valid_float[:, :, None, None])
    grad_y = cotangent_here.astype(jnp.float32) * local_weight[:, None]
    grad_mlp = row_gather(after(low(grad_y), wc_out))
    mlp_chip = corner_pieces(lax.optimization_barrier((mlp_sides, memory_all[0]))[0])
    cross_heads, grad_mlp, mlp_chip = lax.optimization_barrier((cross_heads, grad_mlp, mlp_chip))
    x2 = x1 + spread_out([(cross_heads, wc_out)])
    h3 = low(normed(x2, gain[2]))
    rows_three = row_gather(h3)
    wm_gate, wm_up, wm_out = placed(
        core_pieces(mlp_chip), me, ((0,), (1,), (2,)), WIDE_FLIPS, jnp.bfloat16
    )
    gate = matmul_nt(rows_three, wm_gate)
    up = matmul_nt(rows_three, wm_up)
    hidden = low(jax.nn.gelu(gate, approximate=True) * up)
    grad_hidden = matmul_nt(grad_mlp, wm_out)
    _, gelu_pull = jax.vjp(
        lambda gate_part, up_part: jax.nn.gelu(gate_part, approximate=True) * up_part, gate, up
    )
    grad_gate, grad_up = gelu_pull(grad_hidden)
    grad_gate, grad_up = low(grad_gate), low(grad_up)
    grad_h3 = branch_sum(matmul_nn(grad_gate, wm_gate) + matmul_nn(grad_up, wm_up))
    mlp_terms = ((grad_gate, rows_three), (grad_up, rows_three), (hidden, grad_mlp))
    mlp_packed = jnp.stack(
        [
            low(matmul_tn(mat, rows)).reshape(PLANE, -1, width)
            for mat, rows in mlp_terms
        ],
        axis=1,
    ).reshape(-1, width)
    mlp_packed, grad_h3 = lax.optimization_barrier((mlp_packed, grad_h3))
    mlp_sums = lax.psum_scatter(mlp_packed, "wide", scatter_dimension=0, tiled=True)
    mlp_sums = mlp_sums.reshape(3, -1, width)
    _, norm_pull3 = jax.vjp(normed, x2, gain[2])
    part_x2, grad_gain3 = norm_pull3(grad_h3)
    grad_x2 = grad_y + part_x2
    grad_cross = plane_gather(low(grad_x2))
    grad_cross_heads = project(grad_cross, wc_out)
    grad_cross_heads = jnp.where(
        token_valid[:, :, None, None], grad_cross_heads, jnp.zeros_like(grad_cross_heads)
    )
    grad_cq, grad_ck, grad_cv = (
        merge(mat)
        for mat in group_attend_back(cq, ck, cv, cross_ok, cross_lse, grad_cross_heads)
    )
    grad_h2 = spread_out([(grad_cq, wc_q)])
    _, norm_pull2 = jax.vjp(normed, x1, gain[1])
    part_x1, grad_gain2 = norm_pull2(grad_h2)
    grad_x1 = grad_x2 + part_x1
    grad_x1, mlp_sums = lax.optimization_barrier((grad_x1, mlp_sums))
    grad_self = plane_gather(low(grad_x1))
    memory_parts = [
        low(matmul_nn(grad_ck[part], wc_k) + matmul_nn(grad_cv[part], wc_v)) for part in (0, 1)
    ]
    mlp_here = spread(mlp_sums)
    mid_parts = [
        weight_part(cross_heads, grad_cross),
        weight_part(grad_cv, memory_all),
        weight_part(grad_ck, memory_all),
        weight_part(grad_cq, rows_two),
    ]
    mid_sums = packed_total(mid_parts)
    self_out_part = weight_part(self_heads, grad_self)
    grad_self_heads = project(grad_self, ws_out)
    gsq, gsk, gsv = (
        merge(mat) for mat in group_attend_back(sq, sk, sv, self_ok, self_lse, grad_self_heads)
    )
    gsq, gsk, gsv, memory_parts = lax.optimization_barrier((gsq, gsk, gsv, memory_parts))

    last_parts = [weight_part(term, rows_one) for term in (gsq, gsk, gsv)] + [self_out_part]
    last_parts, mlp_here = lax.optimization_barrier((last_parts, mlp_here))
    last = packed_total(last_parts)
    mlp_sides = side_pieces(mlp_here)
    grad_h1 = spread_out([(gsq, ws_q), (gsk, ws_k), (gsv, ws_v)])
    _, norm_pull1 = jax.vjp(normed, x, gain[0])
    part_x, grad_gain1 = norm_pull1(grad_h1)
    grad_x = low(grad_x1 + part_x)
    gain_terms = jnp.stack([grad_gain1, grad_gain2, grad_gain3])
    for bit in (1, 2):
        pairs = [(i, i ^ bit) for i in range(lax.axis_size("narrow"))]
        gain_terms = gain_terms + lax.ppermute(gain_terms, "narrow", pairs)
    for bit in (CORE, XDIM, YDIM):
        gain_terms = gain_terms + flip(gain_terms, bit)
    own_gains = width // lax.axis_size("narrow")
    gain_total = lax.dynamic_slice_in_dim(gain_terms, level * own_gains, own_gains, 1)
    group_hop = plane_hop(jnp.concatenate([last, mid_sums], axis=0))
    memory_sums = low(plane_scatter(memory_parts[0], memory_parts[1]))
    mlp_sides, group_hop, grad_x, memory_sums = lax.optimization_barrier(
        (mlp_sides, group_hop, grad_x, memory_sums)
    )
    mlp_chip = corner_pieces(mlp_sides)
    group_here = level_hop(group_hop)
    mlp_chip, group_here = lax.optimization_barrier((mlp_chip, group_here))
    grad_memory = unspread(memory_sums)
    mlp_pieces = core_pieces(mlp_chip)
    group_sides = side_pieces(group_here)
    group_sides, mlp_pieces = lax.optimization_barrier((group_sides, mlp_pieces))
    mlp_totals = placed(mlp_pieces, spot_zero, ((0, 1), (2,)))
    group_chip = corner_pieces(group_sides)
    in_totals, *other_totals = placed(
        core_pieces(group_chip), spot_zero, ((0, 1, 2), (3,), (7,), (6, 5), (4,))
    )
    grad_tokens = unspread(grad_x)
    branch_three = branch_sum(after(matmul_nn(hidden, wm_out), group_here))
    output = unspread(low(x2 + branch_three))
    return (
        output,
        grad_tokens,
        grad_memory,
        gain_total,
        in_totals.swapaxes(0, 1),
        *other_totals,
        *mlp_totals,
    )


def solution(mesh):
    in_plane = (mesh.shape["wide"], mesh.shape["narrow"]) == (8, 4)
    return jax.shard_map(
        per_device if in_plane else per_device_general,
        mesh=mesh,
        in_specs=(
            P(("wide", "narrow"), None),
            P(("wide", "narrow"), None),
            P("wide", None),
            P("wide", None),
            P(),
            P(("wide", "narrow"), None, None),
            P(("wide", "narrow"), None),
            P(("wide", "narrow"), None),
            P(("wide", "narrow"), None, None),
            P(("wide", "narrow"), None),
            P(("wide", "narrow"), None, None),
            P(("wide", "narrow"), None),
            P(("wide", "narrow"), None),
        ),
        out_specs=(
            P(("wide", "narrow"), None),
            P(("wide", "narrow"), None),
            P(("wide", "narrow"), None),
            P(None, "narrow"),
            P("narrow", None, None),
            P("narrow", None),
            P("narrow", None),
            P("narrow", None, None),
            P("narrow", None),
            P("narrow", None, None),
            P("narrow", None),
        ),
        check_vma=False,
    )
```
